256 devices in a mesh: tile: 32 (over z, x_hi, core), group: 8 (over y, x_lo).
Axes of the slice: x: 4 (x_hi: 2, x_lo: 2; x = x_hi * 2 + x_lo), y: 4, z: 8, core: 2. Of those that a mesh axis runs over, the one named last changes fastest.
Arguments:
- object_field: float32 [2, 320, 4096], P(None, 'group', 'tile'), may hold values from -6 to 6
- probe_field: float32 [2, 256, 256], replicated, may hold values from -6 to 6
- amplitudes: float32 [256, 256, 256], P(('tile', 'group')), may hold values from 0 to 4
- row_start: int32 [256], P(('tile', 'group')), may hold values from 0 to 64
- column_start: int32 [256], P(('tile', 'group')), may hold values from 0 to 128
- live_slots: int32 [256], P(('tile', 'group')), may hold values 0 or 1
Outputs:
- new_object: float32 [2, 320, 4096], P(None, 'group', 'tile')
- new_probe: float32 [2, 256, 256], replicated
The draws below stay inside these ranges and needn't reach their ends.
All inputs are finite; a program needn't handle non-finite values. No bound on the sum of `live_slots` on one device may be relied on, other than what follows from the above.
Results may differ from the reference program's by a relative error of at most 0.0001.
Values sent between devices are 32-bit elements; how exact they have to be, the bound alone decides.
No kernel may reach another device: no remote copies, remote signals or barrier semaphores. Data moves between devices by JAX's collectives and lax.ppermute only.
A program may use at most 64 MiB of HBM per device.

```python
import math
import jax
import jax.numpy as jnp
from jax import lax

WIN = 256
HALO = 128
ITERS = 1
OBJ_ROWS = 320
COLS_DEV = 128
POS_DEV = 1
OBJ_COLS = 4096
POSITIONS = 256
N_TILE = 32
N_GROUP = 8


def with_ends(drawn, own_key, smallest, top_value):
    longest = drawn.shape.index(max(drawn.shape))
    spots = []
    for shift in (0, 1):
        where = [jax.random.randint(jax.random.fold_in(own_key, axis), (), 0, length) for axis, length in enumerate(drawn.shape)]
        where[longest] = (where[longest] + shift) % drawn.shape[longest]
        spots.append(tuple(where))
    return drawn.at[spots[0]].set(smallest).at[spots[1]].set(top_value)


def shard_levels(stream_key, extent, split, least, top_value):
    def one(position, shards_of):
        steps = jax.random.uniform(jax.random.fold_in(jax.random.fold_in(stream_key, 6), position), (shards_of,), jnp.float32, least / len(split), top_value / len(split))
        return jnp.repeat(jnp.exp(steps), extent[position] // shards_of).reshape((-1,) + (1,) * (len(extent) - position - 1))

    gain = one(*split[0])
    for cut in split[1:]:
        gain = gain * one(*cut)
    return gain


def normal_values(key, dims, spread, most, pieces=(), held_as=jnp.bfloat16):
    drawn = jax.random.normal(key, dims, jnp.float32) * spread
    if len(pieces) > 0:
        drawn = shard_levels(key, dims, pieces, -0.22, 0.18) * drawn
    return jnp.clip(drawn, min=-most, max=most).astype(held_as)


def setup_inputs(seed: int = 0) -> dict:
    arg_keys = jax.random.split(jax.random.key(seed), 7)
    object_field = normal_values(arg_keys[0], (2, OBJ_ROWS, OBJ_COLS), 1.0, 6.0, ((1, 8), (2, 32)), jnp.float32)
    probe_field = normal_values(arg_keys[1], (2, WIN, WIN), 1.0, 6.0, (), jnp.float32)
    amplitudes = jnp.clip(4.0 * jax.random.uniform(arg_keys[2], (POSITIONS, WIN, WIN), jnp.float32) ** shard_levels(arg_keys[2], (POSITIONS, WIN, WIN), ((0, 256),), -0.2, 0.2), 0.0, 4.0)
    row_start = with_ends(jax.random.randint(arg_keys[3], (POSITIONS,), 0, OBJ_ROWS - WIN + 1), jax.random.fold_in(arg_keys[3], 1), 0, OBJ_ROWS - WIN).astype(jnp.int32)
    column_start = with_ends(jax.random.randint(arg_keys[4], (POSITIONS,), 0, COLS_DEV + 2 * HALO - WIN + 1), jax.random.fold_in(arg_keys[4], 1), 0, COLS_DEV + 2 * HALO - WIN).astype(jnp.int32)
    live_slots = with_ends((jax.random.randint(arg_keys[5], (POSITIONS,), 0, 4) < 3).astype(jnp.int32), jax.random.fold_in(arg_keys[5], 1), 0, 1)
    return dict(object_field=object_field, probe_field=probe_field, amplitudes=amplitudes, row_start=row_start, column_start=column_start, live_slots=live_slots)


def dft_tables(length):
    counter = jnp.arange(length, dtype=jnp.int32)
    product = counter[:, None] * counter[None, :] % length
    angles = 2.0 * math.pi / length * product.astype(jnp.float32)
    factor = 1.0 / math.sqrt(length)
    return (jnp.cos(angles) * factor, jnp.sin(angles) * factor)

def apply_left(matrix, values):
    return jnp.einsum('jk,pkl->pjl', matrix, values, precision=lax.Precision.HIGHEST)

def apply_right(values, matrix):
    return jnp.einsum('pjk,kl->pjl', values, matrix, precision=lax.Precision.HIGHEST)

def transform(real_part, imag_part, cos_table, sin_table, sign):
    left_real = apply_left(cos_table, real_part) - sign * apply_left(sin_table, imag_part)
    left_imag = apply_left(cos_table, imag_part) + sign * apply_left(sin_table, real_part)
    right_real = apply_right(left_real, cos_table) - sign * apply_right(left_imag, sin_table)
    right_imag = apply_right(left_imag, cos_table) + sign * apply_right(left_real, sin_table)
    return (right_real, right_imag)

def window_terms(windows, probe_field, amplitudes, live_slots, cos_table, sin_table):
    sample_real = windows[:, 0]
    sample_imag = windows[:, 1]
    probe_real = probe_field[0]
    probe_imag = probe_field[1]
    exit_real = probe_real * sample_real - probe_imag * sample_imag
    exit_imag = probe_real * sample_imag + probe_imag * sample_real
    far_real, far_imag = transform(exit_real, exit_imag, cos_table, sin_table, -1.0)
    modulus = jnp.maximum(jnp.sqrt(far_real * far_real + far_imag * far_imag), 0.25)
    factor = 1.0 - amplitudes / modulus
    miss_real, miss_imag = transform(far_real * factor, far_imag * factor, cos_table, sin_table, 1.0)
    weight = live_slots.astype(jnp.float32)[:, None, None]
    miss_real = miss_real * weight
    miss_imag = miss_imag * weight
    grad_real = probe_real * miss_real + probe_imag * miss_imag
    grad_imag = probe_real * miss_imag - probe_imag * miss_real
    probe_light = weight * (probe_real * probe_real + probe_imag * probe_imag)
    terms = jnp.stack([grad_real, grad_imag, probe_light], axis=1)
    probe_grad = jnp.stack([lax.optimization_barrier(jnp.sum(sample_real * miss_real + sample_imag * miss_imag, axis=0)), lax.optimization_barrier(jnp.sum(sample_real * miss_imag - sample_imag * miss_real, axis=0))], axis=0)
    window_light = lax.optimization_barrier(jnp.sum(weight * (sample_real * sample_real + sample_imag * sample_imag), axis=0))
    return (terms, probe_grad, window_light)

def add_windows(accum, terms, top_rows, left_edges):
    zero_index = jnp.zeros((), jnp.int32)

    def place(slot, current):
        corner = (zero_index, top_rows[slot], left_edges[slot])
        piece = lax.dynamic_slice(current, corner, (3, WIN, WIN))
        return lax.dynamic_update_slice(current, piece + terms[slot], corner)
    return lax.fori_loop(0, terms.shape[0], place, accum)

def cut_windows(padded, top_rows, left_edges):
    zero_index = jnp.zeros((), jnp.int32)

    def single(top_row, left_edge):
        return lax.dynamic_slice(padded, (zero_index, top_row, left_edge), (2, WIN, WIN))
    return jax.vmap(single)(top_rows, left_edges)

def apply_updates(object_field, probe_field, share, probe_grad, window_light):
    light_max = jnp.max(probe_field[0] * probe_field[0] + probe_field[1] * probe_field[1]) + 1e-06
    new_object = object_field - share[0:2] / (share[2:3] + 0.25 * light_max)
    new_probe = probe_field - probe_grad / (window_light + 0.25 * jnp.mean(window_light) + 1e-05)[None]
    return (new_object, new_probe)

def reference(object_field, probe_field, amplitudes, row_start, column_start, live_slots):
    cos_table, sin_table = dft_tables(WIN)
    blocks = N_TILE * N_GROUP
    tile_first = jnp.arange(blocks, dtype=jnp.int32) // N_GROUP * COLS_DEV
    block_cols = (column_start.reshape(blocks, POS_DEV).astype(jnp.int32) + tile_first[:, None]).astype(jnp.int32)
    block_rows = row_start.reshape(blocks, POS_DEV).astype(jnp.int32)
    block_amps = amplitudes.reshape(blocks, POS_DEV, WIN, WIN)
    block_live = live_slots.reshape(blocks, POS_DEV)
    for iteration in range(ITERS):
        padded = jnp.pad(object_field, ((0, 0), (0, 0), (HALO, HALO)))

        def visit(carry, block):
            grad_acc, probe_acc, light_acc = carry
            top_rows, left_edges, amps_here, live_here = block
            windows = cut_windows(padded, top_rows, left_edges)
            terms, probe_grad, window_light = window_terms(windows, probe_field, amps_here, live_here, cos_table, sin_table)
            grad_acc = add_windows(grad_acc, terms, top_rows, left_edges)
            return ((grad_acc, probe_acc + probe_grad, light_acc + window_light), None)
        start = (jnp.zeros((3, OBJ_ROWS, OBJ_COLS + 2 * HALO), jnp.float32), jnp.zeros((2, WIN, WIN), jnp.float32), jnp.zeros((WIN, WIN), jnp.float32))
        (grad_acc, probe_grad, window_light), unused = lax.scan(visit, start, (block_rows, block_cols, block_amps, block_live))
        share = grad_acc[:, :, HALO:HALO + OBJ_COLS]
        object_field, probe_field = apply_updates(object_field, probe_field, share, probe_grad, window_light)
    return (object_field, probe_field)
```

```python
import jax
import jax.numpy as jnp
import ml_dtypes
import numpy as np
from jax import lax
from jax.experimental import pallas as pl
from jax.experimental.pallas import tpu as pltpu
from jax.sharding import PartitionSpec as P

WIN = 256
LANES = 128
X_LO, Y_A, Y_B = 1, 2, 6
SMEM = pltpu.MemorySpace.SMEM
VMEM = pltpu.MemorySpace.VMEM


def split_tables():
    counter = np.arange(WIN)
    angles = 2.0 * np.pi / WIN * (counter[:, None] * counter[None, :] % WIN)
    cos, sin = np.cos(angles) / np.sqrt(WIN), np.sin(angles) / np.sqrt(WIN)
    both = np.concatenate([cos, sin], axis=0)
    high = both.astype(ml_dtypes.bfloat16)
    low = (both - high.astype(np.float64)).astype(ml_dtypes.bfloat16)
    return high, low


def member(position):
    offset = 0
    for bit, mask in ((4, X_LO), (2, Y_A), (1, Y_B)):
        if position & bit:
            offset ^= mask
    return offset


def halves(value):
    high = value.astype(jnp.bfloat16)
    low = (value - high.astype(jnp.float32)).astype(jnp.bfloat16)
    return high, low


def product(left, right):
    def dot(a, b):
        return jnp.dot(a, b, preferred_element_type=jnp.float32)

    return dot(left[0], right[0]) + dot(left[0], right[1]) + dot(left[1], right[0])


def transform(real, imag, tall, wide, sign):
    cols = product(tall, halves(jnp.concatenate([real, imag], axis=1)))
    left_real = cols[:WIN, :WIN] - sign * cols[WIN:, WIN:]
    left_imag = cols[:WIN, WIN:] + sign * cols[WIN:, :WIN]
    rows = product(halves(jnp.concatenate([left_real, left_imag], axis=0)), wide)
    right_real = rows[:WIN, :WIN] - sign * rows[WIN:, WIN:]
    right_imag = rows[WIN:, :WIN] + sign * rows[:WIN, WIN:]
    return right_real, right_imag


def piece_of(tile, group):
    y_b = (group >> 2) & 1
    y_a = ((group >> 1) & 1) ^ y_b
    return (tile & 1) * 8 + (group & 1) * 4 + y_a * 2 + y_b


def window_kernel(
    place, row_ref, col_ref, live_ref, mid, near, far, probe, amps, high, low,
    send, keep, near_out, far_out, mid_out, peak, field, grads,
):
    tile, group = place[0], place[1]
    row, col = row_ref[0], col_ref[0]
    live = live_ref[0].astype(jnp.float32)
    odd = tile & 1
    for position in range(8):
        top = pl.multiple_of((group ^ member(position)) * 40, 8)
        for part in range(2):
            field[part, 1, pl.ds(top, 40), :] = mid[position, part]
            field[part, 2 - 2 * odd, pl.ds(top, 40), :] = near[position, part]
            field[part, 2 * odd, pl.ds(top, 40), :] = far[position, part]
    lane = lax.broadcasted_iota(jnp.int32, (WIN, LANES), 1)
    back = lax.rem(LANES - col, LANES)
    ahead = lax.rem(col, LANES)
    first = lane < LANES - col

    def cut(part):
        turned = [
            pltpu.roll(field[part, block, pl.ds(row, WIN), :], back, 1) for block in range(3)
        ]
        return jnp.concatenate(
            [jnp.where(first, turned[0], turned[1]), jnp.where(first, turned[1], turned[2])], axis=1
        )

    sample_real, sample_imag = cut(0), cut(1)
    probe_real, probe_imag = probe[0], probe[1]
    exit_real = probe_real * sample_real - probe_imag * sample_imag
    exit_imag = probe_real * sample_imag + probe_imag * sample_real
    tall = (high[...], low[...])
    wide = tuple(jnp.concatenate([table[:WIN], table[WIN:]], axis=1) for table in tall)
    far_real, far_imag = transform(exit_real, exit_imag, tall, wide, -1.0)
    power = far_real * far_real + far_imag * far_imag
    factor = 1.0 - amps[0] * lax.rsqrt(jnp.maximum(power, 0.0625))
    miss_real, miss_imag = transform(far_real * factor, far_imag * factor, tall, wide, 1.0)
    miss_real = miss_real * live
    miss_imag = miss_imag * live
    light = probe_real * probe_real + probe_imag * probe_imag
    peak[...] = jnp.full((8, LANES), jnp.max(light), jnp.float32)

    terms = (
        probe_real * miss_real + probe_imag * miss_imag,
        probe_real * miss_imag - probe_imag * miss_real,
        live * light,
    )
    wrapped = lane < col
    zero = jnp.zeros((WIN, LANES), jnp.float32)
    grads[...] = jnp.zeros_like(grads)
    for part in range(3):
        start = pltpu.roll(terms[part][:, :LANES], ahead, 1)
        end = pltpu.roll(terms[part][:, LANES:], ahead, 1)
        grads[part, 0, pl.ds(row, WIN), :] = jnp.where(wrapped, zero, start)
        grads[part, 1, pl.ds(row, WIN), :] = jnp.where(wrapped, start, end)
        grads[part, 2, pl.ds(row, WIN), :] = jnp.where(wrapped, end, zero)
    for position in range(8):
        top = pl.multiple_of((group ^ member(position)) * 40, 8)
        for part in range(3):
            mid_out[position, part] = grads[part, 1, pl.ds(top, 40), :]
            near_out[position, part] = grads[part, 2 - 2 * odd, pl.ds(top, 40), :]
            far_out[position, part] = grads[part, 2 * odd, pl.ds(top, 40), :]

    window_light = live * (sample_real * sample_real + sample_imag * sample_imag)
    sums = (
        sample_real * miss_real + sample_imag * miss_imag,
        sample_real * miss_imag - sample_imag * miss_real,
        window_light,
    )
    total = jnp.zeros((8, LANES), jnp.float32)
    for line in range(0, WIN, 8):
        total = total + window_light[line : line + 8, :LANES] + window_light[line : line + 8, LANES:]
    mine = piece_of(tile, group)
    keep_top = mine >> 3
    for piece in range(16):
        entry = piece ^ (mine & 7)
        slot = entry & 7
        for part in range(3):
            for side in range(2):
                lines = pl.ds(part * 32 + side * 16, 16)
                value = sums[part][piece * 16 : piece * 16 + 16, side * LANES : (side + 1) * LANES]
                grads_store(send, keep, (piece >> 3) == keep_top, slot, lines, value)
        grads_store(send, keep, (piece >> 3) == keep_top, slot, pl.ds(96, 8), total)


def grads_store(send, keep, stays, slot, lines, value):
    @pl.when(stays)
    def _():
        keep[slot, lines, :] = value

    @pl.when(jnp.logical_not(stays))
    def _():
        send[slot, lines, :] = value


def probe_kernel(place, one, two, probe, out):
    piece = piece_of(place[0], place[1])
    summed = one[0] + two[0]
    mean = jnp.sum(summed[96:104]) * (1.0 / (WIN * WIN))
    for side in range(2):
        bottom = summed[64 + side * 16 : 80 + side * 16] + 0.25 * mean + 1e-05
        for part in range(2):
            lines = part * 32 + side * 16
            top = pl.multiple_of(piece * 16, 16)
            old = probe[part, pl.ds(top, 16), side * LANES : (side + 1) * LANES]
            out[0, lines : lines + 16, :] = old - summed[lines : lines + 16] / bottom


def gather_kernel(place, one, two, out):
    piece = piece_of(place[0], place[1])
    for entry in range(16):
        source, slot = (one, entry) if entry < 8 else (two, entry - 8)
        top = pl.multiple_of((piece ^ entry) * 16, 16)
        for part in range(2):
            for side in range(2):
                lines = part * 32 + side * 16
                out[part, pl.ds(top, 16), side * LANES : (side + 1) * LANES] = source[
                    slot, lines : lines + 16, :
                ]


def object_kernel(one, two, old, peak, out):
    summed = one[0] + two[0]
    bottom = summed[2] + 0.25 * (peak[0:1, :] + 1e-06)
    out[0] = old[0] - summed[0] / bottom
    out[1] = old[1] - summed[1] / bottom


def pair_up(axis, mask):
    return [(i, i ^ mask) for i in range(lax.axis_size(axis))]


def swap(value, axis, mask):
    return lax.ppermute(value, axis, pair_up(axis, mask))


def swap_far(value):
    count = lax.axis_size("tile")
    pairs = []
    for i in range(1, count - 1, 2):
        pairs += [(i, i + 1), (i + 1, i)]
    return lax.ppermute(value, "tile", pairs)


def local(object_field, probe_field, amplitudes, row_start, column_start, live_slots):
    f32 = jnp.float32
    smem, vmem = pl.BlockSpec(memory_space=SMEM), pl.BlockSpec(memory_space=VMEM)
    place = jnp.stack([lax.axis_index("tile"), lax.axis_index("group")]).astype(jnp.int32)
    high, low = split_tables()

    held = object_field[None]
    for mask in (Y_B, Y_A, X_LO):
        held = jnp.concatenate([held, swap(held, "group", mask)], axis=0)
    near, far = swap(held, "tile", 1), swap_far(held)

    shape = jax.ShapeDtypeStruct
    send, keep, near_out, far_out, mid_out, peak = pl.pallas_call(
        window_kernel,
        out_shape=(
            shape((8, 104, LANES), f32),
            shape((8, 104, LANES), f32),
            shape((8, 3, 40, LANES), f32),
            shape((8, 3, 40, LANES), f32),
            shape((8, 3, 40, LANES), f32),
            shape((8, LANES), f32),
        ),
        in_specs=[smem] * 4 + [vmem] * 7,
        out_specs=(vmem,) * 6,
        scratch_shapes=[
            pltpu.VMEM((2, 3, 320, LANES), f32),
            pltpu.VMEM((3, 3, 320, LANES), f32),
        ],
        name="window",
    )(
        place, row_start, column_start, live_slots, held, near, far,
        probe_field, amplitudes, jnp.asarray(high), jnp.asarray(low),
    )

    got = swap(send, "tile", 1)
    for count, mask in ((4, X_LO), (2, Y_A), (1, Y_B)):
        send, keep = keep[count:] + got[count:], keep[:count] + got[:count]
        got = swap(send, "group", mask)
    for mask in (2, 4, 8):
        keep = keep + got
        got = swap(keep, "tile", mask)
    keep = keep + got
    got = swap(keep, "tile", 28)
    piece = pl.pallas_call(
        probe_kernel,
        out_shape=shape((1, 64, LANES), f32),
        in_specs=[smem] + [vmem] * 3,
        out_specs=vmem,
        name="probe",
    )(place, keep, got, probe_field)

    mine = mid_out + swap(near_out, "tile", 1) + swap_far(far_out)
    for count, mask in ((4, X_LO), (2, Y_A), (1, Y_B)):
        got = swap(mine[count:], "group", mask)
        if count > 1:
            mine = mine[:count] + got
    new_object = pl.pallas_call(
        object_kernel,
        out_shape=shape((2, 40, LANES), f32),
        in_specs=[vmem] * 4,
        out_specs=vmem,
        name="object",
    )(mine[:1], got, object_field, peak)

    for mask in (Y_B, Y_A, X_LO):
        piece = jnp.concatenate([piece, swap(piece, "group", mask)], axis=0)
    new_probe = pl.pallas_call(
        gather_kernel,
        out_shape=shape((2, WIN, WIN), f32),
        in_specs=[smem] + [vmem] * 2,
        out_specs=vmem,
        name="gather",
    )(place, piece, swap(piece, "tile", 1))
    return new_object, new_probe


def solution(mesh):
    return jax.shard_map(
        local,
        mesh=mesh,
        in_specs=(
            P(None, "group", "tile"),
            P(),
            P(("tile", "group"), None, None),
            P(("tile", "group")),
            P(("tile", "group")),
            P(("tile", "group")),
        ),
        out_specs=(P(None, "group", "tile"), P()),
        check_vma=False,
    )
```

```python
import jax
import jax.numpy as jnp
import ml_dtypes
import numpy as np
from jax import lax
from jax.experimental import pallas as pl
from jax.experimental.pallas import tpu as pltpu
from jax.sharding import PartitionSpec as P

WIN = 256
LANES = 128
PIECE = 104
SMEM = pltpu.MemorySpace.SMEM
VMEM = pltpu.MemorySpace.VMEM


def split_tables():
    counter = np.arange(WIN)
    angles = 2.0 * np.pi / WIN * (counter[:, None] * counter[None, :] % WIN)
    cos, sin = np.cos(angles) / np.sqrt(WIN), np.sin(angles) / np.sqrt(WIN)
    both = np.concatenate([cos, sin], axis=0)
    high = both.astype(ml_dtypes.bfloat16)
    low = (both - high.astype(np.float64)).astype(ml_dtypes.bfloat16)
    return high, low


def halves(value):
    high = value.astype(jnp.bfloat16)
    low = (value - high.astype(jnp.float32)).astype(jnp.bfloat16)
    return high, low


def product(left, right):
    def dot(a, b):
        return jnp.dot(a, b, preferred_element_type=jnp.float32)

    return dot(left[0], right[0]) + dot(left[0], right[1]) + dot(left[1], right[0])


def transform(real, imag, tall, wide, sign):
    cols = product(tall, halves(jnp.concatenate([real, imag], axis=1)))
    left_real = cols[:WIN, :WIN] - sign * cols[WIN:, WIN:]
    left_imag = cols[:WIN, WIN:] + sign * cols[WIN:, :WIN]
    rows = product(halves(jnp.concatenate([left_real, left_imag], axis=0)), wide)
    right_real = rows[:WIN, :WIN] - sign * rows[WIN:, WIN:]
    right_imag = rows[WIN:, :WIN] + sign * rows[:WIN, WIN:]
    return right_real, right_imag


def window_kernel(
    place, row_ref, col_ref, live_ref, stack, probe, amps, high, low,
    keep, send, far_out, peak, field, grads, sums,
):
    row, col = row_ref[0], col_ref[0]
    live = live_ref[0].astype(jnp.float32)
    odd = place[0] & 1
    for member in range(8):
        lines = slice(member * 40, member * 40 + 40)
        for part in range(2):
            for block, where in enumerate((1, 2 - 2 * odd, 2 * odd)):
                first_line = block * 80 + part * 40
                field[part, where, lines, :] = stack[member, first_line : first_line + 40, :]
    lane = lax.broadcasted_iota(jnp.int32, (WIN, LANES), 1)
    back = lax.rem(LANES - col, LANES)
    ahead = lax.rem(col, LANES)
    first = lane < LANES - col

    def cut(part):
        turned = [
            pltpu.roll(field[part, block, pl.ds(row, WIN), :], back, 1) for block in range(3)
        ]
        return jnp.concatenate(
            [jnp.where(first, turned[0], turned[1]), jnp.where(first, turned[1], turned[2])], axis=1
        )

    sample_real, sample_imag = cut(0), cut(1)
    probe_real, probe_imag = probe[0], probe[1]
    exit_real = probe_real * sample_real - probe_imag * sample_imag
    exit_imag = probe_real * sample_imag + probe_imag * sample_real
    tall = (high[...], low[...])
    wide = tuple(jnp.concatenate([table[:WIN], table[WIN:]], axis=1) for table in tall)
    far_real, far_imag = transform(exit_real, exit_imag, tall, wide, -1.0)
    power = far_real * far_real + far_imag * far_imag
    factor = 1.0 - amps[0] * lax.rsqrt(jnp.maximum(power, 0.0625))
    miss_real, miss_imag = transform(far_real * factor, far_imag * factor, tall, wide, 1.0)
    miss_real = miss_real * live
    miss_imag = miss_imag * live
    light = probe_real * probe_real + probe_imag * probe_imag
    peak[...] = jnp.full((8, LANES), jnp.max(light), jnp.float32)

    terms = (
        probe_real * miss_real + probe_imag * miss_imag,
        probe_real * miss_imag - probe_imag * miss_real,
        live * light,
    )
    wrapped = lane < col
    zero = jnp.zeros((WIN, LANES), jnp.float32)
    grads[...] = jnp.zeros_like(grads)
    for part in range(3):
        start = pltpu.roll(terms[part][:, :LANES], ahead, 1)
        end = pltpu.roll(terms[part][:, LANES:], ahead, 1)
        grads[part, 0, pl.ds(row, WIN), :] = jnp.where(wrapped, zero, start)
        grads[part, 1, pl.ds(row, WIN), :] = jnp.where(wrapped, start, end)
        grads[part, 2, pl.ds(row, WIN), :] = jnp.where(wrapped, end, zero)
    window_light = live * (sample_real * sample_real + sample_imag * sample_imag)
    sums[0] = sample_real * miss_real + sample_imag * miss_imag
    sums[1] = sample_real * miss_imag - sample_imag * miss_real
    sums[2] = window_light
    total = jnp.zeros((8, LANES), jnp.float32)
    for line in range(0, WIN, 8):
        total = total + window_light[line : line + 8, :LANES] + window_light[line : line + 8, LANES:]
    for member in range(8):
        lines = slice(member * 40, member * 40 + 40)
        for out, half, block in ((keep, odd, 1), (send, 1 - odd, 2 - 2 * odd)):
            top = pl.multiple_of(half * 128 + member * 16, 16)
            for part in range(3):
                for side in range(2):
                    put = part * 32 + side * 16
                    out[member, put : put + 16, :] = sums[
                        part, pl.ds(top, 16), side * LANES : (side + 1) * LANES
                    ]
                put = PIECE + part * 40
                out[member, put : put + 40, :] = grads[part, block, lines, :]
            out[member, 96:PIECE, :] = total
        for part in range(3):
            far_out[member, part * 40 : part * 40 + 40, :] = grads[part, 2 * odd, lines, :]


def probe_kernel(place, one, two, probe, out):
    piece = (place[0] & 1) * 8 + place[1]
    summed = one[...] + two[...]
    mean = jnp.sum(summed[96:PIECE]) * (1.0 / (WIN * WIN))
    for side in range(2):
        bottom = summed[64 + side * 16 : 80 + side * 16] + 0.25 * mean + 1e-05
        for part in range(2):
            lines = part * 32 + side * 16
            top = pl.multiple_of(piece * 16, 16)
            old = probe[part, pl.ds(top, 16), side * LANES : (side + 1) * LANES]
            out[lines : lines + 16, :] = old - summed[lines : lines + 16] / bottom


def gather_kernel(place, mine, other, out):
    odd = place[0] & 1
    for source, half in ((mine, odd), (other, 1 - odd)):
        for member in range(8):
            top = pl.multiple_of(half * 128 + member * 16, 16)
            for part in range(2):
                for side in range(2):
                    lines = part * 32 + side * 16
                    out[part, pl.ds(top, 16), side * LANES : (side + 1) * LANES] = source[
                        member, lines : lines + 16, :
                    ]


def object_kernel(pieces, old, peak, out):
    summed = pieces[0, 64:184, :]
    for member in range(1, 8):
        summed = summed + pieces[member, 64:184, :]
    bottom = summed[80:120] + 0.25 * (peak[0:1, :] + 1e-06)
    out[0] = old[0] - summed[0:40] / bottom
    out[1] = old[1] - summed[40:80] / bottom


def pair_up(axis, mask):
    return [(i, i ^ mask) for i in range(lax.axis_size(axis))]


def swap(value, axis, mask):
    return lax.ppermute(value, axis, pair_up(axis, mask))


def swap_far(value):
    count = lax.axis_size("tile")
    pairs = []
    for i in range(1, count - 1, 2):
        pairs += [(i, i + 1), (i + 1, i)]
    return lax.ppermute(value, "tile", pairs)


def on_chip(value):
    return pltpu.with_memory_space_constraint(value, pltpu.VMEM)


def sum_first(value):
    total = value[0]
    for index in range(1, value.shape[0]):
        total = total + value[index]
    return total


def local(object_field, probe_field, amplitudes, row_start, column_start, live_slots):
    smem, vmem = pl.BlockSpec(memory_space=SMEM), pl.BlockSpec(memory_space=VMEM)
    place = jnp.stack([lax.axis_index("tile"), lax.axis_index("group")]).astype(jnp.int32)
    high, low = (on_chip(jnp.asarray(table)) for table in split_tables())
    probe = on_chip(probe_field)

    def buffer(*dims):
        return pltpu.VMEM(dims, jnp.float32)

    own = object_field.reshape(80, LANES)
    rows = jnp.concatenate([own, swap(own, "tile", 1), swap_far(own)], axis=0)
    stack = lax.all_to_all(jnp.broadcast_to(rows, (8, 240, LANES)), "group", 0, 0)

    keep, send, far_out, peak = pl.pallas_call(
        window_kernel,
        out_shape=(
            buffer(8, PIECE + 120, LANES),
            buffer(8, PIECE + 120, LANES),
            buffer(8, 120, LANES),
            buffer(8, LANES),
        ),
        in_specs=[smem] * 4 + [vmem] * 5,
        out_specs=(vmem,) * 4,
        scratch_shapes=[buffer(2, 3, 320, LANES), buffer(3, 3, 320, LANES), buffer(3, WIN, WIN)],
        compiler_params=pltpu.CompilerParams(vmem_limit_bytes=24 << 20),
        name="window",
    )(
        place, row_start, column_start, live_slots, on_chip(stack), probe, on_chip(amplitudes),
        high, low,
    )

    both = keep + swap(send, "tile", 1)
    eighths = lax.all_to_all(both[:, :PIECE], "group", 0, 0)
    gradient = both[:, PIECE:] + swap_far(far_out)
    total = sum_first(eighths)
    for mask in (2, 4, 8):
        total = total + swap(total, "tile", mask)
    piece = pl.pallas_call(
        probe_kernel,
        out_shape=buffer(64, LANES),
        in_specs=[smem] + [vmem] * 3,
        out_specs=vmem,
        compiler_params=pltpu.CompilerParams(vmem_limit_bytes=4 << 20),
        name="probe",
    )(place, on_chip(total), on_chip(swap(total, "tile", 28)), probe)

    outgoing = jnp.concatenate([jnp.broadcast_to(piece, (8, 64, LANES)), gradient], axis=1)
    pieces = lax.all_to_all(outgoing, "group", 0, 0)
    mine = pieces[:, :64]
    new_object = pl.pallas_call(
        object_kernel,
        out_shape=jax.ShapeDtypeStruct((2, 40, LANES), jnp.float32),
        in_specs=[vmem] * 3,
        out_specs=vmem,
        compiler_params=pltpu.CompilerParams(vmem_limit_bytes=4 << 20),
        name="object",
    )(on_chip(pieces), on_chip(object_field), peak)
    new_probe = pl.pallas_call(
        gather_kernel,
        out_shape=jax.ShapeDtypeStruct((2, WIN, WIN), jnp.float32),
        in_specs=[smem] + [vmem] * 2,
        out_specs=vmem,
        compiler_params=pltpu.CompilerParams(vmem_limit_bytes=4 << 20),
        name="gather",
    )(place, on_chip(pieces), on_chip(swap(mine, "tile", 1)))
    return new_object, new_probe


def solution(mesh):
    return jax.shard_map(
        local,
        mesh=mesh,
        in_specs=(
            P(None, "group", "tile"),
            P(),
            P(("tile", "group"), None, None),
            P(("tile", "group")),
            P(("tile", "group")),
            P(("tile", "group")),
        ),
        out_specs=(P(None, "group", "tile"), P()),
        check_vma=False,
    )
```

```python
import jax
import jax.numpy as jnp
import ml_dtypes
import numpy as np
from jax import lax
from jax.experimental import pallas as pl
from jax.experimental.pallas import tpu as pltpu
from jax.sharding import PartitionSpec as P

WIN = 256
LANES = 128
PIECE = 104
SMEM = pltpu.MemorySpace.SMEM
VMEM = pltpu.MemorySpace.VMEM


def split_tables():
    counter = np.arange(WIN)
    angles = 2.0 * np.pi / WIN * (counter[:, None] * counter[None, :] % WIN)
    cos, sin = np.cos(angles) / np.sqrt(WIN), np.sin(angles) / np.sqrt(WIN)
    both = np.concatenate([cos, sin], axis=0)
    high = both.astype(ml_dtypes.bfloat16)
    low = (both - high.astype(np.float64)).astype(ml_dtypes.bfloat16)
    return high, low


def halves(value):
    high = value.astype(jnp.bfloat16)
    low = (value - high.astype(jnp.float32)).astype(jnp.bfloat16)
    return high, low


def product(left, right):
    def dot(a, b):
        return jnp.dot(a, b, preferred_element_type=jnp.float32)

    return dot(left[0], right[0]) + dot(left[0], right[1]) + dot(left[1], right[0])


def transform(real, imag, tall, wide, sign):
    cols = product(tall, halves(jnp.concatenate([real, imag], axis=1)))
    left_real = cols[:WIN, :WIN] - sign * cols[WIN:, WIN:]
    left_imag = cols[:WIN, WIN:] + sign * cols[WIN:, :WIN]
    rows = product(halves(jnp.concatenate([left_real, left_imag], axis=0)), wide)
    right_real = rows[:WIN, :WIN] - sign * rows[WIN:, WIN:]
    right_imag = rows[WIN:, :WIN] + sign * rows[:WIN, WIN:]
    return right_real, right_imag


def window_kernel(
    place, row_ref, col_ref, live_ref, stack, probe, amps, high, low,
    keep, send, far_out, peak, field, grads, sums,
):
    row, col = row_ref[0], col_ref[0]
    live = live_ref[0].astype(jnp.float32)
    odd = place[0] & 1
    for member in range(8):
        lines = slice(member * 40, member * 40 + 40)
        for part in range(2):
            for block, where in enumerate((1, 2 - 2 * odd, 2 * odd)):
                first_line = block * 80 + part * 40
                field[part, where, lines, :] = stack[member, first_line : first_line + 40, :]
    lane = lax.broadcasted_iota(jnp.int32, (WIN, LANES), 1)
    back = lax.rem(LANES - col, LANES)
    ahead = lax.rem(col, LANES)
    first = lane < LANES - col

    def cut(part):
        turned = [
            pltpu.roll(field[part, block, pl.ds(row, WIN), :], back, 1) for block in range(3)
        ]
        return jnp.concatenate(
            [jnp.where(first, turned[0], turned[1]), jnp.where(first, turned[1], turned[2])], axis=1
        )

    sample_real, sample_imag = cut(0), cut(1)
    probe_real, probe_imag = probe[0], probe[1]
    exit_real = probe_real * sample_real - probe_imag * sample_imag
    exit_imag = probe_real * sample_imag + probe_imag * sample_real
    tall = (high[...], low[...])
    wide = tuple(jnp.concatenate([table[:WIN], table[WIN:]], axis=1) for table in tall)
    far_real, far_imag = transform(exit_real, exit_imag, tall, wide, -1.0)
    power = far_real * far_real + far_imag * far_imag
    factor = 1.0 - amps[0] * lax.rsqrt(jnp.maximum(power, 0.0625))
    miss_real, miss_imag = transform(far_real * factor, far_imag * factor, tall, wide, 1.0)
    miss_real = miss_real * live
    miss_imag = miss_imag * live
    light = probe_real * probe_real + probe_imag * probe_imag
    peak[...] = jnp.full((8, LANES), jnp.max(light), jnp.float32)

    terms = (
        probe_real * miss_real + probe_imag * miss_imag,
        probe_real * miss_imag - probe_imag * miss_real,
        live * light,
    )
    wrapped = lane < col
    zero = jnp.zeros((WIN, LANES), jnp.float32)
    grads[...] = jnp.zeros_like(grads)
    for part in range(3):
        start = pltpu.roll(terms[part][:, :LANES], ahead, 1)
        end = pltpu.roll(terms[part][:, LANES:], ahead, 1)
        grads[part, 0, pl.ds(row, WIN), :] = jnp.where(wrapped, zero, start)
        grads[part, 1, pl.ds(row, WIN), :] = jnp.where(wrapped, start, end)
        grads[part, 2, pl.ds(row, WIN), :] = jnp.where(wrapped, end, zero)
    window_light = live * (sample_real * sample_real + sample_imag * sample_imag)
    sums[0] = sample_real * miss_real + sample_imag * miss_imag
    sums[1] = sample_real * miss_imag - sample_imag * miss_real
    sums[2] = window_light
    total = jnp.zeros((8, LANES), jnp.float32)
    for line in range(0, WIN, 8):
        total = total + window_light[line : line + 8, :LANES] + window_light[line : line + 8, LANES:]
    for member in range(8):
        lines = slice(member * 40, member * 40 + 40)
        for out, half, block in ((keep, odd, 1), (send, 1 - odd, 2 - 2 * odd)):
            top = pl.multiple_of(half * 128 + member * 16, 16)
            for part in range(3):
                for side in range(2):
                    put = part * 32 + side * 16
                    out[member, put : put + 16, :] = sums[
                        part, pl.ds(top, 16), side * LANES : (side + 1) * LANES
                    ]
                put = PIECE + part * 40
                out[member, put : put + 40, :] = grads[part, block, lines, :]
            out[member, 96:PIECE, :] = total
        for part in range(3):
            far_out[member, part * 40 : part * 40 + 40, :] = grads[part, 2 * odd, lines, :]


def probe_kernel(place, one, two, probe, out):
    piece = (place[0] & 1) * 8 + place[1]
    summed = one[...] + two[...]
    mean = jnp.sum(summed[96:PIECE]) * (1.0 / (WIN * WIN))
    for side in range(2):
        bottom = summed[64 + side * 16 : 80 + side * 16] + 0.25 * mean + 1e-05
        for part in range(2):
            lines = part * 32 + side * 16
            top = pl.multiple_of(piece * 16, 16)
            old = probe[part, pl.ds(top, 16), side * LANES : (side + 1) * LANES]
            out[lines : lines + 16, :] = old - summed[lines : lines + 16] / bottom


def gather_kernel(place, mine, other, out):
    odd = place[0] & 1
    for source, half in ((mine, odd), (other, 1 - odd)):
        for member in range(8):
            top = pl.multiple_of(half * 128 + member * 16, 16)
            for part in range(2):
                for side in range(2):
                    lines = part * 32 + side * 16
                    out[part, pl.ds(top, 16), side * LANES : (side + 1) * LANES] = source[
                        member, lines : lines + 16, :
                    ]


def object_kernel(pieces, old, peak, out):
    summed = pieces[0, 64:184, :]
    for member in range(1, 8):
        summed = summed + pieces[member, 64:184, :]
    bottom = summed[80:120] + 0.25 * (peak[0:1, :] + 1e-06)
    out[0] = old[0] - summed[0:40] / bottom
    out[1] = old[1] - summed[40:80] / bottom


def pair_up(axis, mask):
    return [(i, i ^ mask) for i in range(lax.axis_size(axis))]


def swap(value, axis, mask):
    return lax.ppermute(value, axis, pair_up(axis, mask))


def swap_far(value):
    count = lax.axis_size("tile")
    pairs = []
    for i in range(1, count - 1, 2):
        pairs += [(i, i + 1), (i + 1, i)]
    return lax.ppermute(value, "tile", pairs)


def on_chip(value):
    return pltpu.with_memory_space_constraint(value, pltpu.VMEM)


def sum_first(value):
    total = value[0]
    for index in range(1, value.shape[0]):
        total = total + value[index]
    return total


def local(object_field, probe_field, amplitudes, row_start, column_start, live_slots):
    smem, vmem = pl.BlockSpec(memory_space=SMEM), pl.BlockSpec(memory_space=VMEM)
    place = jnp.stack([lax.axis_index("tile"), lax.axis_index("group")]).astype(jnp.int32)
    high, low = (on_chip(jnp.asarray(table)) for table in split_tables())
    probe = on_chip(probe_field)

    def buffer(*dims):
        return pltpu.VMEM(dims, jnp.float32)

    own = object_field.reshape(80, LANES)
    rows = (own, swap(own, "tile", 1), swap_far(own))
    rows = jnp.concatenate([jnp.broadcast_to(block, (8, 80, LANES)) for block in rows], axis=1)
    stack = lax.all_to_all(rows, "group", 0, 0)

    keep, send, far_out, peak = pl.pallas_call(
        window_kernel,
        out_shape=(
            buffer(8, PIECE + 120, LANES),
            buffer(8, PIECE + 120, LANES),
            buffer(8, 120, LANES),
            buffer(8, LANES),
        ),
        in_specs=[smem] * 4 + [vmem] * 5,
        out_specs=(vmem,) * 4,
        scratch_shapes=[buffer(2, 3, 320, LANES), buffer(3, 3, 320, LANES), buffer(3, WIN, WIN)],
        compiler_params=pltpu.CompilerParams(vmem_limit_bytes=24 << 20),
        name="window",
    )(
        place, row_start, column_start, live_slots, on_chip(stack), probe, on_chip(amplitudes),
        high, low,
    )

    got = swap(send, "tile", 1)
    eighths = lax.all_to_all(keep[:, :PIECE] + got[:, :PIECE], "group", 0, 0)
    gradient = keep[:, PIECE:] + got[:, PIECE:] + swap_far(far_out)
    total = sum_first(eighths)
    for mask in (4, 8, 28):
        total = total + swap(total, "tile", mask)
    piece = pl.pallas_call(
        probe_kernel,
        out_shape=buffer(64, LANES),
        in_specs=[smem] + [vmem] * 3,
        out_specs=vmem,
        compiler_params=pltpu.CompilerParams(vmem_limit_bytes=4 << 20),
        name="probe",
    )(place, on_chip(total), on_chip(swap(total, "tile", 2)), probe)

    outgoing = jnp.concatenate([jnp.broadcast_to(piece, (8, 64, LANES)), gradient], axis=1)
    pieces = lax.all_to_all(outgoing, "group", 0, 0)
    mine = pieces[:, :64]
    new_object = pl.pallas_call(
        object_kernel,
        out_shape=jax.ShapeDtypeStruct((2, 40, LANES), jnp.float32),
        in_specs=[vmem] * 3,
        out_specs=vmem,
        compiler_params=pltpu.CompilerParams(vmem_limit_bytes=4 << 20),
        name="object",
    )(on_chip(pieces), on_chip(object_field), peak)
    new_probe = pl.pallas_call(
        gather_kernel,
        out_shape=jax.ShapeDtypeStruct((2, WIN, WIN), jnp.float32),
        in_specs=[smem] + [vmem] * 2,
        out_specs=vmem,
        compiler_params=pltpu.CompilerParams(vmem_limit_bytes=4 << 20),
        name="gather",
    )(place, on_chip(pieces), on_chip(swap(mine, "tile", 1)))
    return new_object, new_probe


def solution(mesh):
    return jax.shard_map(
        local,
        mesh=mesh,
        in_specs=(
            P(None, "group", "tile"),
            P(),
            P(("tile", "group"), None, None),
            P(("tile", "group")),
            P(("tile", "group")),
            P(("tile", "group")),
        ),
        out_specs=(P(None, "group", "tile"), P()),
        check_vma=False,
    )
```

```python
import jax
import jax.numpy as jnp
import ml_dtypes
import numpy as np
from jax import lax
from jax.experimental import pallas as pl
from jax.experimental.pallas import tpu as pltpu
from jax.sharding import PartitionSpec as P

WIN = 256
LANES = 128
SPARE = 96
PIECE = 104
NEAR = 184
ROWS = 264
SMEM = pltpu.MemorySpace.SMEM
VMEM = pltpu.MemorySpace.VMEM


def split_tables():
    counter = np.arange(WIN)
    angles = 2.0 * np.pi / WIN * (counter[:, None] * counter[None, :] % WIN)
    cos, sin = np.cos(angles) / np.sqrt(WIN), np.sin(angles) / np.sqrt(WIN)
    both = np.concatenate([cos, sin], axis=0)
    high = both.astype(ml_dtypes.bfloat16)
    low = (both - high.astype(np.float64)).astype(ml_dtypes.bfloat16)
    return high, low


def halves(value):
    high = value.astype(jnp.bfloat16)
    low = (value - high.astype(jnp.float32)).astype(jnp.bfloat16)
    return high, low


def product(left, right):
    def dot(a, b):
        return jnp.dot(a, b, preferred_element_type=jnp.float32)

    return dot(left[0], right[0]) + dot(left[0], right[1]) + dot(left[1], right[0])


def transform(real, imag, tall, wide, sign):
    cols = product(tall, halves(jnp.concatenate([real, imag], axis=1)))
    left_real = cols[:WIN, :WIN] - sign * cols[WIN:, WIN:]
    left_imag = cols[:WIN, WIN:] + sign * cols[WIN:, :WIN]
    rows = product(halves(jnp.concatenate([left_real, left_imag], axis=0)), wide)
    right_real = rows[:WIN, :WIN] - sign * rows[WIN:, WIN:]
    right_imag = rows[WIN:, :WIN] + sign * rows[:WIN, WIN:]
    return right_real, right_imag


def window_kernel(
    place, row_ref, col_ref, live_ref, stack, probe, amps, high, low,
    keep, send, peak, field, grads, sums,
):
    row, col = row_ref[0], col_ref[0]
    live = live_ref[0].astype(jnp.float32)
    odd = place[0] & 1
    for member in range(8):
        lines = slice(member * 40, member * 40 + 40)
        for part in range(2):
            for block, where in enumerate((1, 2 - 2 * odd, 2 * odd)):
                first_line = block * 80 + part * 40
                field[part, where, lines, :] = stack[member, first_line : first_line + 40, :]
    lane = lax.broadcasted_iota(jnp.int32, (WIN, LANES), 1)
    back = lax.rem(LANES - col, LANES)
    ahead = lax.rem(col, LANES)
    first = lane < LANES - col

    def cut(part):
        turned = [
            pltpu.roll(field[part, block, pl.ds(row, WIN), :], back, 1) for block in range(3)
        ]
        return jnp.concatenate(
            [jnp.where(first, turned[0], turned[1]), jnp.where(first, turned[1], turned[2])], axis=1
        )

    sample_real, sample_imag = cut(0), cut(1)
    probe_real, probe_imag = probe[0], probe[1]
    exit_real = probe_real * sample_real - probe_imag * sample_imag
    exit_imag = probe_real * sample_imag + probe_imag * sample_real
    tall = (high[...], low[...])
    wide = tuple(jnp.concatenate([table[:WIN], table[WIN:]], axis=1) for table in tall)
    far_real, far_imag = transform(exit_real, exit_imag, tall, wide, -1.0)
    power = far_real * far_real + far_imag * far_imag
    factor = 1.0 - amps[0] * lax.rsqrt(jnp.maximum(power, 0.0625))
    miss_real, miss_imag = transform(far_real * factor, far_imag * factor, tall, wide, 1.0)
    miss_real = miss_real * live
    miss_imag = miss_imag * live
    light = probe_real * probe_real + probe_imag * probe_imag
    peak[...] = jnp.full((8, LANES), jnp.max(light), jnp.float32)

    terms = (
        probe_real * miss_real + probe_imag * miss_imag,
        probe_real * miss_imag - probe_imag * miss_real,
    )
    wrapped = lane < col
    zero = jnp.zeros((WIN, LANES), jnp.float32)
    grads[...] = jnp.zeros_like(grads)
    for part in range(2):
        start = pltpu.roll(terms[part][:, :LANES], ahead, 1)
        end = pltpu.roll(terms[part][:, LANES:], ahead, 1)
        grads[part, 0, pl.ds(row, WIN), :] = jnp.where(wrapped, zero, start)
        grads[part, 1, pl.ds(row, WIN), :] = jnp.where(wrapped, start, end)
        grads[part, 2, pl.ds(row, WIN), :] = jnp.where(wrapped, end, zero)
    window_light = live * (sample_real * sample_real + sample_imag * sample_imag)
    sums[0] = sample_real * miss_real + sample_imag * miss_imag
    sums[1] = sample_real * miss_imag - sample_imag * miss_real
    sums[2] = window_light
    total = jnp.zeros((8, LANES), jnp.float32)
    for line in range(0, WIN, 8):
        total = total + window_light[line : line + 8, :LANES] + window_light[line : line + 8, LANES:]
    spare_line = lax.broadcasted_iota(jnp.int32, (8, LANES), 0)
    spare_lane = lax.broadcasted_iota(jnp.int32, (8, LANES), 1)
    where_mine = jnp.where(
        spare_lane == 0,
        row.astype(jnp.float32),
        jnp.where(spare_lane == 1, col.astype(jnp.float32), jnp.where(spare_lane == 2, live, 0.0)),
    )
    spare = jnp.where(
        spare_line == 0,
        jnp.broadcast_to(jnp.sum(total, axis=0, keepdims=True), (8, LANES)),
        jnp.where(spare_line == 1 + odd, where_mine, 0.0),
    )
    for member in range(8):
        lines = slice(member * 40, member * 40 + 40)
        for out, half, block in ((keep, odd, 1), (send, 1 - odd, 2 - 2 * odd)):
            top = pl.multiple_of(half * 128 + member * 16, 16)
            for part in range(3):
                for side in range(2):
                    put = part * 32 + side * 16
                    out[member, put : put + 16, :] = sums[
                        part, pl.ds(top, 16), side * LANES : (side + 1) * LANES
                    ]
            out[member, SPARE:PIECE, :] = spare
            for part in range(2):
                put = PIECE + part * 40
                out[member, put : put + 40, :] = grads[part, block, lines, :]
        for part in range(2):
            put = NEAR + part * 40
            keep[member, put : put + 40, :] = grads[part, 2 * odd, lines, :]


def pack_kernel(own, near, far, out):
    for member in range(8):
        out[member, 0:80, :] = own[...]
        out[member, 80:160, :] = near[...]
        out[member, 160:240, :] = far[...]


def merge_kernel(keep, got, out):
    out[:, :NEAR, :] = keep[:, :NEAR, :] + got[...]
    out[:, NEAR:, :] = keep[:, NEAR:, :]


def reduce_kernel(place, pieces, probe_sum, own_sum, far_sum):
    def added(start, end):
        total = pieces[0, start:end, :]
        for member in range(1, 8):
            total = total + pieces[member, start:end, :]
        return total

    probe_sum[...] = added(0, PIECE)
    own_sum[...] = added(PIECE, NEAR)
    far_sum[0:80, :] = added(NEAR, ROWS)
    line = lax.broadcasted_iota(jnp.int32, (8, LANES), 0)
    mine = jnp.zeros((8, LANES), jnp.float32)
    for member in range(8):
        spare = pieces[member, SPARE:PIECE, :]
        place_row = jnp.where((place[0] & 1) == 1, spare[2:3], spare[1:2])
        mine = jnp.where(line == member, place_row, mine)
    far_sum[80:88, :] = mine


def probe_kernel(place, one, two, probe, out):
    piece = (place[0] & 1) * 8 + place[1]
    summed = one[...] + two[...]
    mean = jnp.sum(summed[SPARE : SPARE + 1]) * (1.0 / (WIN * WIN))
    for side in range(2):
        bottom = summed[64 + side * 16 : 80 + side * 16] + 0.25 * mean + 1e-05
        for part in range(2):
            lines = part * 32 + side * 16
            top = pl.multiple_of(piece * 16, 16)
            old = probe[part, pl.ds(top, 16), side * LANES : (side + 1) * LANES]
            new = old - summed[lines : lines + 16] / bottom
            for member in range(8):
                out[member, lines : lines + 16, :] = new


def gather_kernel(place, mine, other, out):
    odd = place[0] & 1
    for source, half in ((mine, odd), (other, 1 - odd)):
        for member in range(8):
            top = pl.multiple_of(half * 128 + member * 16, 16)
            for part in range(2):
                for side in range(2):
                    lines = part * 32 + side * 16
                    out[part, pl.ds(top, 16), side * LANES : (side + 1) * LANES] = source[
                        member, lines : lines + 16, :
                    ]


def object_kernel(place, pieces, own_sum, far_sum, old, probe, peak, out, light, near_at, far_at, sems):
    copies = [
        pltpu.make_async_copy(pieces.at[:, SPARE:PIECE, :], near_at, sems.at[0]),
        pltpu.make_async_copy(far_sum.at[80:88, :], far_at, sems.at[1]),
    ]
    for copy in copies:
        copy.start()
    odd = place[0] & 1
    blank = jnp.zeros((64, LANES), jnp.float32)
    for side in range(2):
        cols = slice(side * LANES, (side + 1) * LANES)
        light[1 + side, 64:320, :] = probe[0, :, cols] * probe[0, :, cols] + (
            probe[1, :, cols] * probe[1, :, cols]
        )
        light[1 + side, 0:64, :] = blank
        light[1 + side, 320:384, :] = blank
        light[3 * side, :, :] = jnp.zeros((384, LANES), jnp.float32)
    for copy in copies:
        copy.wait()
    lane = lax.broadcasted_iota(jnp.int32, (40, LANES), 1)

    def shine(total, row, col, live, block):
        row, col = row.astype(jnp.int32), col.astype(jnp.int32)
        top = 64 + place[1] * 40 - row
        turn = lax.rem(col, LANES)
        before = pltpu.roll(light[block, pl.ds(top, 40), :], turn, 1)
        after = pltpu.roll(light[block + 1, pl.ds(top, 40), :], turn, 1)
        return total + live * jnp.where(lane < col, before, after)

    total = jnp.zeros((40, LANES), jnp.float32)
    for member in range(8):
        for core in range(2):
            block = 1 + core * (1 - odd) * -1 + (1 - core) * odd
            at = [near_at[member, 1 + core, k] for k in range(3)]
            total = shine(total, *at, block)
        total = shine(total, *[far_at[member, k] for k in range(3)], 2 - 2 * odd)
    bottom = total + 0.25 * (peak[0:1, :] + 1e-06)
    for part in range(2):
        lines = slice(part * 40, part * 40 + 40)
        out[part] = old[part] - (own_sum[lines, :] + far_sum[lines, :]) / bottom


def pair_up(axis, mask):
    return [(i, i ^ mask) for i in range(lax.axis_size(axis))]


def swap(value, axis, mask):
    return lax.ppermute(value, axis, pair_up(axis, mask))


def swap_far(value):
    count = lax.axis_size("tile")
    pairs = []
    for i in range(1, count - 1, 2):
        pairs += [(i, i + 1), (i + 1, i)]
    return lax.ppermute(value, "tile", pairs)


def on_chip(value):
    return pltpu.with_memory_space_constraint(value, pltpu.VMEM)


def kernel_call(body, out_shape, in_specs, out_specs, megabytes, **kwargs):
    return pl.pallas_call(
        body,
        out_shape=out_shape,
        in_specs=in_specs,
        out_specs=out_specs,
        compiler_params=pltpu.CompilerParams(vmem_limit_bytes=megabytes << 20),
        name=body.__name__.removesuffix("_kernel"),
        **kwargs,
    )


def local(object_field, probe_field, amplitudes, row_start, column_start, live_slots):
    smem, vmem = pl.BlockSpec(memory_space=SMEM), pl.BlockSpec(memory_space=VMEM)
    place = jnp.stack([lax.axis_index("tile"), lax.axis_index("group")]).astype(jnp.int32)
    high, low = (on_chip(jnp.asarray(table)) for table in split_tables())
    probe = on_chip(probe_field)

    def buffer(*dims):
        return pltpu.VMEM(dims, jnp.float32)

    own = object_field.reshape(80, LANES)
    near, far = swap(own, "tile", 1), swap_far(own)
    rows = kernel_call(pack_kernel, buffer(8, 240, LANES), [vmem] * 3, vmem, 4)(
        *map(on_chip, (own, near, far))
    )
    stack = lax.all_to_all(rows, "group", 0, 0)
    keep, send, peak = kernel_call(
        window_kernel,
        (buffer(8, ROWS, LANES), buffer(8, NEAR, LANES), buffer(8, LANES)),
        [smem] * 4 + [vmem] * 5,
        (vmem,) * 3,
        24,
        scratch_shapes=[buffer(2, 3, 320, LANES), buffer(2, 3, 320, LANES), buffer(3, WIN, WIN)],
    )(
        place, row_start, column_start, live_slots, on_chip(stack), probe, on_chip(amplitudes),
        high, low,
    )

    merged = kernel_call(merge_kernel, buffer(8, ROWS, LANES), [vmem] * 2, vmem, 4)(
        keep, on_chip(swap(send, "tile", 1))
    )
    pieces = on_chip(lax.all_to_all(merged, "group", 0, 0))
    total, own_sum, far_sum = kernel_call(
        reduce_kernel,
        (buffer(PIECE, LANES), buffer(80, LANES), buffer(88, LANES)),
        [smem, vmem],
        (vmem,) * 3,
        4,
    )(place, pieces)
    far_got = swap_far(far_sum)
    for mask in (4, 8, 28):
        total = total + swap(total, "tile", mask)
    piece = kernel_call(probe_kernel, buffer(8, 64, LANES), [smem] + [vmem] * 3, vmem, 4)(
        place, on_chip(total), on_chip(swap(total, "tile", 2)), probe
    )
    new_object = kernel_call(
        object_kernel,
        jax.ShapeDtypeStruct((2, 40, LANES), jnp.float32),
        [smem] + [vmem] * 6,
        vmem,
        8,
        scratch_shapes=[
            buffer(4, 384, LANES),
            pltpu.SMEM((8, 8, LANES), jnp.float32),
            pltpu.SMEM((8, LANES), jnp.float32),
            pltpu.SemaphoreType.DMA((2,)),
        ],
    )(place, pieces, own_sum, on_chip(far_got), on_chip(object_field), probe, peak)

    mine = lax.all_to_all(piece, "group", 0, 0)
    new_probe = kernel_call(
        gather_kernel,
        jax.ShapeDtypeStruct((2, WIN, WIN), jnp.float32),
        [smem] + [vmem] * 2,
        vmem,
        4,
    )(place, on_chip(mine), on_chip(swap(mine, "tile", 1)))
    return new_object, new_probe


def solution(mesh):
    return jax.shard_map(
        local,
        mesh=mesh,
        in_specs=(
            P(None, "group", "tile"),
            P(),
            P(("tile", "group"), None, None),
            P(("tile", "group")),
            P(("tile", "group")),
            P(("tile", "group")),
        ),
        out_specs=(P(None, "group", "tile"), P()),
        check_vma=False,
    )
```

```python
import jax
import jax.numpy as jnp
import ml_dtypes
import numpy as np
from jax import lax
from jax.experimental import pallas as pl
from jax.experimental.pallas import tpu as pltpu
from jax.sharding import PartitionSpec as P

WIN = 256
LANES = 128
SPARE = 96
PIECE = 104
NEAR = 184
LAST = 152
SMEM = pltpu.MemorySpace.SMEM
VMEM = pltpu.MemorySpace.VMEM


def split_tables():
    counter = np.arange(WIN)
    angles = 2.0 * np.pi / WIN * (counter[:, None] * counter[None, :] % WIN)
    cos, sin = np.cos(angles) / np.sqrt(WIN), np.sin(angles) / np.sqrt(WIN)
    both = np.concatenate([cos, sin], axis=0)
    high = both.astype(ml_dtypes.bfloat16)
    low = (both - high.astype(np.float64)).astype(ml_dtypes.bfloat16)
    return high, low


def halves(value):
    high = value.astype(jnp.bfloat16)
    low = (value - high.astype(jnp.float32)).astype(jnp.bfloat16)
    return high, low


def product(left, right):
    def dot(a, b):
        return jnp.dot(a, b, preferred_element_type=jnp.float32)

    return dot(left[0], right[0]) + dot(left[0], right[1]) + dot(left[1], right[0])


def transform(real, imag, tall, wide, sign):
    cols = product(tall, halves(jnp.concatenate([real, imag], axis=1)))
    left_real = cols[:WIN, :WIN] - sign * cols[WIN:, WIN:]
    left_imag = cols[:WIN, WIN:] + sign * cols[WIN:, :WIN]
    rows = product(halves(jnp.concatenate([left_real, left_imag], axis=0)), wide)
    right_real = rows[:WIN, :WIN] - sign * rows[WIN:, WIN:]
    right_imag = rows[WIN:, :WIN] + sign * rows[:WIN, WIN:]
    return right_real, right_imag


def window_kernel(
    place, row_ref, col_ref, live_ref, stack, near, probe, amps, high, low,
    keep, send, far_out, peak, field, grads, sums,
):
    row, col = row_ref[0], col_ref[0]
    live = live_ref[0].astype(jnp.float32)
    odd = place[0] & 1
    for member in range(8):
        lines = slice(member * 40, member * 40 + 40)
        for part in range(2):
            field[part, 1, lines, :] = stack[member, part * 40 : part * 40 + 40, :]
            field[part, 2 * odd, lines, :] = stack[member, 80 + part * 40 : 120 + part * 40, :]
            field[part, 2 - 2 * odd, lines, :] = near[member, part * 40 : part * 40 + 40, :]
    lane = lax.broadcasted_iota(jnp.int32, (WIN, LANES), 1)
    back = lax.rem(LANES - col, LANES)
    ahead = lax.rem(col, LANES)
    first = lane < LANES - col

    def cut(part):
        turned = [
            pltpu.roll(field[part, block, pl.ds(row, WIN), :], back, 1) for block in range(3)
        ]
        return jnp.concatenate(
            [jnp.where(first, turned[0], turned[1]), jnp.where(first, turned[1], turned[2])], axis=1
        )

    sample_real, sample_imag = cut(0), cut(1)
    probe_real, probe_imag = probe[0], probe[1]
    exit_real = probe_real * sample_real - probe_imag * sample_imag
    exit_imag = probe_real * sample_imag + probe_imag * sample_real
    tall = (high[...], low[...])
    wide = tuple(jnp.concatenate([table[:WIN], table[WIN:]], axis=1) for table in tall)
    far_real, far_imag = transform(exit_real, exit_imag, tall, wide, -1.0)
    power = far_real * far_real + far_imag * far_imag
    factor = 1.0 - amps[0] * lax.rsqrt(jnp.maximum(power, 0.0625))
    miss_real, miss_imag = transform(far_real * factor, far_imag * factor, tall, wide, 1.0)
    miss_real = miss_real * live
    miss_imag = miss_imag * live
    light = probe_real * probe_real + probe_imag * probe_imag
    peak[...] = jnp.full((8, LANES), jnp.max(light), jnp.float32)

    terms = (
        probe_real * miss_real + probe_imag * miss_imag,
        probe_real * miss_imag - probe_imag * miss_real,
    )
    wrapped = lane < col
    zero = jnp.zeros((WIN, LANES), jnp.float32)
    grads[...] = jnp.zeros_like(grads)
    for part in range(2):
        start = pltpu.roll(terms[part][:, :LANES], ahead, 1)
        end = pltpu.roll(terms[part][:, LANES:], ahead, 1)
        grads[part, 0, pl.ds(row, WIN), :] = jnp.where(wrapped, zero, start)
        grads[part, 1, pl.ds(row, WIN), :] = jnp.where(wrapped, start, end)
        grads[part, 2, pl.ds(row, WIN), :] = jnp.where(wrapped, end, zero)
    window_light = live * (sample_real * sample_real + sample_imag * sample_imag)
    sums[0] = sample_real * miss_real + sample_imag * miss_imag
    sums[1] = sample_real * miss_imag - sample_imag * miss_real
    sums[2] = window_light
    total = jnp.zeros((8, LANES), jnp.float32)
    for line in range(0, WIN, 8):
        total = total + window_light[line : line + 8, :LANES] + window_light[line : line + 8, LANES:]
    spare_line = lax.broadcasted_iota(jnp.int32, (8, LANES), 0)
    spare_lane = lax.broadcasted_iota(jnp.int32, (8, LANES), 1)
    where_mine = jnp.where(
        spare_lane == 0,
        row.astype(jnp.float32),
        jnp.where(spare_lane == 1, col.astype(jnp.float32), jnp.where(spare_lane == 2, live, 0.0)),
    )
    spare = jnp.where(
        spare_line == 0,
        jnp.broadcast_to(jnp.sum(total, axis=0, keepdims=True), (8, LANES)),
        jnp.where(spare_line == 1 + odd, where_mine, 0.0),
    )
    for member in range(8):
        lines = slice(member * 40, member * 40 + 40)
        for out, half, block in ((keep, odd, 1), (send, 1 - odd, 2 - 2 * odd)):
            top = pl.multiple_of(half * 128 + member * 16, 16)
            for part in range(3):
                for side in range(2):
                    put = part * 32 + side * 16
                    out[member, put : put + 16, :] = sums[
                        part, pl.ds(top, 16), side * LANES : (side + 1) * LANES
                    ]
            out[member, SPARE:PIECE, :] = spare
            for part in range(2):
                put = PIECE + part * 40
                out[member, put : put + 40, :] = grads[part, block, lines, :]
        for part in range(2):
            put = member * 80 + part * 40
            far_out[put : put + 40, :] = grads[part, 2 * odd, lines, :]
    far_out[640:648, :] = where_mine


def pack_kernel(own, far, out, sems):
    copies = [
        pltpu.make_async_copy(own, out.at[member, 0:80, :], sems.at[member]) for member in range(8)
    ]
    for copy in copies:
        copy.start()
    for member in range(8):
        out[member, 80:160, :] = far[...]
    for copy in copies:
        copy.wait()


def merge_kernel(keep, got, sums, gradient):
    sums[...] = keep[:, :PIECE, :] + got[:, :PIECE, :]
    gradient[...] = keep[:, PIECE:, :] + got[:, PIECE:, :]


def reduce_kernel(pieces, out):
    total = pieces[0]
    for member in range(1, 8):
        total = total + pieces[member]
    out[...] = total


def probe_kernel(place, one, two, probe, gradient, far, out):
    piece = (place[0] & 1) * 8 + place[1]
    summed = one[...] + two[...]
    mean = jnp.sum(summed[SPARE : SPARE + 1]) * (1.0 / (WIN * WIN))
    for side in range(2):
        bottom = summed[64 + side * 16 : 80 + side * 16] + 0.25 * mean + 1e-05
        for part in range(2):
            lines = part * 32 + side * 16
            top = pl.multiple_of(piece * 16, 16)
            old = probe[part, pl.ds(top, 16), side * LANES : (side + 1) * LANES]
            new = old - summed[lines : lines + 16] / bottom
            for member in range(8):
                out[member, lines : lines + 16, :] = new
    for member in range(8):
        out[member, 64:144, :] = gradient[member] + far[member * 80 : member * 80 + 80, :]
        out[member, 144:LAST, :] = far[640:648, :]


def gather_kernel(place, mine, other, out):
    odd = place[0] & 1
    for source, half in ((mine, odd), (other, 1 - odd)):
        for member in range(8):
            top = pl.multiple_of(half * 128 + member * 16, 16)
            for part in range(2):
                for side in range(2):
                    lines = part * 32 + side * 16
                    out[part, pl.ds(top, 16), side * LANES : (side + 1) * LANES] = source[
                        member, lines : lines + 16, :
                    ]


def shine(light, group, total, at, block):
    row, col = at[0].astype(jnp.int32), at[1].astype(jnp.int32)
    top = 64 + group * 40 - row
    turn = lax.rem(col, LANES)
    lane = lax.broadcasted_iota(jnp.int32, (40, LANES), 1)
    before = pltpu.roll(light[block, pl.ds(top, 40), :], turn, 1)
    after = pltpu.roll(light[block + 1, pl.ds(top, 40), :], turn, 1)
    return total + at[2] * jnp.where(lane < col, before, after)


def light_kernel(place, pieces, probe, out, light, at, sem):
    copy = pltpu.make_async_copy(pieces.at[:, SPARE:PIECE, :], at, sem)
    copy.start()
    odd = place[0] & 1
    blank = jnp.zeros((64, LANES), jnp.float32)
    for side in range(2):
        cols = slice(side * LANES, (side + 1) * LANES)
        light[1 + side, 64:320, :] = probe[0, :, cols] * probe[0, :, cols] + (
            probe[1, :, cols] * probe[1, :, cols]
        )
        light[1 + side, 0:64, :] = blank
        light[1 + side, 320:384, :] = blank
        light[3 * side, :, :] = jnp.zeros((384, LANES), jnp.float32)
    copy.wait()
    total = jnp.zeros((40, LANES), jnp.float32)
    for member in range(8):
        for core in range(2):
            block = 1 - core * (1 - odd) + (1 - core) * odd
            total = shine(light, place[1], total, [at[member, 1 + core, k] for k in range(3)], block)
    out[...] = total


def object_kernel(place, pieces, old, near_light, light, peak, out, at, sem):
    copy = pltpu.make_async_copy(pieces.at[:, 144:LAST, :], at, sem)
    copy.start()
    summed = pieces[0, 64:144, :]
    for member in range(1, 8):
        summed = summed + pieces[member, 64:144, :]
    copy.wait()
    total = near_light[...]
    block = 2 - 2 * (place[0] & 1)
    for member in range(8):
        total = shine(light, place[1], total, [at[member, 0, k] for k in range(3)], block)
    bottom = total + 0.25 * (peak[0:1, :] + 1e-06)
    for part in range(2):
        out[part] = old[part] - summed[part * 40 : part * 40 + 40, :] / bottom


def pair_up(axis, mask):
    return [(i, i ^ mask) for i in range(lax.axis_size(axis))]


def swap(value, axis, mask):
    return lax.ppermute(value, axis, pair_up(axis, mask))


def swap_far(value):
    count = lax.axis_size("tile")
    pairs = []
    for i in range(1, count - 1, 2):
        pairs += [(i, i + 1), (i + 1, i)]
    return lax.ppermute(value, "tile", pairs)


def on_chip(value):
    return pltpu.with_memory_space_constraint(value, pltpu.VMEM)


def kernel_call(body, out_shape, in_specs, out_specs, megabytes, **kwargs):
    return pl.pallas_call(
        body,
        out_shape=out_shape,
        in_specs=in_specs,
        out_specs=out_specs,
        compiler_params=pltpu.CompilerParams(vmem_limit_bytes=megabytes << 20),
        name=body.__name__.removesuffix("_kernel"),
        **kwargs,
    )


def local(object_field, probe_field, amplitudes, row_start, column_start, live_slots):
    smem, vmem = pl.BlockSpec(memory_space=SMEM), pl.BlockSpec(memory_space=VMEM)
    place = jnp.stack([lax.axis_index("tile"), lax.axis_index("group")]).astype(jnp.int32)
    high, low = (on_chip(jnp.asarray(table)) for table in split_tables())
    probe = on_chip(probe_field)

    def buffer(*dims):
        return pltpu.VMEM(dims, jnp.float32)

    own = object_field.reshape(80, LANES)
    rows = kernel_call(
        pack_kernel,
        buffer(8, 160, LANES),
        [pl.BlockSpec(memory_space=pltpu.MemorySpace.HBM), vmem],
        vmem,
        4,
        scratch_shapes=[pltpu.SemaphoreType.DMA((8,))],
    )(own, on_chip(swap_far(own)))
    stack = lax.all_to_all(rows, "group", 0, 0)
    near = swap(stack[:, :80], "tile", 1)
    keep, send, far_out, peak = kernel_call(
        window_kernel,
        (buffer(8, NEAR, LANES), buffer(8, NEAR, LANES), buffer(648, LANES), buffer(8, LANES)),
        [smem] * 4 + [vmem] * 6,
        (vmem,) * 4,
        24,
        scratch_shapes=[buffer(2, 3, 320, LANES), buffer(2, 3, 320, LANES), buffer(3, WIN, WIN)],
    )(
        place, row_start, column_start, live_slots, on_chip(stack), on_chip(near), probe,
        on_chip(amplitudes), high, low,
    )

    sums, gradient = kernel_call(
        merge_kernel, (buffer(8, PIECE, LANES), buffer(8, 80, LANES)), [vmem] * 2, (vmem,) * 2, 4
    )(keep, on_chip(swap(send, "tile", 1)))
    pieces = lax.all_to_all(sums, "group", 0, 0)
    pieces, far_out = lax.optimization_barrier((pieces, far_out))
    far_got = swap_far(far_out)
    total = kernel_call(reduce_kernel, buffer(PIECE, LANES), [vmem], vmem, 4)(on_chip(pieces))
    near_light, light = kernel_call(
        light_kernel,
        (buffer(40, LANES), buffer(4, 384, LANES)),
        [smem] + [vmem] * 2,
        (vmem,) * 2,
        4,
        scratch_shapes=[pltpu.SMEM((8, 8, LANES), jnp.float32), pltpu.SemaphoreType.DMA],
        cost_estimate=pl.CostEstimate(flops=500000, bytes_accessed=1500000, transcendentals=0),
    )(place, on_chip(pieces), probe)
    for mask in (4, 8, 28):
        total = total + swap(total, "tile", mask)
    total, near_light = lax.optimization_barrier((total, near_light))
    outgoing = kernel_call(probe_kernel, buffer(8, LAST, LANES), [smem] + [vmem] * 5, vmem, 8)(
        place, on_chip(total), on_chip(swap(total, "tile", 2)), probe, gradient, on_chip(far_got)
    )

    arrived = lax.all_to_all(outgoing, "group", 0, 0)
    other = swap(arrived[:, :64], "tile", 1)
    new_object = kernel_call(
        object_kernel,
        jax.ShapeDtypeStruct((2, 40, LANES), jnp.float32),
        [smem] + [vmem] * 5,
        vmem,
        4,
        scratch_shapes=[pltpu.SMEM((8, 8, LANES), jnp.float32), pltpu.SemaphoreType.DMA],
    )(place, on_chip(arrived), on_chip(object_field), on_chip(near_light), light, peak)
    new_probe = kernel_call(
        gather_kernel,
        jax.ShapeDtypeStruct((2, WIN, WIN), jnp.float32),
        [smem] + [vmem] * 2,
        vmem,
        4,
    )(place, on_chip(arrived), on_chip(other))
    return new_object, new_probe


def solution(mesh):
    return jax.shard_map(
        local,
        mesh=mesh,
        in_specs=(
            P(None, "group", "tile"),
            P(),
            P(("tile", "group"), None, None),
            P(("tile", "group")),
            P(("tile", "group")),
            P(("tile", "group")),
        ),
        out_specs=(P(None, "group", "tile"), P()),
        check_vma=False,
    )
```

```python
import jax
import jax.numpy as jnp
import ml_dtypes
import numpy as np
from jax import lax
from jax.experimental import pallas as pl
from jax.experimental.pallas import tpu as pltpu
from jax.sharding import PartitionSpec as P

WIN = 256
LANES = 128
TILES = 32
SPARE = 48
PIECE = 56
LINES = 136
SMEM = pltpu.MemorySpace.SMEM
VMEM = pltpu.MemorySpace.VMEM


def split_tables():
    counter = np.arange(WIN)
    angles = 2.0 * np.pi / WIN * (counter[:, None] * counter[None, :] % WIN)
    cos, sin = np.cos(angles) / np.sqrt(WIN), np.sin(angles) / np.sqrt(WIN)
    both = np.concatenate([cos, sin], axis=0)
    high = both.astype(ml_dtypes.bfloat16)
    low = (both - high.astype(np.float64)).astype(ml_dtypes.bfloat16)
    return high, low


def halves(value):
    high = value.astype(jnp.bfloat16)
    low = (value - high.astype(jnp.float32)).astype(jnp.bfloat16)
    return high, low


def product(left, right):
    def dot(a, b):
        return jnp.dot(a, b, preferred_element_type=jnp.float32)

    return dot(left[0], right[0]) + dot(left[0], right[1]) + dot(left[1], right[0])


def transform(real, imag, tall, wide, sign):
    cols = product(tall, halves(jnp.concatenate([real, imag], axis=1)))
    left_real = cols[:WIN, :WIN] - sign * cols[WIN:, WIN:]
    left_imag = cols[:WIN, WIN:] + sign * cols[WIN:, :WIN]
    rows = product(halves(jnp.concatenate([left_real, left_imag], axis=0)), wide)
    right_real = rows[:WIN, :WIN] - sign * rows[WIN:, WIN:]
    right_imag = rows[WIN:, :WIN] + sign * rows[:WIN, WIN:]
    return right_real, right_imag


def window_kernel(
    place, row_ref, col_ref, live_ref, stack, near, probe, amps, high, low,
    keep, send, peak, field, grads, sums,
):
    row, col = row_ref[0], col_ref[0]
    live = live_ref[0].astype(jnp.float32)
    odd, half = place[0] & 1, half_of(place[0])
    inside = far_exists(place[0])
    for member in range(8):
        lines = slice(member * 40, member * 40 + 40)
        for part in range(2):
            rows = slice(part * 40, part * 40 + 40)
            field[part, 1, lines, :] = stack[8 - 8 * odd + member, rows, :]
            field[part, 2 * odd, lines, :] = jnp.where(inside, stack[8 * odd + member, rows, :], 0.0)
            field[part, 2 - 2 * odd, lines, :] = near[8 * odd + member, rows, :]
    lane = lax.broadcasted_iota(jnp.int32, (WIN, LANES), 1)
    back = lax.rem(LANES - col, LANES)
    ahead = lax.rem(col, LANES)
    first = lane < LANES - col

    def cut(part):
        turned = [
            pltpu.roll(field[part, block, pl.ds(row, WIN), :], back, 1) for block in range(3)
        ]
        return jnp.concatenate(
            [jnp.where(first, turned[0], turned[1]), jnp.where(first, turned[1], turned[2])], axis=1
        )

    sample_real, sample_imag = cut(0), cut(1)
    probe_real, probe_imag = probe[0], probe[1]
    exit_real = probe_real * sample_real - probe_imag * sample_imag
    exit_imag = probe_real * sample_imag + probe_imag * sample_real
    tall = (high[...], low[...])
    wide = tuple(jnp.concatenate([table[:WIN], table[WIN:]], axis=1) for table in tall)
    far_real, far_imag = transform(exit_real, exit_imag, tall, wide, -1.0)
    power = far_real * far_real + far_imag * far_imag
    factor = 1.0 - amps[0] * lax.rsqrt(jnp.maximum(power, 0.0625))
    miss_real, miss_imag = transform(far_real * factor, far_imag * factor, tall, wide, 1.0)
    miss_real = miss_real * live
    miss_imag = miss_imag * live
    light = probe_real * probe_real + probe_imag * probe_imag
    peak[...] = jnp.full((8, LANES), jnp.max(light), jnp.float32)

    terms = (
        probe_real * miss_real + probe_imag * miss_imag,
        probe_real * miss_imag - probe_imag * miss_real,
    )
    wrapped = lane < col
    zero = jnp.zeros((WIN, LANES), jnp.float32)
    grads[...] = jnp.zeros_like(grads)
    for part in range(2):
        start = pltpu.roll(terms[part][:, :LANES], ahead, 1)
        end = pltpu.roll(terms[part][:, LANES:], ahead, 1)
        grads[part, 0, pl.ds(row, WIN), :] = jnp.where(wrapped, zero, start)
        grads[part, 1, pl.ds(row, WIN), :] = jnp.where(wrapped, start, end)
        grads[part, 2, pl.ds(row, WIN), :] = jnp.where(wrapped, end, zero)
    window_light = live * (sample_real * sample_real + sample_imag * sample_imag)
    sums[0] = sample_real * miss_real + sample_imag * miss_imag
    sums[1] = sample_real * miss_imag - sample_imag * miss_real
    sums[2] = window_light
    total = jnp.zeros((8, LANES), jnp.float32)
    for line in range(0, WIN, 8):
        total = total + window_light[line : line + 8, :LANES] + window_light[line : line + 8, LANES:]
    spare_line = lax.broadcasted_iota(jnp.int32, (8, LANES), 0)
    spare_lane = lax.broadcasted_iota(jnp.int32, (8, LANES), 1)
    where_mine = jnp.where(
        spare_lane == 0,
        row.astype(jnp.float32),
        jnp.where(spare_lane == 1, col.astype(jnp.float32), jnp.where(spare_lane == 2, live, 0.0)),
    )
    spare = jnp.where(
        spare_line == 2,
        jnp.broadcast_to(jnp.sum(total, axis=0, keepdims=True), (8, LANES)),
        jnp.where(spare_line == odd, where_mine, 0.0),
    )
    for member in range(16):
        for kept, side_half in ((True, half), (False, 1 - half)):
            top = pl.multiple_of(side_half * 128 + member * 8, 8)
            for part in range(3):
                for side in range(2):
                    put = part * 16 + side * 8
                    value = sums[part, pl.ds(top, 8), side * LANES : (side + 1) * LANES]
                    if kept:
                        keep[member, put : put + 8, :] = value
                    else:
                        send[member * PIECE + put : member * PIECE + put + 8, :] = value
            if kept:
                keep[member, SPARE:PIECE, :] = spare
            else:
                send[member * PIECE + SPARE : member * PIECE + PIECE, :] = spare
    for member in range(8):
        lines = slice(member * 40, member * 40 + 40)
        for part in range(2):
            put = PIECE + part * 40
            keep[8 - 8 * odd + member, put : put + 40, :] = grads[part, 1, lines, :]
            keep[8 * odd + member, put : put + 40, :] = jnp.where(
                inside, grads[part, 2 * odd, lines, :], 0.0
            )
            put = 16 * PIECE + member * 80 + part * 40
            send[put : put + 40, :] = grads[part, 2 - 2 * odd, lines, :]


def merge_kernel(place, keep, got, out):
    mine = 8 - 8 * (place[0] & 1)
    for member in range(16):
        out[member, :PIECE, :] = keep[member, :PIECE, :] + got[member * PIECE : (member + 1) * PIECE, :]
    for member in range(8):
        put = 16 * PIECE + member * 80
        out[mine + member, PIECE:, :] = keep[mine + member, PIECE:, :] + got[put : put + 80, :]
        out[8 - mine + member, PIECE:, :] = keep[8 - mine + member, PIECE:, :]


def reduce_kernel(pieces, probe_sum, gradient):
    total = pieces[0]
    for member in range(1, 16):
        total = total + pieces[member]
    probe_sum[...] = total[:PIECE]
    gradient[...] = total[PIECE:]


def probe_kernel(place, one, two, probe, out):
    odd = place[0] & 1
    top = pl.multiple_of(half_of(place[0]) * 128 + (8 - 8 * odd + place[1]) * 8, 8)
    summed = one[...] + two[...]
    mean = jnp.sum(summed[SPARE + 2 : SPARE + 3]) * (1.0 / (WIN * WIN))
    for side in range(2):
        bottom = summed[32 + side * 8 : 40 + side * 8] + 0.25 * mean + 1e-05
        for part in range(2):
            lines = part * 16 + side * 8
            old = probe[part, pl.ds(top, 8), side * LANES : (side + 1) * LANES]
            new = old - summed[lines : lines + 8] / bottom
            for member in range(16):
                out[member, lines : lines + 8, :] = new


def gather_kernel(place, mine, other, out):
    half = half_of(place[0])
    for source, which in ((mine, half), (other, 1 - half)):
        for member in range(16):
            top = pl.multiple_of(which * 128 + member * 8, 8)
            for part in range(2):
                for side in range(2):
                    lines = part * 16 + side * 8
                    out[part, pl.ds(top, 8), side * LANES : (side + 1) * LANES] = source[
                        member, lines : lines + 8, :
                    ]


def shine(light, group, total, at, block):
    row, col = at[0].astype(jnp.int32), at[1].astype(jnp.int32)
    top = 64 + group * 40 - row
    turn = lax.rem(col, LANES)
    lane = lax.broadcasted_iota(jnp.int32, (40, LANES), 1)
    before = pltpu.roll(light[block, pl.ds(top, 40), :], turn, 1)
    after = pltpu.roll(light[block + 1, pl.ds(top, 40), :], turn, 1)
    return total + at[2] * jnp.where(lane < col, before, after)


def object_kernel(place, pieces, gradient, old, probe, peak, out, light, at, sem):
    copy = pltpu.make_async_copy(pieces.at[:, SPARE:PIECE, :], at, sem)
    copy.start()
    odd = place[0] & 1
    blank = jnp.zeros((64, LANES), jnp.float32)
    for side in range(2):
        cols = slice(side * LANES, (side + 1) * LANES)
        light[1 + side, 64:320, :] = probe[0, :, cols] * probe[0, :, cols] + (
            probe[1, :, cols] * probe[1, :, cols]
        )
        light[1 + side, 0:64, :] = blank
        light[1 + side, 320:384, :] = blank
        light[3 * side, :, :] = jnp.zeros((384, LANES), jnp.float32)
    copy.wait()
    mine = 8 - 8 * odd
    total = jnp.zeros((40, LANES), jnp.float32)
    outside = jnp.zeros((40, LANES), jnp.float32)
    for member in range(8):
        for core in range(2):
            block = 1 - core * (1 - odd) + (1 - core) * odd
            total = shine(light, place[1], total, [at[mine + member, core, k] for k in range(3)], block)
        outside = shine(
            light, place[1], outside, [at[8 - mine + member, 1 - odd, k] for k in range(3)], 2 - 2 * odd
        )
    total = total + jnp.where(far_exists(place[0]), outside, 0.0)
    bottom = total + 0.25 * (peak[0:1, :] + 1e-06)
    for part in range(2):
        out[part] = old[part] - gradient[part * 40 : part * 40 + 40, :] / bottom


def half_of(tile):
    return (tile ^ (tile >> 1)) & 1


def far_exists(tile):
    return jnp.logical_and(tile > 0, tile < TILES - 1)


def swap_cores(value):
    return lax.ppermute(value, "tile", [(i, i ^ 1) for i in range(TILES)])


def swap_z(value, mask):
    pairs = []
    for tile in range(TILES):
        layer, rest = divmod(tile, 4)
        ahead = 1 if rest == 0 else 0
        other = (((layer - ahead) % (TILES // 4)) ^ mask) + ahead
        pairs.append((tile, other % (TILES // 4) * 4 + rest))
    return lax.ppermute(value, "tile", pairs)


def exchange(value):
    groups = []
    for first in range(1, TILES, 2):
        second = (first + 1) % TILES
        groups.append([first * 8 + i for i in range(8)] + [second * 8 + i for i in range(8)])
    return lax.all_to_all(value, ("tile", "group"), 0, 0, axis_index_groups=groups)


def on_chip(value):
    return pltpu.with_memory_space_constraint(value, pltpu.VMEM)


def kernel_call(body, out_shape, in_specs, out_specs, megabytes, **kwargs):
    return pl.pallas_call(
        body,
        out_shape=out_shape,
        in_specs=in_specs,
        out_specs=out_specs,
        compiler_params=pltpu.CompilerParams(vmem_limit_bytes=megabytes << 20),
        name=body.__name__.removesuffix("_kernel"),
        **kwargs,
    )


def local(object_field, probe_field, amplitudes, row_start, column_start, live_slots):
    smem, vmem = pl.BlockSpec(memory_space=SMEM), pl.BlockSpec(memory_space=VMEM)
    place = jnp.stack([lax.axis_index("tile"), lax.axis_index("group")]).astype(jnp.int32)
    high, low = (on_chip(jnp.asarray(table)) for table in split_tables())
    probe = on_chip(probe_field)

    def buffer(*dims):
        return pltpu.VMEM(dims, jnp.float32)

    own = object_field.reshape(80, LANES)
    stack = exchange(jnp.broadcast_to(own, (16, 80, LANES)))
    keep, send, peak = kernel_call(
        window_kernel,
        (buffer(16, LINES, LANES), buffer(16 * PIECE + 640, LANES), buffer(8, LANES)),
        [smem] * 4 + [vmem] * 6,
        (vmem,) * 3,
        24,
        scratch_shapes=[buffer(2, 3, 320, LANES), buffer(2, 3, 320, LANES), buffer(3, WIN, WIN)],
    )(
        place, row_start, column_start, live_slots, on_chip(stack), on_chip(swap_cores(stack)),
        probe, on_chip(amplitudes), high, low,
    )

    merged = kernel_call(merge_kernel, buffer(16, LINES, LANES), [smem] + [vmem] * 2, vmem, 4)(
        place, keep, on_chip(swap_cores(send))
    )
    pieces = on_chip(exchange(merged))
    total, gradient = kernel_call(
        reduce_kernel, (buffer(PIECE, LANES), buffer(80, LANES)), [vmem], (vmem,) * 2, 4
    )(pieces)
    new_object = kernel_call(
        object_kernel,
        jax.ShapeDtypeStruct((2, 40, LANES), jnp.float32),
        [smem] + [vmem] * 5,
        vmem,
        8,
        scratch_shapes=[
            buffer(4, 384, LANES),
            pltpu.SMEM((16, 8, LANES), jnp.float32),
            pltpu.SemaphoreType.DMA,
        ],
        cost_estimate=pl.CostEstimate(flops=700000, bytes_accessed=2000000, transcendentals=0),
    )(place, pieces, gradient, on_chip(object_field), probe, peak)
    for mask in (1, 2):
        total = total + swap_z(total, mask)
    total, new_object = lax.optimization_barrier((total, new_object))
    piece = kernel_call(probe_kernel, buffer(16, 32, LANES), [smem] + [vmem] * 3, vmem, 4)(
        place, on_chip(total), on_chip(swap_z(total, 6)), probe
    )

    mine = exchange(piece)
    new_probe = kernel_call(
        gather_kernel,
        jax.ShapeDtypeStruct((2, WIN, WIN), jnp.float32),
        [smem] + [vmem] * 2,
        vmem,
        4,
    )(place, on_chip(mine), on_chip(swap_cores(mine)))
    return new_object, new_probe


def solution(mesh):
    return jax.shard_map(
        local,
        mesh=mesh,
        in_specs=(
            P(None, "group", "tile"),
            P(),
            P(("tile", "group"), None, None),
            P(("tile", "group")),
            P(("tile", "group")),
            P(("tile", "group")),
        ),
        out_specs=(P(None, "group", "tile"), P()),
        check_vma=False,
    )
```

```python
import jax
import jax.numpy as jnp
import ml_dtypes
import numpy as np
from jax import lax
from jax.experimental import pallas as pl
from jax.experimental.pallas import tpu as pltpu
from jax.sharding import PartitionSpec as P

WIN = 256
LANES = 128
TILES = 32
SPARE = 48
PIECE = 56
SMEM = pltpu.MemorySpace.SMEM
VMEM = pltpu.MemorySpace.VMEM


def split_tables():
    counter = np.arange(WIN)
    angles = 2.0 * np.pi / WIN * (counter[:, None] * counter[None, :] % WIN)
    cos, sin = np.cos(angles) / np.sqrt(WIN), np.sin(angles) / np.sqrt(WIN)
    both = np.concatenate([cos, sin], axis=0)
    high = both.astype(ml_dtypes.bfloat16)
    low = (both - high.astype(np.float64)).astype(ml_dtypes.bfloat16)
    return high, low


def halves(value):
    high = value.astype(jnp.bfloat16)
    low = (value - high.astype(jnp.float32)).astype(jnp.bfloat16)
    return high, low


def product(left, right):
    def dot(a, b):
        return jnp.dot(a, b, preferred_element_type=jnp.float32)

    return dot(left[0], right[0]) + dot(left[0], right[1]) + dot(left[1], right[0])


def transform(real, imag, tall, wide, sign):
    cols = product(tall, halves(jnp.concatenate([real, imag], axis=1)))
    left_real = cols[:WIN, :WIN] - sign * cols[WIN:, WIN:]
    left_imag = cols[:WIN, WIN:] + sign * cols[WIN:, :WIN]
    rows = product(halves(jnp.concatenate([left_real, left_imag], axis=0)), wide)
    right_real = rows[:WIN, :WIN] - sign * rows[WIN:, WIN:]
    right_imag = rows[WIN:, :WIN] + sign * rows[:WIN, WIN:]
    return right_real, right_imag


def window_kernel(
    place, stack, near, probe, amps, high, low, keep, keep_grad, send, field, grads, sums
):
    row, col = place[2], place[3]
    live = place[4].astype(jnp.float32)
    odd, half = place[0] & 1, half_of(place[0])
    inside = far_exists(place[0])
    for member in range(8):
        lines = slice(member * 40, member * 40 + 40)
        for part in range(2):
            rows = slice(part * 40, part * 40 + 40)
            field[part, 1, lines, :] = stack[8 - 8 * odd + member, rows, :]
            field[part, 2 * odd, lines, :] = jnp.where(inside, stack[8 * odd + member, rows, :], 0.0)
            field[part, 2 - 2 * odd, lines, :] = near[8 * odd + member, rows, :]
    lane = lax.broadcasted_iota(jnp.int32, (WIN, LANES), 1)
    back = lax.rem(LANES - col, LANES)
    ahead = lax.rem(col, LANES)
    first = lane < LANES - col

    def cut(part):
        turned = [
            pltpu.roll(field[part, block, pl.ds(row, WIN), :], back, 1) for block in range(3)
        ]
        return jnp.concatenate(
            [jnp.where(first, turned[0], turned[1]), jnp.where(first, turned[1], turned[2])], axis=1
        )

    sample_real, sample_imag = cut(0), cut(1)
    probe_real, probe_imag = probe[0], probe[1]
    exit_real = probe_real * sample_real - probe_imag * sample_imag
    exit_imag = probe_real * sample_imag + probe_imag * sample_real
    tall = (high[...], low[...])
    wide = tuple(jnp.concatenate([table[:WIN], table[WIN:]], axis=1) for table in tall)
    far_real, far_imag = transform(exit_real, exit_imag, tall, wide, -1.0)
    power = far_real * far_real + far_imag * far_imag
    factor = 1.0 - amps[0] * lax.rsqrt(jnp.maximum(power, 0.0625))
    miss_real, miss_imag = transform(far_real * factor, far_imag * factor, tall, wide, 1.0)
    miss_real = miss_real * live
    miss_imag = miss_imag * live
    terms = (
        probe_real * miss_real + probe_imag * miss_imag,
        probe_real * miss_imag - probe_imag * miss_real,
    )
    wrapped = lane < col
    zero = jnp.zeros((WIN, LANES), jnp.float32)
    grads[...] = jnp.zeros_like(grads)
    for part in range(2):
        start = pltpu.roll(terms[part][:, :LANES], ahead, 1)
        end = pltpu.roll(terms[part][:, LANES:], ahead, 1)
        grads[part, 0, pl.ds(row, WIN), :] = jnp.where(wrapped, zero, start)
        grads[part, 1, pl.ds(row, WIN), :] = jnp.where(wrapped, start, end)
        grads[part, 2, pl.ds(row, WIN), :] = jnp.where(wrapped, end, zero)
    window_light = live * (sample_real * sample_real + sample_imag * sample_imag)
    sums[0] = sample_real * miss_real + sample_imag * miss_imag
    sums[1] = sample_real * miss_imag - sample_imag * miss_real
    sums[2] = window_light
    total = jnp.zeros((8, LANES), jnp.float32)
    for line in range(0, WIN, 8):
        total = total + window_light[line : line + 8, :LANES] + window_light[line : line + 8, LANES:]
    spare_line = lax.broadcasted_iota(jnp.int32, (8, LANES), 0)
    spare_lane = lax.broadcasted_iota(jnp.int32, (8, LANES), 1)
    first_lane = 8 * odd
    spare = jnp.where(
        spare_line == 1,
        jnp.broadcast_to(jnp.sum(total, axis=0, keepdims=True), (8, LANES)),
        0.0,
    )
    for lane_off, number in enumerate((row.astype(jnp.float32), col.astype(jnp.float32), live)):
        here = jnp.logical_and(spare_line == 0, spare_lane == first_lane + lane_off)
        spare = jnp.where(here, number, spare)
    for member in range(16):
        for kept, side_half in ((True, half), (False, 1 - half)):
            top = pl.multiple_of(side_half * 128 + member * 8, 8)
            for part in range(3):
                for side in range(2):
                    put = part * 16 + side * 8
                    value = sums[part, pl.ds(top, 8), side * LANES : (side + 1) * LANES]
                    if kept:
                        keep[member, put : put + 8, :] = value
                    else:
                        send[member * PIECE + put : member * PIECE + put + 8, :] = value
            if kept:
                keep[member, SPARE:PIECE, :] = spare
            else:
                send[member * PIECE + SPARE : member * PIECE + PIECE, :] = spare
    for member in range(8):
        lines = slice(member * 40, member * 40 + 40)
        for part in range(2):
            put = part * 40
            keep_grad[8 - 8 * odd + member, put : put + 40, :] = grads[part, 1, lines, :]
            keep_grad[8 * odd + member, put : put + 40, :] = jnp.where(
                inside, grads[part, 2 * odd, lines, :], 0.0
            )
            put = 16 * PIECE + member * 80 + part * 40
            send[put : put + 40, :] = grads[part, 2 - 2 * odd, lines, :]


def merge_kernel(place, keep, keep_grad, got, out, out_grad):
    for member in range(16):
        out[member] = keep[member] + got[member * PIECE : (member + 1) * PIECE, :]
    mine = 8 - 8 * (place[0] & 1)
    for member in range(8):
        put = 16 * PIECE + member * 80
        out_grad[mine + member] = keep_grad[mine + member] + got[put : put + 80, :]
        out_grad[8 - mine + member] = keep_grad[8 - mine + member]


def reduce_kernel(pieces, out):
    total = pieces[0]
    for member in range(1, 16):
        total = total + pieces[member]
    out[...] = total


def probe_kernel(place, one, two, probe, out):
    odd = place[0] & 1
    top = pl.multiple_of(half_of(place[0]) * 128 + (8 - 8 * odd + place[1]) * 8, 8)
    summed = one[...] + two[...]
    mean = jnp.sum(summed[SPARE + 1 : SPARE + 2]) * (1.0 / (WIN * WIN))
    for side in range(2):
        bottom = summed[32 + side * 8 : 40 + side * 8] + 0.25 * mean + 1e-05
        for part in range(2):
            lines = part * 16 + side * 8
            old = probe[part, pl.ds(top, 8), side * LANES : (side + 1) * LANES]
            new = old - summed[lines : lines + 8] / bottom
            for member in range(16):
                out[member, lines : lines + 8, :] = new


def gather_kernel(place, mine, other, out):
    half = half_of(place[0])
    for source, which in ((mine, half), (other, 1 - half)):
        for member in range(16):
            top = pl.multiple_of(which * 128 + member * 8, 8)
            for part in range(2):
                for side in range(2):
                    lines = part * 16 + side * 8
                    out[part, pl.ds(top, 8), side * LANES : (side + 1) * LANES] = source[
                        member, lines : lines + 8, :
                    ]


def shine(light, group, total, at, block):
    row, col = at[0].astype(jnp.int32), at[1].astype(jnp.int32)
    top = 64 + group * 40 - row
    turn = lax.rem(col, LANES)
    lane = lax.broadcasted_iota(jnp.int32, (40, LANES), 1)
    before = pltpu.roll(light[block, pl.ds(top, 40), :], turn, 1)
    after = pltpu.roll(light[block + 1, pl.ds(top, 40), :], turn, 1)
    return total + at[2] * jnp.where(lane < col, before, after)


def prep_kernel(probe, light, peak):
    blank = jnp.zeros((64, LANES), jnp.float32)
    most = jnp.zeros((WIN, LANES), jnp.float32)
    for side in range(2):
        cols = slice(side * LANES, (side + 1) * LANES)
        bright = probe[0, :, cols] * probe[0, :, cols] + probe[1, :, cols] * probe[1, :, cols]
        most = jnp.maximum(most, bright)
        light[1 + side, 64:320, :] = bright
        light[1 + side, 0:64, :] = blank
        light[1 + side, 320:384, :] = blank
        light[3 * side, :, :] = jnp.zeros((384, LANES), jnp.float32)
    peak[...] = jnp.full((8, LANES), jnp.max(most), jnp.float32)


def object_kernel(place, pieces, grads, old, light, peak, out, at, sem):
    copy = pltpu.make_async_copy(pieces.at[:, SPARE : SPARE + 1, :], at, sem)
    copy.start()
    gradient = grads[0]
    for member in range(1, 16):
        gradient = gradient + grads[member]
    copy.wait()
    odd = place[0] & 1
    mine = 8 - 8 * odd
    total = jnp.zeros((40, LANES), jnp.float32)
    outside = jnp.zeros((40, LANES), jnp.float32)
    for member in range(8):
        for core in range(2):
            block = 1 - core * (1 - odd) + (1 - core) * odd
            seen = [at[mine + member, 0, core * 8 + k] for k in range(3)]
            total = shine(light, place[1], total, seen, block)
        seen = [at[8 - mine + member, 0, (1 - odd) * 8 + k] for k in range(3)]
        outside = shine(light, place[1], outside, seen, 2 - 2 * odd)
    total = total + jnp.where(far_exists(place[0]), outside, 0.0)
    bottom = total + 0.25 * (peak[0:1, :] + 1e-06)
    for part in range(2):
        out[part] = old[part] - gradient[part * 40 : part * 40 + 40, :] / bottom


def half_of(tile):
    return (tile ^ (tile >> 1)) & 1


def far_exists(tile):
    return jnp.logical_and(tile > 0, tile < TILES - 1)


def swap_cores(value):
    return lax.ppermute(value, "tile", [(i, i ^ 1) for i in range(TILES)])


def swap_z(value, mask):
    pairs = []
    for tile in range(TILES):
        layer, rest = divmod(tile, 4)
        ahead = 1 if rest == 0 else 0
        other = (((layer - ahead) % (TILES // 4)) ^ mask) + ahead
        pairs.append((tile, other % (TILES // 4) * 4 + rest))
    return lax.ppermute(value, "tile", pairs)


def exchange(value):
    groups = []
    for first in range(1, TILES, 2):
        second = (first + 1) % TILES
        groups.append([first * 8 + i for i in range(8)] + [second * 8 + i for i in range(8)])
    return lax.all_to_all(value, ("tile", "group"), 0, 0, axis_index_groups=groups)


def on_chip(value):
    return pltpu.with_memory_space_constraint(value, pltpu.VMEM)


def kernel_call(body, out_shape, in_specs, out_specs, megabytes, **kwargs):
    return pl.pallas_call(
        body,
        out_shape=out_shape,
        in_specs=in_specs,
        out_specs=out_specs,
        compiler_params=pltpu.CompilerParams(vmem_limit_bytes=megabytes << 20),
        name=body.__name__.removesuffix("_kernel"),
        **kwargs,
    )


def local(object_field, probe_field, amplitudes, row_start, column_start, live_slots):
    smem, vmem = pl.BlockSpec(memory_space=SMEM), pl.BlockSpec(memory_space=VMEM)
    high, low = (on_chip(jnp.asarray(table)) for table in split_tables())
    probe = on_chip(probe_field)

    def buffer(*dims):
        return pltpu.VMEM(dims, jnp.float32)

    own = object_field.reshape(80, LANES)
    here = [lax.axis_index(axis)[None].astype(jnp.int32) for axis in ("tile", "group")]
    place = jnp.concatenate([*here, row_start, column_start, live_slots])
    stack, place = lax.optimization_barrier((exchange(jnp.broadcast_to(own, (16, 80, LANES))), place))
    light, peak = kernel_call(
        prep_kernel,
        (buffer(4, 384, LANES), buffer(8, LANES)),
        [vmem],
        (vmem,) * 2,
        4,
        cost_estimate=pl.CostEstimate(flops=300000, bytes_accessed=2000000, transcendentals=0),
    )(probe)
    keep, keep_grad, send = kernel_call(
        window_kernel,
        (buffer(16, PIECE, LANES), buffer(16, 80, LANES), buffer(16 * PIECE + 640, LANES)),
        [smem] + [vmem] * 6,
        (vmem,) * 3,
        24,
        scratch_shapes=[buffer(2, 3, 320, LANES), buffer(2, 3, 320, LANES), buffer(3, WIN, WIN)],
    )(
        place, on_chip(stack), on_chip(swap_cores(stack)), probe, on_chip(amplitudes), high, low
    )

    got, light = lax.optimization_barrier((swap_cores(send), light))
    sums, grads = kernel_call(
        merge_kernel,
        (buffer(16, PIECE, LANES), buffer(16, 80, LANES)),
        [smem] + [vmem] * 3,
        (vmem,) * 2,
        4,
    )(place, keep, keep_grad, on_chip(got))
    pieces = exchange(sums)
    total = kernel_call(reduce_kernel, buffer(PIECE, LANES), [vmem], vmem, 4)(on_chip(pieces))
    total, grads = lax.optimization_barrier((total, grads))
    grads = exchange(grads)
    for mask in (1, 2):
        total = total + swap_z(total, mask)
    total, grads = lax.optimization_barrier((total, grads))
    new_object = kernel_call(
        object_kernel,
        jax.ShapeDtypeStruct((2, 40, LANES), jnp.float32),
        [smem] + [vmem] * 5,
        vmem,
        8,
        scratch_shapes=[pltpu.SMEM((16, 1, LANES), jnp.float32), pltpu.SemaphoreType.DMA],
        cost_estimate=pl.CostEstimate(flops=700000, bytes_accessed=2000000, transcendentals=0),
    )(place, on_chip(pieces), on_chip(grads), on_chip(object_field), on_chip(light), peak)
    got, new_object = lax.optimization_barrier((swap_z(total, 6), new_object))
    piece = kernel_call(probe_kernel, buffer(16, 32, LANES), [smem] + [vmem] * 3, vmem, 4)(
        place, on_chip(total), on_chip(got), probe
    )

    mine = exchange(piece)
    new_probe = kernel_call(
        gather_kernel,
        jax.ShapeDtypeStruct((2, WIN, WIN), jnp.float32),
        [smem] + [vmem] * 2,
        vmem,
        4,
    )(place, on_chip(mine), on_chip(swap_cores(mine)))
    return new_object, new_probe


def solution(mesh):
    return jax.shard_map(
        local,
        mesh=mesh,
        in_specs=(
            P(None, "group", "tile"),
            P(),
            P(("tile", "group"), None, None),
            P(("tile", "group")),
            P(("tile", "group")),
            P(("tile", "group")),
        ),
        out_specs=(P(None, "group", "tile"), P()),
        check_vma=False,
    )
```

```python
import jax
import jax.numpy as jnp
import ml_dtypes
import numpy as np
from jax import lax
from jax.experimental import pallas as pl
from jax.experimental.pallas import tpu as pltpu
from jax.sharding import PartitionSpec as P

WIN = 256
LANES = 128
TILES = 32
SPARE = 48
PIECE = 56
LINES = 136
SMEM = pltpu.MemorySpace.SMEM
VMEM = pltpu.MemorySpace.VMEM


def split_tables():
    counter = np.arange(WIN)
    angles = 2.0 * np.pi / WIN * (counter[:, None] * counter[None, :] % WIN)
    cos, sin = np.cos(angles) / np.sqrt(WIN), np.sin(angles) / np.sqrt(WIN)
    both = np.concatenate([cos[:LANES], cos[LANES : LANES + 1], sin[1:LANES]], axis=0)
    order = np.concatenate([counter[: LANES + 1], counter[:LANES:-1]])
    high = both.astype(ml_dtypes.bfloat16)
    low = (both - high.astype(np.float64)).astype(ml_dtypes.bfloat16)
    select = (order[:, None] == counter[None, :]).astype(ml_dtypes.bfloat16)
    rows = np.concatenate([high, low, select], axis=0)
    return rows, np.concatenate([high.T, low.T, select.T], axis=0)


def halves(value):
    high = value.astype(jnp.bfloat16)
    low = (value - high.astype(jnp.float32)).astype(jnp.bfloat16)
    return high, low


def dot(left, right):
    return jnp.dot(left, right, preferred_element_type=jnp.float32)


def product(left, right):
    return dot(left[0], right[0]) + dot(left[0], right[1]) + dot(left[1], right[0])


def unfold(cos_real, cos_imag, sin_real, sin_imag, axis):
    zeroth = lax.broadcasted_iota(jnp.int32, cos_real.shape, axis) == 0
    odd_real, odd_imag = jnp.where(zeroth, 0.0, sin_imag), jnp.where(zeroth, 0.0, sin_real)
    low = cos_real + odd_real, cos_imag - odd_imag
    high = (
        jnp.where(zeroth, sin_real, cos_real - odd_real),
        jnp.where(zeroth, sin_imag, cos_imag + odd_imag),
    )
    return tuple(jnp.concatenate(pair, axis=axis) for pair in zip(low, high))


def fold(real, imag, axis):
    if axis == 0:
        (low_r, high_r), (low_i, high_i) = ((v[:LANES], v[LANES:]) for v in (real, imag))
    else:
        (low_r, high_r), (low_i, high_i) = ((v[:, :LANES], v[:, LANES:]) for v in (real, imag))
    zeroth = lax.broadcasted_iota(jnp.int32, low_r.shape, axis) == 0
    even = (low_r + jnp.where(zeroth, 0.0, high_r), low_i + jnp.where(zeroth, 0.0, high_i))
    odd = (jnp.where(zeroth, high_r, high_i - low_i), jnp.where(zeroth, high_i, low_r - high_r))
    return tuple(jnp.concatenate(pair, axis=axis) for pair in zip(even, odd))


def parts(table):
    return table[0:WIN], table[WIN : 2 * WIN]


def forward(real, imag, rows, cols):
    along = product(parts(rows), halves(jnp.concatenate([real, imag], axis=1)))
    real, imag = unfold(
        along[:LANES, :WIN], along[:LANES, WIN:], along[LANES:, :WIN], along[LANES:, WIN:], 0
    )
    across = product(halves(jnp.concatenate([real, imag], axis=0)), parts(cols))
    return unfold(
        across[:WIN, :LANES], across[WIN:, :LANES], across[:WIN, LANES:], across[WIN:, LANES:], 1
    )


def inverse(real, imag, rows, cols):
    real, imag = fold(real, imag, 0)
    along = product(parts(cols), halves(jnp.concatenate([real, imag], axis=1)))
    real, imag = fold(along[:, :WIN], along[:, WIN:], 1)
    across = product(halves(jnp.concatenate([real, imag], axis=0)), parts(rows))
    return across[:WIN], across[WIN:]


def reordered(value, rows, cols):
    taken = dot(rows[2 * WIN :], jnp.concatenate(halves(value), axis=1)).astype(jnp.bfloat16)
    taken = dot(jnp.concatenate([taken[:, :WIN], taken[:, WIN:]], axis=0), cols[2 * WIN :])
    return taken[:WIN] + taken[WIN:]


def window_kernel(
    place, stack, near, probe, amps, row_table, col_table, keep, send, field, grads, sums
):
    row, col = place[2], place[3]
    live = place[4].astype(jnp.float32)
    odd, half = place[0] & 1, half_of(place[0])
    inside = far_exists(place[0])
    for member in range(8):
        lines = slice(member * 40, member * 40 + 40)
        for part in range(2):
            held = slice(part * 40, part * 40 + 40)
            field[part, 1, lines, :] = stack[8 - 8 * odd + member, held, :]
            field[part, 2 * odd, lines, :] = jnp.where(inside, stack[8 * odd + member, held, :], 0.0)
            field[part, 2 - 2 * odd, lines, :] = near[8 * odd + member, held, :]
    lane = lax.broadcasted_iota(jnp.int32, (WIN, LANES), 1)
    back = lax.rem(LANES - col, LANES)
    ahead = lax.rem(col, LANES)
    first = lane < LANES - col

    def cut(part):
        turned = [
            pltpu.roll(field[part, block, pl.ds(row, WIN), :], back, 1) for block in range(3)
        ]
        return jnp.concatenate(
            [jnp.where(first, turned[0], turned[1]), jnp.where(first, turned[1], turned[2])], axis=1
        )

    sample_real, sample_imag = cut(0), cut(1)
    probe_real, probe_imag = probe[0], probe[1]
    exit_real = probe_real * sample_real - probe_imag * sample_imag
    exit_imag = probe_real * sample_imag + probe_imag * sample_real
    rows, cols = row_table[...], col_table[...]
    far_real, far_imag = forward(exit_real, exit_imag, rows, cols)
    power = far_real * far_real + far_imag * far_imag
    factor = 1.0 - reordered(amps[0], rows, cols) * lax.rsqrt(jnp.maximum(power, 0.0625))
    miss_real, miss_imag = inverse(far_real * factor, far_imag * factor, rows, cols)
    miss_real = miss_real * live
    miss_imag = miss_imag * live
    terms = (
        probe_real * miss_real + probe_imag * miss_imag,
        probe_real * miss_imag - probe_imag * miss_real,
    )
    wrapped = lane < col
    zero = jnp.zeros((WIN, LANES), jnp.float32)
    grads[...] = jnp.zeros_like(grads)
    for part in range(2):
        start = pltpu.roll(terms[part][:, :LANES], ahead, 1)
        end = pltpu.roll(terms[part][:, LANES:], ahead, 1)
        grads[part, 0, pl.ds(row, WIN), :] = jnp.where(wrapped, zero, start)
        grads[part, 1, pl.ds(row, WIN), :] = jnp.where(wrapped, start, end)
        grads[part, 2, pl.ds(row, WIN), :] = jnp.where(wrapped, end, zero)
    window_light = live * (sample_real * sample_real + sample_imag * sample_imag)
    sums[0] = sample_real * miss_real + sample_imag * miss_imag
    sums[1] = sample_real * miss_imag - sample_imag * miss_real
    sums[2] = window_light
    total = jnp.zeros((8, LANES), jnp.float32)
    for line in range(0, WIN, 8):
        total = total + window_light[line : line + 8, :LANES] + window_light[line : line + 8, LANES:]
    spare_line = lax.broadcasted_iota(jnp.int32, (8, LANES), 0)
    spare_lane = lax.broadcasted_iota(jnp.int32, (8, LANES), 1)
    first_lane = 8 * odd
    spare = jnp.where(
        spare_line == 1,
        jnp.broadcast_to(jnp.sum(total, axis=0, keepdims=True), (8, LANES)),
        0.0,
    )
    for lane_off, number in enumerate((row.astype(jnp.float32), col.astype(jnp.float32), live)):
        here = jnp.logical_and(spare_line == 0, spare_lane == first_lane + lane_off)
        spare = jnp.where(here, number, spare)
    for member in range(16):
        for kept, side_half in ((True, half), (False, 1 - half)):
            top = pl.multiple_of(side_half * 128 + member * 8, 8)
            for part in range(3):
                for side in range(2):
                    put = part * 16 + side * 8
                    value = sums[part, pl.ds(top, 8), side * LANES : (side + 1) * LANES]
                    if kept:
                        keep[member, put : put + 8, :] = value
                    else:
                        send[member * PIECE + put : member * PIECE + put + 8, :] = value
            if kept:
                keep[member, SPARE:PIECE, :] = spare
            else:
                send[member * PIECE + SPARE : member * PIECE + PIECE, :] = spare
    for member in range(8):
        lines = slice(member * 40, member * 40 + 40)
        for part in range(2):
            put = PIECE + part * 40
            keep[8 - 8 * odd + member, put : put + 40, :] = grads[part, 1, lines, :]
            keep[8 * odd + member, put : put + 40, :] = jnp.where(
                inside, grads[part, 2 * odd, lines, :], 0.0
            )
            put = 16 * PIECE + member * 80 + part * 40
            send[put : put + 40, :] = grads[part, 2 - 2 * odd, lines, :]


def merge_kernel(place, keep, got, out):
    for member in range(16):
        out[member, :PIECE, :] = keep[member, :PIECE, :] + got[member * PIECE : (member + 1) * PIECE, :]
    mine = 8 - 8 * (place[0] & 1)
    for member in range(8):
        put = 16 * PIECE + member * 80
        out[mine + member, PIECE:, :] = keep[mine + member, PIECE:, :] + got[put : put + 80, :]
        out[8 - mine + member, PIECE:, :] = keep[8 - mine + member, PIECE:, :]


def reduce_kernel(pieces, out):
    total = pieces[0, :PIECE, :]
    for member in range(1, 16):
        total = total + pieces[member, :PIECE, :]
    out[...] = total


def probe_kernel(place, one, two, probe, out):
    odd = place[0] & 1
    top = pl.multiple_of(half_of(place[0]) * 128 + (8 - 8 * odd + place[1]) * 8, 8)
    summed = one[...] + two[...]
    mean = jnp.sum(summed[SPARE + 1 : SPARE + 2]) * (1.0 / (WIN * WIN))
    for side in range(2):
        bottom = summed[32 + side * 8 : 40 + side * 8] + 0.25 * mean + 1e-05
        for part in range(2):
            lines = part * 16 + side * 8
            old = probe[part, pl.ds(top, 8), side * LANES : (side + 1) * LANES]
            new = old - summed[lines : lines + 8] / bottom
            for member in range(16):
                out[member, lines : lines + 8, :] = new


def gather_kernel(place, which, source, *refs):
    out, block, sem = refs[-3:]
    half = half_of(place[0]) ^ which
    for member in range(16):
        for part in range(2):
            for side in range(2):
                lines = part * 16 + side * 8
                block[part, member * 8 : member * 8 + 8, side * LANES : (side + 1) * LANES] = source[
                    member, lines : lines + 8, :
                ]
    rows = pl.ds(pl.multiple_of(half * 128, 128), 128)
    copy = pltpu.make_async_copy(block, out.at[:, rows, :], sem)
    copy.start()
    copy.wait()


def shine(light, group, total, at, block):
    row, col = at[0].astype(jnp.int32), at[1].astype(jnp.int32)
    top = 64 + group * 40 - row
    turn = lax.rem(col, LANES)
    lane = lax.broadcasted_iota(jnp.int32, (40, LANES), 1)
    before = pltpu.roll(light[block, pl.ds(top, 40), :], turn, 1)
    after = pltpu.roll(light[block + 1, pl.ds(top, 40), :], turn, 1)
    return total + at[2] * jnp.where(lane < col, before, after)


def prep_kernel(probe, light, peak):
    blank = jnp.zeros((64, LANES), jnp.float32)
    most = jnp.zeros((WIN, LANES), jnp.float32)
    for side in range(2):
        cols = slice(side * LANES, (side + 1) * LANES)
        bright = probe[0, :, cols] * probe[0, :, cols] + probe[1, :, cols] * probe[1, :, cols]
        most = jnp.maximum(most, bright)
        light[1 + side, 64:320, :] = bright
        light[1 + side, 0:64, :] = blank
        light[1 + side, 320:384, :] = blank
        light[3 * side, :, :] = jnp.zeros((384, LANES), jnp.float32)
    peak[...] = jnp.full((8, LANES), jnp.max(most), jnp.float32)


def object_kernel(place, pieces, old, light, peak, out, at, sem):
    copy = pltpu.make_async_copy(pieces.at[:, SPARE : SPARE + 1, :], at, sem)
    copy.start()
    gradient = pieces[0, PIECE:, :]
    for member in range(1, 16):
        gradient = gradient + pieces[member, PIECE:, :]
    copy.wait()
    odd = place[0] & 1
    mine = 8 - 8 * odd
    total = jnp.zeros((40, LANES), jnp.float32)
    outside = jnp.zeros((40, LANES), jnp.float32)
    for member in range(8):
        for core in range(2):
            block = 1 - core * (1 - odd) + (1 - core) * odd
            seen = [at[mine + member, 0, core * 8 + k] for k in range(3)]
            total = shine(light, place[1], total, seen, block)
        seen = [at[8 - mine + member, 0, (1 - odd) * 8 + k] for k in range(3)]
        outside = shine(light, place[1], outside, seen, 2 - 2 * odd)
    total = total + jnp.where(far_exists(place[0]), outside, 0.0)
    bottom = total + 0.25 * (peak[0:1, :] + 1e-06)
    for part in range(2):
        out[part] = old[part] - gradient[part * 40 : part * 40 + 40, :] / bottom


def half_of(tile):
    return (tile ^ (tile >> 1)) & 1


def far_exists(tile):
    return jnp.logical_and(tile > 0, tile < TILES - 1)


def swap_cores(value):
    return lax.ppermute(value, "tile", [(i, i ^ 1) for i in range(TILES)])


def swap_z(value, mask):
    pairs = []
    for tile in range(TILES):
        layer, rest = divmod(tile, 4)
        ahead = 1 if rest == 0 else 0
        other = (((layer - ahead) % (TILES // 4)) ^ mask) + ahead
        pairs.append((tile, other % (TILES // 4) * 4 + rest))
    return lax.ppermute(value, "tile", pairs)


def exchange(value):
    groups = []
    for first in range(1, TILES, 2):
        second = (first + 1) % TILES
        groups.append([first * 8 + i for i in range(8)] + [second * 8 + i for i in range(8)])
    return lax.all_to_all(value, ("tile", "group"), 0, 0, axis_index_groups=groups)


def on_chip(value):
    return pltpu.with_memory_space_constraint(value, pltpu.VMEM)


def kernel_call(body, out_shape, in_specs, out_specs, megabytes, **kwargs):
    return pl.pallas_call(
        body,
        out_shape=out_shape,
        in_specs=in_specs,
        out_specs=out_specs,
        compiler_params=pltpu.CompilerParams(vmem_limit_bytes=megabytes << 20),
        name=body.__name__.removesuffix("_kernel"),
        **kwargs,
    )


def local(object_field, probe_field, amplitudes, row_start, column_start, live_slots):
    smem, vmem = pl.BlockSpec(memory_space=SMEM), pl.BlockSpec(memory_space=VMEM)
    row_table, col_table = (on_chip(jnp.asarray(table)) for table in split_tables())
    probe = on_chip(probe_field)

    def buffer(*dims):
        return pltpu.VMEM(dims, jnp.float32)

    own = object_field.reshape(80, LANES)
    here = [lax.axis_index(axis)[None].astype(jnp.int32) for axis in ("tile", "group")]
    place = jnp.concatenate([*here, row_start, column_start, live_slots])
    stack = exchange(jnp.broadcast_to(own, (16, 80, LANES)))
    light, peak = kernel_call(
        prep_kernel,
        (buffer(4, 384, LANES), buffer(8, LANES)),
        [vmem],
        (vmem,) * 2,
        4,
        cost_estimate=pl.CostEstimate(flops=300000, bytes_accessed=2000000, transcendentals=0),
    )(probe)
    keep, send = kernel_call(
        window_kernel,
        (buffer(16, LINES, LANES), buffer(16 * PIECE + 640, LANES)),
        [smem] + [vmem] * 6,
        (vmem,) * 2,
        24,
        scratch_shapes=[buffer(2, 3, 320, LANES), buffer(2, 3, 320, LANES), buffer(3, WIN, WIN)],
    )(
        place, on_chip(stack), on_chip(swap_cores(stack)), probe, on_chip(amplitudes),
        row_table, col_table,
    )

    got, light = lax.optimization_barrier((swap_cores(send), light))
    merged = kernel_call(merge_kernel, buffer(16, LINES, LANES), [smem] + [vmem] * 2, vmem, 4)(
        place, keep, on_chip(got)
    )
    pieces = exchange(merged)
    total = kernel_call(reduce_kernel, buffer(PIECE, LANES), [vmem], vmem, 4)(on_chip(pieces))
    new_object = kernel_call(
        object_kernel,
        jax.ShapeDtypeStruct((2, 40, LANES), jnp.float32),
        [smem] + [vmem] * 4,
        vmem,
        4,
        scratch_shapes=[pltpu.SMEM((16, 1, LANES), jnp.float32), pltpu.SemaphoreType.DMA],
        cost_estimate=pl.CostEstimate(flops=700000, bytes_accessed=2000000, transcendentals=0),
    )(place, on_chip(pieces), on_chip(object_field), on_chip(light), peak)
    for mask in (1, 2):
        total = total + swap_z(total, mask)
    got, new_object = lax.optimization_barrier((swap_z(total, 6), new_object))
    piece = kernel_call(probe_kernel, buffer(16, 32, LANES), [smem] + [vmem] * 3, vmem, 4)(
        place, on_chip(total), on_chip(got), probe
    )

    mine = exchange(piece)
    other = swap_cores(mine)
    hbm = pl.BlockSpec(memory_space=pltpu.MemorySpace.HBM)

    def put(which, source, *before):
        def gather_half_kernel(place, *refs):
            gather_kernel(place, which, *refs)

        return kernel_call(
            gather_half_kernel,
            pltpu.HBM((2, WIN, WIN), jnp.float32),
            [smem, vmem] + [hbm] * len(before),
            hbm,
            4,
            scratch_shapes=[buffer(2, WIN // 2, WIN), pltpu.SemaphoreType.DMA],
            input_output_aliases={2: 0} if before else {},
            cost_estimate=pl.CostEstimate(flops=0, bytes_accessed=1000000, transcendentals=0),
        )(place, on_chip(source), *before)

    first_half = put(0, mine)
    other, first_half = lax.optimization_barrier((other, first_half))
    new_probe = put(1, other, first_half)
    return new_object, new_probe


def solution(mesh):
    return jax.shard_map(
        local,
        mesh=mesh,
        in_specs=(
            P(None, "group", "tile"),
            P(),
            P(("tile", "group"), None, None),
            P(("tile", "group")),
            P(("tile", "group")),
            P(("tile", "group")),
        ),
        out_specs=(P(None, "group", "tile"), P()),
        check_vma=False,
    )
```

```python
import jax
import jax.numpy as jnp
import ml_dtypes
import numpy as np
from jax import lax
from jax.experimental import pallas as pl
from jax.experimental.pallas import tpu as pltpu
from jax.sharding import PartitionSpec as P

WIN = 256
LANES = 128
TILES = 32
SPARE = 48
PIECE = 56
LINES = 136
SMEM = pltpu.MemorySpace.SMEM
VMEM = pltpu.MemorySpace.VMEM


def split_tables():
    counter = np.arange(WIN)
    angles = 2.0 * np.pi / WIN * (counter[:, None] * counter[None, :] % WIN)
    cos, sin = np.cos(angles) / np.sqrt(WIN), np.sin(angles) / np.sqrt(WIN)
    both = np.concatenate([cos[:LANES], cos[LANES : LANES + 1], sin[1:LANES]], axis=0)
    order = np.concatenate([counter[: LANES + 1], counter[:LANES:-1]])
    high = both.astype(ml_dtypes.bfloat16)
    low = (both - high.astype(np.float64)).astype(ml_dtypes.bfloat16)
    select = (order[:, None] == counter[None, :]).astype(ml_dtypes.bfloat16)
    rows = np.concatenate([high, low, select], axis=0)
    return rows, np.concatenate([high.T, low.T, select.T], axis=0)


def halves(value):
    high = value.astype(jnp.bfloat16)
    low = (value - high.astype(jnp.float32)).astype(jnp.bfloat16)
    return high, low


def dot(left, right):
    return jnp.dot(left, right, preferred_element_type=jnp.float32)


def product(left, right):
    return dot(left[0], right[0]) + dot(left[0], right[1]) + dot(left[1], right[0])


def unfold(cos_real, cos_imag, sin_real, sin_imag, axis):
    zeroth = lax.broadcasted_iota(jnp.int32, cos_real.shape, axis) == 0
    odd_real, odd_imag = jnp.where(zeroth, 0.0, sin_imag), jnp.where(zeroth, 0.0, sin_real)
    low = cos_real + odd_real, cos_imag - odd_imag
    high = (
        jnp.where(zeroth, sin_real, cos_real - odd_real),
        jnp.where(zeroth, sin_imag, cos_imag + odd_imag),
    )
    return tuple(jnp.concatenate(pair, axis=axis) for pair in zip(low, high))


def fold(real, imag, axis):
    if axis == 0:
        (low_r, high_r), (low_i, high_i) = ((v[:LANES], v[LANES:]) for v in (real, imag))
    else:
        (low_r, high_r), (low_i, high_i) = ((v[:, :LANES], v[:, LANES:]) for v in (real, imag))
    zeroth = lax.broadcasted_iota(jnp.int32, low_r.shape, axis) == 0
    even = (low_r + jnp.where(zeroth, 0.0, high_r), low_i + jnp.where(zeroth, 0.0, high_i))
    odd = (jnp.where(zeroth, high_r, high_i - low_i), jnp.where(zeroth, high_i, low_r - high_r))
    return tuple(jnp.concatenate(pair, axis=axis) for pair in zip(even, odd))


def parts(table):
    return table[0:WIN], table[WIN : 2 * WIN]


def forward(real, imag, rows, cols):
    along = product(parts(rows), halves(jnp.concatenate([real, imag], axis=1)))
    real, imag = unfold(
        along[:LANES, :WIN], along[:LANES, WIN:], along[LANES:, :WIN], along[LANES:, WIN:], 0
    )
    across = product(halves(jnp.concatenate([real, imag], axis=0)), parts(cols))
    return unfold(
        across[:WIN, :LANES], across[WIN:, :LANES], across[:WIN, LANES:], across[WIN:, LANES:], 1
    )


def inverse(real, imag, rows, cols):
    real, imag = fold(real, imag, 0)
    along = product(parts(cols), halves(jnp.concatenate([real, imag], axis=1)))
    real, imag = fold(along[:, :WIN], along[:, WIN:], 1)
    across = product(halves(jnp.concatenate([real, imag], axis=0)), parts(rows))
    return across[:WIN], across[WIN:]


def reordered(value, rows, cols):
    taken = dot(rows[2 * WIN :], jnp.concatenate(halves(value), axis=1)).astype(jnp.bfloat16)
    taken = dot(jnp.concatenate([taken[:, :WIN], taken[:, WIN:]], axis=0), cols[2 * WIN :])
    return taken[:WIN] + taken[WIN:]


def window_kernel(
    row_ref, col_ref, live_ref, stack, near, probe, amps, row_table, col_table,
    keep, send, field, grads, sums,
):
    row, col = row_ref[0], col_ref[0]
    live = live_ref[0].astype(jnp.float32)
    tile, _ = my_place()
    odd, half = tile & 1, half_of(tile)
    inside = far_exists(tile)
    for member in range(8):
        lines = slice(member * 40, member * 40 + 40)
        for part in range(2):
            held = slice(part * 40, part * 40 + 40)
            field[part, 1, lines, :] = stack[8 - 8 * odd + member, held, :]
            field[part, 2 * odd, lines, :] = jnp.where(inside, stack[8 * odd + member, held, :], 0.0)
            field[part, 2 - 2 * odd, lines, :] = near[8 * odd + member, held, :]
    lane = lax.broadcasted_iota(jnp.int32, (WIN, LANES), 1)
    back = lax.rem(LANES - col, LANES)
    ahead = lax.rem(col, LANES)
    first = lane < LANES - col

    def cut(part):
        turned = [
            pltpu.roll(field[part, block, pl.ds(row, WIN), :], back, 1) for block in range(3)
        ]
        return jnp.concatenate(
            [jnp.where(first, turned[0], turned[1]), jnp.where(first, turned[1], turned[2])], axis=1
        )

    sample_real, sample_imag = cut(0), cut(1)
    probe_real, probe_imag = probe[0], probe[1]
    exit_real = probe_real * sample_real - probe_imag * sample_imag
    exit_imag = probe_real * sample_imag + probe_imag * sample_real
    rows, cols = row_table[...], col_table[...]
    far_real, far_imag = forward(exit_real, exit_imag, rows, cols)
    power = far_real * far_real + far_imag * far_imag
    factor = 1.0 - reordered(amps[0], rows, cols) * lax.rsqrt(jnp.maximum(power, 0.0625))
    miss_real, miss_imag = inverse(far_real * factor, far_imag * factor, rows, cols)
    miss_real = miss_real * live
    miss_imag = miss_imag * live
    terms = (
        probe_real * miss_real + probe_imag * miss_imag,
        probe_real * miss_imag - probe_imag * miss_real,
    )
    wrapped = lane < col
    zero = jnp.zeros((WIN, LANES), jnp.float32)
    grads[...] = jnp.zeros_like(grads)
    for part in range(2):
        start = pltpu.roll(terms[part][:, :LANES], ahead, 1)
        end = pltpu.roll(terms[part][:, LANES:], ahead, 1)
        grads[part, 0, pl.ds(row, WIN), :] = jnp.where(wrapped, zero, start)
        grads[part, 1, pl.ds(row, WIN), :] = jnp.where(wrapped, start, end)
        grads[part, 2, pl.ds(row, WIN), :] = jnp.where(wrapped, end, zero)
    window_light = live * (sample_real * sample_real + sample_imag * sample_imag)
    sums[0] = sample_real * miss_real + sample_imag * miss_imag
    sums[1] = sample_real * miss_imag - sample_imag * miss_real
    sums[2] = window_light
    total = jnp.zeros((8, LANES), jnp.float32)
    for line in range(0, WIN, 8):
        total = total + window_light[line : line + 8, :LANES] + window_light[line : line + 8, LANES:]
    spare_line = lax.broadcasted_iota(jnp.int32, (8, LANES), 0)
    spare_lane = lax.broadcasted_iota(jnp.int32, (8, LANES), 1)
    first_lane = 8 * odd
    spare = jnp.where(
        spare_line == 1,
        jnp.broadcast_to(jnp.sum(total, axis=0, keepdims=True), (8, LANES)),
        0.0,
    )
    for lane_off, number in enumerate((row.astype(jnp.float32), col.astype(jnp.float32), live)):
        here = jnp.logical_and(spare_line == 0, spare_lane == first_lane + lane_off)
        spare = jnp.where(here, number, spare)
    for member in range(16):
        for kept, side_half in ((True, half), (False, 1 - half)):
            top = pl.multiple_of(side_half * 128 + member * 8, 8)
            for part in range(3):
                for side in range(2):
                    put = part * 16 + side * 8
                    value = sums[part, pl.ds(top, 8), side * LANES : (side + 1) * LANES]
                    if kept:
                        keep[member, put : put + 8, :] = value
                    else:
                        send[member * PIECE + put : member * PIECE + put + 8, :] = value
            if kept:
                keep[member, SPARE:PIECE, :] = spare
            else:
                send[member * PIECE + SPARE : member * PIECE + PIECE, :] = spare
    for member in range(8):
        lines = slice(member * 40, member * 40 + 40)
        for part in range(2):
            put = PIECE + part * 40
            keep[8 - 8 * odd + member, put : put + 40, :] = grads[part, 1, lines, :]
            keep[8 * odd + member, put : put + 40, :] = jnp.where(
                inside, grads[part, 2 * odd, lines, :], 0.0
            )
            put = 16 * PIECE + member * 80 + part * 40
            send[put : put + 40, :] = grads[part, 2 - 2 * odd, lines, :]


def merge_kernel(keep, got, out):
    for member in range(16):
        out[member, :PIECE, :] = keep[member, :PIECE, :] + got[member * PIECE : (member + 1) * PIECE, :]
    mine = 8 - 8 * (my_place()[0] & 1)
    for member in range(8):
        put = 16 * PIECE + member * 80
        out[mine + member, PIECE:, :] = keep[mine + member, PIECE:, :] + got[put : put + 80, :]
        out[8 - mine + member, PIECE:, :] = keep[8 - mine + member, PIECE:, :]


def reduce_kernel(pieces, out):
    total = pieces[0, :PIECE, :]
    for member in range(1, 16):
        total = total + pieces[member, :PIECE, :]
    for layer in range(8):
        out[layer] = total


def probe_kernel(layers, probe, out):
    tile, group = my_place()
    top = pl.multiple_of(half_of(tile) * 128 + (8 - 8 * (tile & 1) + group) * 8, 8)
    summed = layers[0]
    for layer in range(1, 8):
        summed = summed + layers[layer]
    mean = jnp.sum(summed[SPARE + 1 : SPARE + 2]) * (1.0 / (WIN * WIN))
    for side in range(2):
        bottom = summed[32 + side * 8 : 40 + side * 8] + 0.25 * mean + 1e-05
        for part in range(2):
            lines = part * 16 + side * 8
            old = probe[part, pl.ds(top, 8), side * LANES : (side + 1) * LANES]
            new = old - summed[lines : lines + 8] / bottom
            for member in range(16):
                out[member, lines : lines + 8, :] = new


def gather_kernel(mine, other, out):
    half = half_of(my_place()[0])
    for source, which in ((mine, half), (other, 1 - half)):
        for member in range(16):
            top = pl.multiple_of(which * 128 + member * 8, 8)
            for part in range(2):
                for side in range(2):
                    lines = part * 16 + side * 8
                    out[part, pl.ds(top, 8), side * LANES : (side + 1) * LANES] = source[
                        member, lines : lines + 8, :
                    ]


def shine(light, group, total, at, block):
    row, col = at[0].astype(jnp.int32), at[1].astype(jnp.int32)
    top = 64 + group * 40 - row
    turn = lax.rem(col, LANES)
    lane = lax.broadcasted_iota(jnp.int32, (40, LANES), 1)
    before = pltpu.roll(light[block, pl.ds(top, 40), :], turn, 1)
    after = pltpu.roll(light[block + 1, pl.ds(top, 40), :], turn, 1)
    return total + at[2] * jnp.where(lane < col, before, after)


def prep_kernel(probe, light, peak):
    blank = jnp.zeros((64, LANES), jnp.float32)
    most = jnp.zeros((WIN, LANES), jnp.float32)
    for side in range(2):
        cols = slice(side * LANES, (side + 1) * LANES)
        bright = probe[0, :, cols] * probe[0, :, cols] + probe[1, :, cols] * probe[1, :, cols]
        most = jnp.maximum(most, bright)
        light[1 + side, 64:320, :] = bright
        light[1 + side, 0:64, :] = blank
        light[1 + side, 320:384, :] = blank
        light[3 * side, :, :] = jnp.zeros((384, LANES), jnp.float32)
    peak[...] = jnp.full((8, LANES), jnp.max(most), jnp.float32)


def object_kernel(pieces, old, light, peak, out, at, sem):
    copy = pltpu.make_async_copy(pieces.at[:, SPARE : SPARE + 1, :], at, sem)
    copy.start()
    gradient = pieces[0, PIECE:, :]
    for member in range(1, 16):
        gradient = gradient + pieces[member, PIECE:, :]
    copy.wait()
    tile, group = my_place()
    odd = tile & 1
    mine = 8 - 8 * odd
    total = jnp.zeros((40, LANES), jnp.float32)
    outside = jnp.zeros((40, LANES), jnp.float32)
    for member in range(8):
        for core in range(2):
            block = 1 - core * (1 - odd) + (1 - core) * odd
            seen = [at[mine + member, 0, core * 8 + k] for k in range(3)]
            total = shine(light, group, total, seen, block)
        seen = [at[8 - mine + member, 0, (1 - odd) * 8 + k] for k in range(3)]
        outside = shine(light, group, outside, seen, 2 - 2 * odd)
    total = total + jnp.where(far_exists(tile), outside, 0.0)
    bottom = total + 0.25 * (peak[0:1, :] + 1e-06)
    for part in range(2):
        out[part] = old[part] - gradient[part * 40 : part * 40 + 40, :] / bottom


def my_place():
    return lax.axis_index("tile"), lax.axis_index("group")


def half_of(tile):
    return (tile ^ (tile >> 1)) & 1


def far_exists(tile):
    return jnp.logical_and(tile > 0, tile < TILES - 1)


def swap_cores(value):
    return lax.ppermute(value, "tile", [(i, i ^ 1) for i in range(TILES)])


def exchange_z(value):
    groups = [[4 * layer + rest for layer in range(TILES // 4)] for rest in range(4)]
    return lax.all_to_all(value, "tile", 0, 0, axis_index_groups=groups)


def exchange(value):
    groups = []
    for first in range(1, TILES, 2):
        second = (first + 1) % TILES
        groups.append([first * 8 + i for i in range(8)] + [second * 8 + i for i in range(8)])
    return lax.all_to_all(value, ("tile", "group"), 0, 0, axis_index_groups=groups)


def on_chip(value):
    return pltpu.with_memory_space_constraint(value, pltpu.VMEM)


def kernel_call(body, out_shape, in_specs, out_specs, megabytes, **kwargs):
    return pl.pallas_call(
        body,
        out_shape=out_shape,
        in_specs=in_specs,
        out_specs=out_specs,
        compiler_params=pltpu.CompilerParams(vmem_limit_bytes=megabytes << 20),
        name=body.__name__.removesuffix("_kernel"),
        **kwargs,
    )


def local(object_field, probe_field, amplitudes, row_start, column_start, live_slots):
    smem, vmem = pl.BlockSpec(memory_space=SMEM), pl.BlockSpec(memory_space=VMEM)
    row_table, col_table = (on_chip(jnp.asarray(table)) for table in split_tables())
    probe = on_chip(probe_field)

    def buffer(*dims):
        return pltpu.VMEM(dims, jnp.float32)

    own = object_field.reshape(80, LANES)
    stack = exchange(jnp.broadcast_to(own, (16, 80, LANES)))
    light, peak = kernel_call(
        prep_kernel,
        (buffer(4, 384, LANES), buffer(8, LANES)),
        [vmem],
        (vmem,) * 2,
        4,
        cost_estimate=pl.CostEstimate(flops=300000, bytes_accessed=2000000, transcendentals=0),
    )(probe)
    keep, send = kernel_call(
        window_kernel,
        (buffer(16, LINES, LANES), buffer(16 * PIECE + 640, LANES)),
        [smem] * 3 + [vmem] * 6,
        (vmem,) * 2,
        24,
        scratch_shapes=[buffer(2, 3, 320, LANES), buffer(2, 3, 320, LANES), buffer(3, WIN, WIN)],
    )(
        row_start, column_start, live_slots, on_chip(stack), on_chip(swap_cores(stack)), probe,
        on_chip(amplitudes), row_table, col_table,
    )

    got, light = lax.optimization_barrier((swap_cores(send), light))
    merged = kernel_call(merge_kernel, buffer(16, LINES, LANES), [vmem] * 2, vmem, 4)(
        keep, on_chip(got)
    )
    pieces = exchange(merged)
    total = kernel_call(reduce_kernel, buffer(8, PIECE, LANES), [vmem], vmem, 4)(on_chip(pieces))
    piece = kernel_call(probe_kernel, buffer(16, 32, LANES), [vmem] * 2, vmem, 4)(
        on_chip(exchange_z(total)), probe
    )

    mine, pieces = lax.optimization_barrier((exchange(piece), pieces))
    new_object = kernel_call(
        object_kernel,
        jax.ShapeDtypeStruct((2, 40, LANES), jnp.float32),
        [vmem] * 4,
        vmem,
        4,
        scratch_shapes=[pltpu.SMEM((16, 1, LANES), jnp.float32), pltpu.SemaphoreType.DMA],
        cost_estimate=pl.CostEstimate(flops=700000, bytes_accessed=2000000, transcendentals=0),
    )(on_chip(pieces), on_chip(object_field), on_chip(light), peak)
    new_probe = kernel_call(
        gather_kernel, jax.ShapeDtypeStruct((2, WIN, WIN), jnp.float32), [vmem] * 2, vmem, 4
    )(on_chip(mine), on_chip(swap_cores(mine)))
    return new_object, new_probe


def solution(mesh):
    return jax.shard_map(
        local,
        mesh=mesh,
        in_specs=(
            P(None, "group", "tile"),
            P(),
            P(("tile", "group"), None, None),
            P(("tile", "group")),
            P(("tile", "group")),
            P(("tile", "group")),
        ),
        out_specs=(P(None, "group", "tile"), P()),
        check_vma=False,
    )
```

```python
import jax
import jax.numpy as jnp
import ml_dtypes
import numpy as np
from jax import lax
from jax.experimental import pallas as pl
from jax.experimental.pallas import tpu as pltpu
from jax.sharding import PartitionSpec as P

WIN = 256
LANES = 128
TILES = 32
SPARE = 48
PIECE = 56
LINES = 136
SMEM = pltpu.MemorySpace.SMEM
VMEM = pltpu.MemorySpace.VMEM


def split_tables():
    counter = np.arange(WIN)
    angles = 2.0 * np.pi / WIN * (counter[:, None] * counter[None, :] % WIN)
    cos, sin = np.cos(angles) / np.sqrt(WIN), np.sin(angles) / np.sqrt(WIN)
    both = np.concatenate([cos[:LANES], cos[LANES : LANES + 1], sin[1:LANES]], axis=0)
    order = np.concatenate([counter[: LANES + 1], counter[:LANES:-1]])
    high = both.astype(ml_dtypes.bfloat16)
    low = (both - high.astype(np.float64)).astype(ml_dtypes.bfloat16)
    select = (order[:, None] == counter[None, :]).astype(ml_dtypes.bfloat16)
    rows = np.concatenate([high, low, select], axis=0)
    return rows, np.concatenate([high.T, low.T, select.T], axis=0)


def halves(value):
    high = value.astype(jnp.bfloat16)
    low = (value - high.astype(jnp.float32)).astype(jnp.bfloat16)
    return high, low


def dot(left, right):
    return jnp.dot(left, right, preferred_element_type=jnp.float32)


def product(left, right):
    return dot(left[0], right[0]) + dot(left[0], right[1]) + dot(left[1], right[0])


def unfold(cos_real, cos_imag, sin_real, sin_imag, axis):
    zeroth = lax.broadcasted_iota(jnp.int32, cos_real.shape, axis) == 0
    odd_real, odd_imag = jnp.where(zeroth, 0.0, sin_imag), jnp.where(zeroth, 0.0, sin_real)
    low = cos_real + odd_real, cos_imag - odd_imag
    high = (
        jnp.where(zeroth, sin_real, cos_real - odd_real),
        jnp.where(zeroth, sin_imag, cos_imag + odd_imag),
    )
    return tuple(jnp.concatenate(pair, axis=axis) for pair in zip(low, high))


def fold(real, imag, axis):
    if axis == 0:
        (low_r, high_r), (low_i, high_i) = ((v[:LANES], v[LANES:]) for v in (real, imag))
    else:
        (low_r, high_r), (low_i, high_i) = ((v[:, :LANES], v[:, LANES:]) for v in (real, imag))
    zeroth = lax.broadcasted_iota(jnp.int32, low_r.shape, axis) == 0
    even = (low_r + jnp.where(zeroth, 0.0, high_r), low_i + jnp.where(zeroth, 0.0, high_i))
    odd = (jnp.where(zeroth, high_r, high_i - low_i), jnp.where(zeroth, high_i, low_r - high_r))
    return tuple(jnp.concatenate(pair, axis=axis) for pair in zip(even, odd))


def parts(table):
    return table[0:WIN], table[WIN : 2 * WIN]


def forward(real, imag, rows, cols):
    along = product(parts(rows), halves(jnp.concatenate([real, imag], axis=1)))
    real, imag = unfold(
        along[:LANES, :WIN], along[:LANES, WIN:], along[LANES:, :WIN], along[LANES:, WIN:], 0
    )
    across = product(halves(jnp.concatenate([real, imag], axis=0)), parts(cols))
    return unfold(
        across[:WIN, :LANES], across[WIN:, :LANES], across[:WIN, LANES:], across[WIN:, LANES:], 1
    )


def inverse(real, imag, rows, cols):
    real, imag = fold(real, imag, 0)
    along = product(parts(cols), halves(jnp.concatenate([real, imag], axis=1)))
    real, imag = fold(along[:, :WIN], along[:, WIN:], 1)
    across = product(halves(jnp.concatenate([real, imag], axis=0)), parts(rows))
    return across[:WIN], across[WIN:]


def reordered(value, rows, cols):
    taken = dot(rows[2 * WIN :], jnp.concatenate(halves(value), axis=1)).astype(jnp.bfloat16)
    taken = dot(jnp.concatenate([taken[:, :WIN], taken[:, WIN:]], axis=0), cols[2 * WIN :])
    return taken[:WIN] + taken[WIN:]


def window_kernel(
    row_ref, col_ref, live_ref, stack, near, probe, amps, row_table, col_table,
    keep, send, field, grads, sums,
):
    row, col = row_ref[0], col_ref[0]
    live = live_ref[0].astype(jnp.float32)
    tile, _ = my_place()
    odd, half = tile & 1, half_of(tile)
    inside = far_exists(tile)
    for member in range(8):
        lines = slice(member * 40, member * 40 + 40)
        for part in range(2):
            held = slice(part * 40, part * 40 + 40)
            field[part, 1, lines, :] = stack[8 - 8 * odd + member, held, :]
            field[part, 2 * odd, lines, :] = jnp.where(inside, stack[8 * odd + member, held, :], 0.0)
            field[part, 2 - 2 * odd, lines, :] = near[8 * odd + member, held, :]
    lane = lax.broadcasted_iota(jnp.int32, (WIN, LANES), 1)
    back = lax.rem(LANES - col, LANES)
    ahead = lax.rem(col, LANES)
    first = lane < LANES - col

    def cut(part):
        turned = [
            pltpu.roll(field[part, block, pl.ds(row, WIN), :], back, 1) for block in range(3)
        ]
        return jnp.concatenate(
            [jnp.where(first, turned[0], turned[1]), jnp.where(first, turned[1], turned[2])], axis=1
        )

    sample_real, sample_imag = cut(0), cut(1)
    probe_real, probe_imag = probe[0], probe[1]
    exit_real = probe_real * sample_real - probe_imag * sample_imag
    exit_imag = probe_real * sample_imag + probe_imag * sample_real
    rows, cols = row_table[...], col_table[...]
    far_real, far_imag = forward(exit_real, exit_imag, rows, cols)
    power = far_real * far_real + far_imag * far_imag
    factor = 1.0 - reordered(amps[0], rows, cols) * lax.rsqrt(jnp.maximum(power, 0.0625))
    miss_real, miss_imag = inverse(far_real * factor, far_imag * factor, rows, cols)
    miss_real = miss_real * live
    miss_imag = miss_imag * live
    terms = (
        probe_real * miss_real + probe_imag * miss_imag,
        probe_real * miss_imag - probe_imag * miss_real,
    )
    wrapped = lane < col
    zero = jnp.zeros((WIN, LANES), jnp.float32)
    grads[...] = jnp.zeros_like(grads)
    for part in range(2):
        start = pltpu.roll(terms[part][:, :LANES], ahead, 1)
        end = pltpu.roll(terms[part][:, LANES:], ahead, 1)
        grads[part, 0, pl.ds(row, WIN), :] = jnp.where(wrapped, zero, start)
        grads[part, 1, pl.ds(row, WIN), :] = jnp.where(wrapped, start, end)
        grads[part, 2, pl.ds(row, WIN), :] = jnp.where(wrapped, end, zero)
    window_light = live * (sample_real * sample_real + sample_imag * sample_imag)
    sums[0] = sample_real * miss_real + sample_imag * miss_imag
    sums[1] = sample_real * miss_imag - sample_imag * miss_real
    sums[2] = window_light
    total = jnp.zeros((8, LANES), jnp.float32)
    for line in range(0, WIN, 8):
        total = total + window_light[line : line + 8, :LANES] + window_light[line : line + 8, LANES:]
    spare_line = lax.broadcasted_iota(jnp.int32, (8, LANES), 0)
    spare_lane = lax.broadcasted_iota(jnp.int32, (8, LANES), 1)
    first_lane = 8 * odd
    spare = jnp.where(
        spare_line == 1,
        jnp.broadcast_to(jnp.sum(total, axis=0, keepdims=True), (8, LANES)),
        0.0,
    )
    for lane_off, number in enumerate((row.astype(jnp.float32), col.astype(jnp.float32), live)):
        here = jnp.logical_and(spare_line == 0, spare_lane == first_lane + lane_off)
        spare = jnp.where(here, number, spare)
    for member in range(16):
        for kept, side_half in ((True, half), (False, 1 - half)):
            top = pl.multiple_of(side_half * 128 + member * 8, 8)
            for part in range(3):
                for side in range(2):
                    put = part * 16 + side * 8
                    value = sums[part, pl.ds(top, 8), side * LANES : (side + 1) * LANES]
                    if kept:
                        keep[member, put : put + 8, :] = value
                    else:
                        send[member * PIECE + put : member * PIECE + put + 8, :] = value
            if kept:
                keep[member, SPARE:PIECE, :] = spare
            else:
                send[member * PIECE + SPARE : member * PIECE + PIECE, :] = spare
    for member in range(8):
        lines = slice(member * 40, member * 40 + 40)
        for part in range(2):
            put = PIECE + part * 40
            keep[8 - 8 * odd + member, put : put + 40, :] = grads[part, 1, lines, :]
            keep[8 * odd + member, put : put + 40, :] = jnp.where(
                inside, grads[part, 2 * odd, lines, :], 0.0
            )
            put = 16 * PIECE + member * 80 + part * 40
            send[put : put + 40, :] = grads[part, 2 - 2 * odd, lines, :]


def merge_kernel(keep, got, out):
    for member in range(16):
        out[member, :PIECE, :] = keep[member, :PIECE, :] + got[member * PIECE : (member + 1) * PIECE, :]
    mine = 8 - 8 * (my_place()[0] & 1)
    for member in range(8):
        put = 16 * PIECE + member * 80
        out[mine + member, PIECE:, :] = keep[mine + member, PIECE:, :] + got[put : put + 80, :]
        out[8 - mine + member, PIECE:, :] = keep[8 - mine + member, PIECE:, :]


def reduce_kernel(pieces, out):
    total = pieces[0, :PIECE, :]
    for member in range(1, 16):
        total = total + pieces[member, :PIECE, :]
    out[...] = total


def probe_kernel(one, two, probe, out):
    tile, group = my_place()
    top = pl.multiple_of(half_of(tile) * 128 + (8 - 8 * (tile & 1) + group) * 8, 8)
    summed = one[...] + two[...]
    mean = jnp.sum(summed[SPARE + 1 : SPARE + 2]) * (1.0 / (WIN * WIN))
    for side in range(2):
        bottom = summed[32 + side * 8 : 40 + side * 8] + 0.25 * mean + 1e-05
        for part in range(2):
            lines = part * 16 + side * 8
            old = probe[part, pl.ds(top, 8), side * LANES : (side + 1) * LANES]
            new = old - summed[lines : lines + 8] / bottom
            for member in range(16):
                out[member, lines : lines + 8, :] = new


def gather_kernel(mine, other, out):
    half = half_of(my_place()[0])
    for source, which in ((mine, half), (other, 1 - half)):
        for member in range(16):
            top = pl.multiple_of(which * 128 + member * 8, 8)
            for part in range(2):
                for side in range(2):
                    lines = part * 16 + side * 8
                    out[part, pl.ds(top, 8), side * LANES : (side + 1) * LANES] = source[
                        member, lines : lines + 8, :
                    ]


def shine(light, group, total, at, block):
    row, col = at[0].astype(jnp.int32), at[1].astype(jnp.int32)
    top = 64 + group * 40 - row
    turn = lax.rem(col, LANES)
    lane = lax.broadcasted_iota(jnp.int32, (40, LANES), 1)
    before = pltpu.roll(light[block, pl.ds(top, 40), :], turn, 1)
    after = pltpu.roll(light[block + 1, pl.ds(top, 40), :], turn, 1)
    return total + at[2] * jnp.where(lane < col, before, after)


def prep_kernel(probe, light, peak):
    blank = jnp.zeros((64, LANES), jnp.float32)
    most = jnp.zeros((WIN, LANES), jnp.float32)
    for side in range(2):
        cols = slice(side * LANES, (side + 1) * LANES)
        bright = probe[0, :, cols] * probe[0, :, cols] + probe[1, :, cols] * probe[1, :, cols]
        most = jnp.maximum(most, bright)
        light[1 + side, 64:320, :] = bright
        light[1 + side, 0:64, :] = blank
        light[1 + side, 320:384, :] = blank
        light[3 * side, :, :] = jnp.zeros((384, LANES), jnp.float32)
    peak[...] = jnp.full((8, LANES), jnp.max(most), jnp.float32)


def object_kernel(pieces, old, light, peak, out, at, sem):
    copy = pltpu.make_async_copy(pieces.at[:, SPARE : SPARE + 1, :], at, sem)
    copy.start()
    gradient = pieces[0, PIECE:, :]
    for member in range(1, 16):
        gradient = gradient + pieces[member, PIECE:, :]
    copy.wait()
    tile, group = my_place()
    odd = tile & 1
    mine = 8 - 8 * odd
    total = jnp.zeros((40, LANES), jnp.float32)
    outside = jnp.zeros((40, LANES), jnp.float32)
    for member in range(8):
        for core in range(2):
            block = 1 - core * (1 - odd) + (1 - core) * odd
            seen = [at[mine + member, 0, core * 8 + k] for k in range(3)]
            total = shine(light, group, total, seen, block)
        seen = [at[8 - mine + member, 0, (1 - odd) * 8 + k] for k in range(3)]
        outside = shine(light, group, outside, seen, 2 - 2 * odd)
    total = total + jnp.where(far_exists(tile), outside, 0.0)
    bottom = total + 0.25 * (peak[0:1, :] + 1e-06)
    for part in range(2):
        out[part] = old[part] - gradient[part * 40 : part * 40 + 40, :] / bottom


def my_place():
    return lax.axis_index("tile"), lax.axis_index("group")


def half_of(tile):
    return (tile ^ (tile >> 1)) & 1


def far_exists(tile):
    return jnp.logical_and(tile > 0, tile < TILES - 1)


def swap_cores(value):
    return lax.ppermute(value, "tile", [(i, i ^ 1) for i in range(TILES)])


def swap_z(value, mask):
    pairs = []
    for tile in range(TILES):
        layer, rest = divmod(tile, 4)
        ahead = 1 if rest == 0 else 0
        other = (((layer - ahead) % (TILES // 4)) ^ mask) + ahead
        pairs.append((tile, other % (TILES // 4) * 4 + rest))
    return lax.ppermute(value, "tile", pairs)


def exchange(value):
    groups = []
    for first in range(1, TILES, 2):
        second = (first + 1) % TILES
        groups.append([first * 8 + i for i in range(8)] + [second * 8 + i for i in range(8)])
    return lax.all_to_all(value, ("tile", "group"), 0, 0, axis_index_groups=groups)


def on_chip(value):
    return pltpu.with_memory_space_constraint(value, pltpu.VMEM)


def kernel_call(body, out_shape, in_specs, out_specs, megabytes, **kwargs):
    return pl.pallas_call(
        body,
        out_shape=out_shape,
        in_specs=in_specs,
        out_specs=out_specs,
        compiler_params=pltpu.CompilerParams(vmem_limit_bytes=megabytes << 20),
        name=body.__name__.removesuffix("_kernel"),
        **kwargs,
    )


def local(object_field, probe_field, amplitudes, row_start, column_start, live_slots):
    smem, vmem = pl.BlockSpec(memory_space=SMEM), pl.BlockSpec(memory_space=VMEM)
    row_table, col_table = (on_chip(jnp.asarray(table)) for table in split_tables())
    probe = on_chip(probe_field)

    def buffer(*dims):
        return pltpu.VMEM(dims, jnp.float32)

    own = object_field.reshape(80, LANES)
    stack = exchange(jnp.broadcast_to(own, (16, 80, LANES)))
    light, peak = kernel_call(
        prep_kernel,
        (buffer(4, 384, LANES), buffer(8, LANES)),
        [vmem],
        (vmem,) * 2,
        4,
        cost_estimate=pl.CostEstimate(flops=300000, bytes_accessed=2000000, transcendentals=0),
    )(probe)
    keep, send = kernel_call(
        window_kernel,
        (buffer(16, LINES, LANES), buffer(16 * PIECE + 640, LANES)),
        [smem] * 3 + [vmem] * 6,
        (vmem,) * 2,
        24,
        scratch_shapes=[buffer(2, 3, 320, LANES), buffer(2, 3, 320, LANES), buffer(3, WIN, WIN)],
    )(
        row_start, column_start, live_slots, on_chip(stack), on_chip(swap_cores(stack)), probe,
        on_chip(amplitudes), row_table, col_table,
    )

    got, light = lax.optimization_barrier((swap_cores(send), light))
    merged = kernel_call(merge_kernel, buffer(16, LINES, LANES), [vmem] * 2, vmem, 4)(
        keep, on_chip(got)
    )
    pieces = exchange(merged)
    total = kernel_call(reduce_kernel, buffer(PIECE, LANES), [vmem], vmem, 4)(on_chip(pieces))
    new_object = kernel_call(
        object_kernel,
        jax.ShapeDtypeStruct((2, 40, LANES), jnp.float32),
        [vmem] * 4,
        vmem,
        4,
        scratch_shapes=[pltpu.SMEM((16, 1, LANES), jnp.float32), pltpu.SemaphoreType.DMA],
        cost_estimate=pl.CostEstimate(flops=700000, bytes_accessed=2000000, transcendentals=0),
    )(on_chip(pieces), on_chip(object_field), on_chip(light), peak)
    for mask in (1, 2):
        total = total + swap_z(total, mask)
    got, new_object = lax.optimization_barrier((swap_z(total, 6), new_object))
    piece = kernel_call(probe_kernel, buffer(16, 32, LANES), [vmem] * 3, vmem, 4)(
        on_chip(total), on_chip(got), probe
    )

    mine = exchange(piece)
    new_probe = kernel_call(
        gather_kernel, jax.ShapeDtypeStruct((2, WIN, WIN), jnp.float32), [vmem] * 2, vmem, 4
    )(on_chip(mine), on_chip(swap_cores(mine)))
    return new_object, new_probe


def solution(mesh):
    return jax.shard_map(
        local,
        mesh=mesh,
        in_specs=(
            P(None, "group", "tile"),
            P(),
            P(("tile", "group"), None, None),
            P(("tile", "group")),
            P(("tile", "group")),
            P(("tile", "group")),
        ),
        out_specs=(P(None, "group", "tile"), P()),
        check_vma=False,
    )
```

```python
import jax
import jax.numpy as jnp
import ml_dtypes
import numpy as np
from jax import lax
from jax.experimental import pallas as pl
from jax.experimental.pallas import tpu as pltpu
from jax.sharding import PartitionSpec as P

WIN = 256
LANES = 128
TILES = 32
SPARE = 48
PIECE = 56
LINES = 136
SMEM = pltpu.MemorySpace.SMEM
VMEM = pltpu.MemorySpace.VMEM


def split_tables():
    counter = np.arange(WIN)
    angles = 2.0 * np.pi / WIN * (counter[:, None] * counter[None, :] % WIN)
    cos, sin = np.cos(angles) / np.sqrt(WIN), np.sin(angles) / np.sqrt(WIN)
    both = np.concatenate([cos[:LANES], cos[LANES : LANES + 1], sin[1:LANES]], axis=0)
    order = np.concatenate([counter[: LANES + 1], counter[:LANES:-1]])
    high = both.astype(ml_dtypes.bfloat16)
    low = (both - high.astype(np.float64)).astype(ml_dtypes.bfloat16)
    select = (order[:, None] == counter[None, :]).astype(ml_dtypes.bfloat16)
    rows = np.concatenate([high, low, select], axis=0)
    return rows, np.concatenate([high.T, low.T, select.T], axis=0)


def halves(value):
    high = value.astype(jnp.bfloat16)
    low = (value - high.astype(jnp.float32)).astype(jnp.bfloat16)
    return high, low


def dot(left, right):
    return jnp.dot(left, right, preferred_element_type=jnp.float32)


def product(left, right):
    return dot(left[0], right[0]) + dot(left[0], right[1]) + dot(left[1], right[0])


def unfold(cos_real, cos_imag, sin_real, sin_imag, axis):
    zeroth = lax.broadcasted_iota(jnp.int32, cos_real.shape, axis) == 0
    odd_real, odd_imag = jnp.where(zeroth, 0.0, sin_imag), jnp.where(zeroth, 0.0, sin_real)
    low = cos_real + odd_real, cos_imag - odd_imag
    high = (
        jnp.where(zeroth, sin_real, cos_real - odd_real),
        jnp.where(zeroth, sin_imag, cos_imag + odd_imag),
    )
    return tuple(jnp.concatenate(pair, axis=axis) for pair in zip(low, high))


def fold(real, imag, axis):
    if axis == 0:
        (low_r, high_r), (low_i, high_i) = ((v[:LANES], v[LANES:]) for v in (real, imag))
    else:
        (low_r, high_r), (low_i, high_i) = ((v[:, :LANES], v[:, LANES:]) for v in (real, imag))
    zeroth = lax.broadcasted_iota(jnp.int32, low_r.shape, axis) == 0
    even = (low_r + jnp.where(zeroth, 0.0, high_r), low_i + jnp.where(zeroth, 0.0, high_i))
    odd = (jnp.where(zeroth, high_r, high_i - low_i), jnp.where(zeroth, high_i, low_r - high_r))
    return tuple(jnp.concatenate(pair, axis=axis) for pair in zip(even, odd))


def parts(table):
    return table[0:WIN], table[WIN : 2 * WIN]


def forward(real, imag, rows, cols):
    along = product(parts(rows), halves(jnp.concatenate([real, imag], axis=1)))
    real, imag = unfold(
        along[:LANES, :WIN], along[:LANES, WIN:], along[LANES:, :WIN], along[LANES:, WIN:], 0
    )
    across = product(halves(jnp.concatenate([real, imag], axis=0)), parts(cols))
    return unfold(
        across[:WIN, :LANES], across[WIN:, :LANES], across[:WIN, LANES:], across[WIN:, LANES:], 1
    )


def inverse(real, imag, rows, cols):
    real, imag = fold(real, imag, 0)
    along = product(parts(cols), halves(jnp.concatenate([real, imag], axis=1)))
    real, imag = fold(along[:, :WIN], along[:, WIN:], 1)
    across = product(halves(jnp.concatenate([real, imag], axis=0)), parts(rows))
    return across[:WIN], across[WIN:]


def reordered(value, rows, cols):
    taken = dot(rows[2 * WIN :], jnp.concatenate(halves(value), axis=1)).astype(jnp.bfloat16)
    taken = dot(jnp.concatenate([taken[:, :WIN], taken[:, WIN:]], axis=0), cols[2 * WIN :])
    return taken[:WIN] + taken[WIN:]


def window_kernel(
    row_ref, col_ref, live_ref, stack, near, probe, amps, row_table, col_table,
    send, sums, grads, spare_out, field,
):
    row, col = row_ref[0], col_ref[0]
    live = live_ref[0].astype(jnp.float32)
    tile, _ = my_place()
    odd, half = tile & 1, half_of(tile)
    inside = far_exists(tile)
    for member in range(8):
        lines = slice(member * 40, member * 40 + 40)
        for part in range(2):
            held = slice(part * 40, part * 40 + 40)
            field[part, 1, lines, :] = stack[8 - 8 * odd + member, held, :]
            field[part, 2 * odd, lines, :] = jnp.where(inside, stack[8 * odd + member, held, :], 0.0)
            field[part, 2 - 2 * odd, lines, :] = near[8 * odd + member, held, :]
    lane = lax.broadcasted_iota(jnp.int32, (WIN, LANES), 1)
    back = lax.rem(LANES - col, LANES)
    ahead = lax.rem(col, LANES)
    first = lane < LANES - col

    def cut(part):
        turned = [
            pltpu.roll(field[part, block, pl.ds(row, WIN), :], back, 1) for block in range(3)
        ]
        return jnp.concatenate(
            [jnp.where(first, turned[0], turned[1]), jnp.where(first, turned[1], turned[2])], axis=1
        )

    sample_real, sample_imag = cut(0), cut(1)
    probe_real, probe_imag = probe[0], probe[1]
    exit_real = probe_real * sample_real - probe_imag * sample_imag
    exit_imag = probe_real * sample_imag + probe_imag * sample_real
    rows, cols = row_table[...], col_table[...]
    far_real, far_imag = forward(exit_real, exit_imag, rows, cols)
    power = far_real * far_real + far_imag * far_imag
    factor = 1.0 - reordered(amps[0], rows, cols) * lax.rsqrt(jnp.maximum(power, 0.0625))
    miss_real, miss_imag = inverse(far_real * factor, far_imag * factor, rows, cols)
    miss_real = miss_real * live
    miss_imag = miss_imag * live
    terms = (
        probe_real * miss_real + probe_imag * miss_imag,
        probe_real * miss_imag - probe_imag * miss_real,
    )
    wrapped = lane < col
    zero = jnp.zeros((WIN, LANES), jnp.float32)
    grads[...] = jnp.zeros_like(grads)
    for part in range(2):
        start = pltpu.roll(terms[part][:, :LANES], ahead, 1)
        end = pltpu.roll(terms[part][:, LANES:], ahead, 1)
        grads[part, 0, pl.ds(row, WIN), :] = jnp.where(wrapped, zero, start)
        grads[part, 1, pl.ds(row, WIN), :] = jnp.where(wrapped, start, end)
        grads[part, 2, pl.ds(row, WIN), :] = jnp.where(wrapped, end, zero)
    window_light = live * (sample_real * sample_real + sample_imag * sample_imag)
    sums[0] = sample_real * miss_real + sample_imag * miss_imag
    sums[1] = sample_real * miss_imag - sample_imag * miss_real
    sums[2] = window_light
    total = jnp.zeros((8, LANES), jnp.float32)
    for line in range(0, WIN, 8):
        total = total + window_light[line : line + 8, :LANES] + window_light[line : line + 8, LANES:]
    spare_line = lax.broadcasted_iota(jnp.int32, (8, LANES), 0)
    spare_lane = lax.broadcasted_iota(jnp.int32, (8, LANES), 1)
    first_lane = 8 * odd
    spare = jnp.where(
        spare_line == 1,
        jnp.broadcast_to(jnp.sum(total, axis=0, keepdims=True), (8, LANES)),
        0.0,
    )
    for lane_off, number in enumerate((row.astype(jnp.float32), col.astype(jnp.float32), live)):
        here = jnp.logical_and(spare_line == 0, spare_lane == first_lane + lane_off)
        spare = jnp.where(here, number, spare)
    spare_out[...] = spare
    for member in range(16):
        first_line = member * PIECE
        top = pl.multiple_of((1 - half) * 128 + member * 8, 8)
        for part in range(3):
            for side in range(2):
                put = first_line + part * 16 + side * 8
                send[put : put + 8, :] = sums[part, pl.ds(top, 8), side * LANES : (side + 1) * LANES]
        send[first_line + SPARE : first_line + PIECE, :] = spare
    for member in range(8):
        lines = slice(member * 40, member * 40 + 40)
        for part in range(2):
            put = 16 * PIECE + member * 80 + part * 40
            send[put : put + 40, :] = grads[part, 2 - 2 * odd, lines, :]


def merge_kernel(sums, grads, spare, got, out):
    tile, _ = my_place()
    odd, half, inside = tile & 1, half_of(tile), far_exists(tile)
    for member in range(16):
        top = pl.multiple_of(half * 128 + member * 8, 8)
        for part in range(3):
            for side in range(2):
                put = part * 16 + side * 8
                other = got[member * PIECE + put : member * PIECE + put + 8, :]
                own = sums[part, pl.ds(top, 8), side * LANES : (side + 1) * LANES]
                out[member, put : put + 8, :] = own + other
        out[member, SPARE:PIECE, :] = spare[...] + got[member * PIECE + SPARE : (member + 1) * PIECE, :]
    for member in range(8):
        lines = slice(member * 40, member * 40 + 40)
        for part in range(2):
            put = PIECE + part * 40
            other = 16 * PIECE + member * 80 + part * 40
            out[8 - 8 * odd + member, put : put + 40, :] = grads[part, 1, lines, :] + got[other : other + 40, :]
            out[8 * odd + member, put : put + 40, :] = jnp.where(
                inside, grads[part, 2 * odd, lines, :], 0.0
            )


def reduce_kernel(pieces, out):
    total = pieces[0, :PIECE, :]
    for member in range(1, 16):
        total = total + pieces[member, :PIECE, :]
    out[...] = total


def probe_kernel(one, two, probe, out):
    tile, group = my_place()
    top = pl.multiple_of(half_of(tile) * 128 + (8 - 8 * (tile & 1) + group) * 8, 8)
    summed = one[...] + two[...]
    mean = jnp.sum(summed[SPARE + 1 : SPARE + 2]) * (1.0 / (WIN * WIN))
    for side in range(2):
        bottom = summed[32 + side * 8 : 40 + side * 8] + 0.25 * mean + 1e-05
        for part in range(2):
            lines = part * 16 + side * 8
            old = probe[part, pl.ds(top, 8), side * LANES : (side + 1) * LANES]
            new = old - summed[lines : lines + 8] / bottom
            for member in range(16):
                out[member, lines : lines + 8, :] = new


def gather_kernel(mine, other, out):
    core = my_place()[0] & 1
    for source, which in ((mine, core), (other, 1 - core)):
        for member in range(16):
            x_hi, group = (member >> 1) & 1, (member >> 2) * 2 + (member & 1)
            top = pl.multiple_of((which ^ x_hi) * 128 + (8 - 8 * which + group) * 8, 8)
            for part in range(2):
                for side in range(2):
                    lines = part * 16 + side * 8
                    out[part, pl.ds(top, 8), side * LANES : (side + 1) * LANES] = source[
                        member, lines : lines + 8, :
                    ]


def shine(light, group, total, at, block):
    row, col = at[0].astype(jnp.int32), at[1].astype(jnp.int32)
    top = 64 + group * 40 - row
    turn = lax.rem(col, LANES)
    lane = lax.broadcasted_iota(jnp.int32, (40, LANES), 1)
    before = pltpu.roll(light[block, pl.ds(top, 40), :], turn, 1)
    after = pltpu.roll(light[block + 1, pl.ds(top, 40), :], turn, 1)
    return total + at[2] * jnp.where(lane < col, before, after)


def prep_kernel(probe, light, peak):
    blank = jnp.zeros((64, LANES), jnp.float32)
    most = jnp.zeros((WIN, LANES), jnp.float32)
    for side in range(2):
        cols = slice(side * LANES, (side + 1) * LANES)
        bright = probe[0, :, cols] * probe[0, :, cols] + probe[1, :, cols] * probe[1, :, cols]
        most = jnp.maximum(most, bright)
        light[1 + side, 64:320, :] = bright
        light[1 + side, 0:64, :] = blank
        light[1 + side, 320:384, :] = blank
        light[3 * side, :, :] = jnp.zeros((384, LANES), jnp.float32)
    peak[...] = jnp.full((8, LANES), jnp.max(most), jnp.float32)


def object_kernel(pieces, old, light, peak, out, at, sem):
    copy = pltpu.make_async_copy(pieces.at[:, SPARE : SPARE + 1, :], at, sem)
    copy.start()
    gradient = pieces[0, PIECE:, :]
    for member in range(1, 16):
        gradient = gradient + pieces[member, PIECE:, :]
    copy.wait()
    tile, group = my_place()
    odd = tile & 1
    mine = 8 - 8 * odd
    total = jnp.zeros((40, LANES), jnp.float32)
    outside = jnp.zeros((40, LANES), jnp.float32)
    for member in range(8):
        for core in range(2):
            block = 1 - core * (1 - odd) + (1 - core) * odd
            seen = [at[mine + member, 0, core * 8 + k] for k in range(3)]
            total = shine(light, group, total, seen, block)
        seen = [at[8 - mine + member, 0, (1 - odd) * 8 + k] for k in range(3)]
        outside = shine(light, group, outside, seen, 2 - 2 * odd)
    total = total + jnp.where(far_exists(tile), outside, 0.0)
    bottom = total + 0.25 * (peak[0:1, :] + 1e-06)
    for part in range(2):
        out[part] = old[part] - gradient[part * 40 : part * 40 + 40, :] / bottom


def my_place():
    return lax.axis_index("tile"), lax.axis_index("group")


def half_of(tile):
    return (tile ^ (tile >> 1)) & 1


def far_exists(tile):
    return jnp.logical_and(tile > 0, tile < TILES - 1)


def swap_cores(value):
    return lax.ppermute(value, "tile", [(i, i ^ 1) for i in range(TILES)])


def swap_z(value, mask):
    pairs = []
    for tile in range(TILES):
        layer, rest = divmod(tile, 4)
        ahead = 1 if rest == 0 else 0
        other = (((layer - ahead) % (TILES // 4)) ^ mask) + ahead
        pairs.append((tile, other % (TILES // 4) * 4 + rest))
    return lax.ppermute(value, "tile", pairs)


def exchange(value):
    groups = []
    for first in range(1, TILES, 2):
        second = (first + 1) % TILES
        groups.append([first * 8 + i for i in range(8)] + [second * 8 + i for i in range(8)])
    return lax.all_to_all(value, ("tile", "group"), 0, 0, axis_index_groups=groups)


def exchange_plane(value):
    groups = []
    for layer in range(TILES // 4):
        for core in range(2):
            groups.append(
                [
                    (layer * 4 + x_hi * 2 + core) * 8 + y * 2 + x_lo
                    for y in range(4)
                    for x_hi in range(2)
                    for x_lo in range(2)
                ]
            )
    return lax.all_to_all(value, ("tile", "group"), 0, 0, axis_index_groups=groups)


def on_chip(value):
    return pltpu.with_memory_space_constraint(value, pltpu.VMEM)


def kernel_call(body, out_shape, in_specs, out_specs, megabytes, **kwargs):
    return pl.pallas_call(
        body,
        out_shape=out_shape,
        in_specs=in_specs,
        out_specs=out_specs,
        compiler_params=pltpu.CompilerParams(vmem_limit_bytes=megabytes << 20),
        name=body.__name__.removesuffix("_kernel"),
        **kwargs,
    )


def local(object_field, probe_field, amplitudes, row_start, column_start, live_slots):
    smem, vmem = pl.BlockSpec(memory_space=SMEM), pl.BlockSpec(memory_space=VMEM)
    row_table, col_table = (on_chip(jnp.asarray(table)) for table in split_tables())
    probe = on_chip(probe_field)

    def buffer(*dims):
        return pltpu.VMEM(dims, jnp.float32)

    own = object_field.reshape(80, LANES)
    stack = exchange(jnp.broadcast_to(own, (16, 80, LANES)))
    light, peak = kernel_call(
        prep_kernel,
        (buffer(4, 384, LANES), buffer(8, LANES)),
        [vmem],
        (vmem,) * 2,
        4,
        cost_estimate=pl.CostEstimate(flops=300000, bytes_accessed=2000000, transcendentals=0),
    )(probe)
    send, sums, grads, spare = kernel_call(
        window_kernel,
        (
            buffer(16 * PIECE + 640, LANES),
            buffer(3, WIN, WIN),
            buffer(2, 3, 320, LANES),
            buffer(8, LANES),
        ),
        [smem] * 3 + [vmem] * 6,
        (vmem,) * 4,
        24,
        scratch_shapes=[buffer(2, 3, 320, LANES)],
    )(
        row_start, column_start, live_slots, on_chip(stack), on_chip(swap_cores(stack)), probe,
        on_chip(amplitudes), row_table, col_table,
    )

    got, light = lax.optimization_barrier((swap_cores(send), light))
    merged = kernel_call(merge_kernel, buffer(16, LINES, LANES), [vmem] * 4, vmem, 4)(
        sums, grads, spare, on_chip(got)
    )
    pieces = exchange(merged)
    total = kernel_call(reduce_kernel, buffer(PIECE, LANES), [vmem], vmem, 4)(on_chip(pieces))
    new_object = kernel_call(
        object_kernel,
        jax.ShapeDtypeStruct((2, 40, LANES), jnp.float32),
        [vmem] * 4,
        vmem,
        4,
        scratch_shapes=[pltpu.SMEM((16, 1, LANES), jnp.float32), pltpu.SemaphoreType.DMA],
        cost_estimate=pl.CostEstimate(flops=700000, bytes_accessed=2000000, transcendentals=0),
    )(on_chip(pieces), on_chip(object_field), on_chip(light), peak)
    for mask in (1, 2):
        total = total + swap_z(total, mask)
    got, new_object = lax.optimization_barrier((swap_z(total, 6), new_object))
    piece = kernel_call(probe_kernel, buffer(16, 32, LANES), [vmem] * 3, vmem, 4)(
        on_chip(total), on_chip(got), probe
    )

    mine = exchange_plane(piece)
    new_probe = kernel_call(
        gather_kernel, jax.ShapeDtypeStruct((2, WIN, WIN), jnp.float32), [vmem] * 2, vmem, 4
    )(on_chip(mine), on_chip(swap_cores(mine)))
    return new_object, new_probe


def solution(mesh):
    return jax.shard_map(
        local,
        mesh=mesh,
        in_specs=(
            P(None, "group", "tile"),
            P(),
            P(("tile", "group"), None, None),
            P(("tile", "group")),
            P(("tile", "group")),
            P(("tile", "group")),
        ),
        out_specs=(P(None, "group", "tile"), P()),
        check_vma=False,
    )
```

```python
import jax
import jax.numpy as jnp
import ml_dtypes
import numpy as np
from jax import lax
from jax.experimental import pallas as pl
from jax.experimental.pallas import tpu as pltpu
from jax.sharding import PartitionSpec as P

WIN = 256
LANES = 128
TILES = 32
SPARE = 48
PIECE = 56
LINES = 136
SMEM = pltpu.MemorySpace.SMEM
VMEM = pltpu.MemorySpace.VMEM


def split_tables():
    counter = np.arange(WIN)
    angles = 2.0 * np.pi / WIN * (counter[:, None] * counter[None, :] % WIN)
    cos, sin = np.cos(angles) / np.sqrt(WIN), np.sin(angles) / np.sqrt(WIN)
    both = np.concatenate([cos[:LANES], cos[LANES : LANES + 1], sin[1:LANES]], axis=0)
    order = np.concatenate([counter[: LANES + 1], counter[:LANES:-1]])
    high = both.astype(ml_dtypes.bfloat16)
    low = (both - high.astype(np.float64)).astype(ml_dtypes.bfloat16)
    select = (order[:, None] == counter[None, :]).astype(ml_dtypes.bfloat16)
    rows = np.concatenate([high, low, select], axis=0)
    return rows, np.concatenate([high.T, low.T, select.T], axis=0)


def halves(value):
    high = value.astype(jnp.bfloat16)
    low = (value - high.astype(jnp.float32)).astype(jnp.bfloat16)
    return high, low


def dot(left, right):
    return jnp.dot(left, right, preferred_element_type=jnp.float32)


def product(left, right):
    return dot(left[0], right[0]) + dot(left[0], right[1]) + dot(left[1], right[0])


def unfold(cos_real, cos_imag, sin_real, sin_imag, axis):
    zeroth = lax.broadcasted_iota(jnp.int32, cos_real.shape, axis) == 0
    odd_real, odd_imag = jnp.where(zeroth, 0.0, sin_imag), jnp.where(zeroth, 0.0, sin_real)
    low = cos_real + odd_real, cos_imag - odd_imag
    high = (
        jnp.where(zeroth, sin_real, cos_real - odd_real),
        jnp.where(zeroth, sin_imag, cos_imag + odd_imag),
    )
    return tuple(jnp.concatenate(pair, axis=axis) for pair in zip(low, high))


def fold(real, imag, axis):
    if axis == 0:
        (low_r, high_r), (low_i, high_i) = ((v[:LANES], v[LANES:]) for v in (real, imag))
    else:
        (low_r, high_r), (low_i, high_i) = ((v[:, :LANES], v[:, LANES:]) for v in (real, imag))
    zeroth = lax.broadcasted_iota(jnp.int32, low_r.shape, axis) == 0
    even = (low_r + jnp.where(zeroth, 0.0, high_r), low_i + jnp.where(zeroth, 0.0, high_i))
    odd = (jnp.where(zeroth, high_r, high_i - low_i), jnp.where(zeroth, high_i, low_r - high_r))
    return tuple(jnp.concatenate(pair, axis=axis) for pair in zip(even, odd))


def parts(table):
    return table[0:WIN], table[WIN : 2 * WIN]


def forward(real, imag, rows, cols):
    along = product(parts(rows), halves(jnp.concatenate([real, imag], axis=1)))
    real, imag = unfold(
        along[:LANES, :WIN], along[:LANES, WIN:], along[LANES:, :WIN], along[LANES:, WIN:], 0
    )
    across = product(halves(jnp.concatenate([real, imag], axis=0)), parts(cols))
    return unfold(
        across[:WIN, :LANES], across[WIN:, :LANES], across[:WIN, LANES:], across[WIN:, LANES:], 1
    )


def inverse(real, imag, rows, cols):
    real, imag = fold(real, imag, 0)
    along = product(parts(cols), halves(jnp.concatenate([real, imag], axis=1)))
    real, imag = fold(along[:, :WIN], along[:, WIN:], 1)
    across = product(halves(jnp.concatenate([real, imag], axis=0)), parts(rows))
    return across[:WIN], across[WIN:]


def reordered(value, rows, cols):
    taken = dot(rows[2 * WIN :], jnp.concatenate(halves(value), axis=1)).astype(jnp.bfloat16)
    taken = dot(jnp.concatenate([taken[:, :WIN], taken[:, WIN:]], axis=0), cols[2 * WIN :])
    return taken[:WIN] + taken[WIN:]


def window_kernel(
    row_ref, col_ref, live_ref, stack, near, probe, amps, row_table, col_table,
    send, sums, grads, spare_out, field,
):
    row, col = row_ref[0], col_ref[0]
    live = live_ref[0].astype(jnp.float32)
    tile, _ = my_place()
    odd, half = tile & 1, half_of(tile)
    inside = far_exists(tile)
    for member in range(8):
        lines = slice(member * 40, member * 40 + 40)
        for part in range(2):
            held = slice(part * 40, part * 40 + 40)
            field[part, 1, lines, :] = stack[8 - 8 * odd + member, held, :]
            field[part, 2 * odd, lines, :] = jnp.where(inside, stack[8 * odd + member, held, :], 0.0)
            field[part, 2 - 2 * odd, lines, :] = near[8 * odd + member, held, :]
    lane = lax.broadcasted_iota(jnp.int32, (WIN, LANES), 1)
    back = lax.rem(LANES - col, LANES)
    ahead = lax.rem(col, LANES)
    first = lane < LANES - col

    def cut(part):
        turned = [
            pltpu.roll(field[part, block, pl.ds(row, WIN), :], back, 1) for block in range(3)
        ]
        return jnp.concatenate(
            [jnp.where(first, turned[0], turned[1]), jnp.where(first, turned[1], turned[2])], axis=1
        )

    sample_real, sample_imag = cut(0), cut(1)
    probe_real, probe_imag = probe[0], probe[1]
    exit_real = probe_real * sample_real - probe_imag * sample_imag
    exit_imag = probe_real * sample_imag + probe_imag * sample_real
    rows, cols = row_table[...], col_table[...]
    far_real, far_imag = forward(exit_real, exit_imag, rows, cols)
    power = far_real * far_real + far_imag * far_imag
    factor = 1.0 - reordered(amps[0], rows, cols) * lax.rsqrt(jnp.maximum(power, 0.0625))
    miss_real, miss_imag = inverse(far_real * factor, far_imag * factor, rows, cols)
    miss_real = miss_real * live
    miss_imag = miss_imag * live
    terms = (
        probe_real * miss_real + probe_imag * miss_imag,
        probe_real * miss_imag - probe_imag * miss_real,
    )
    wrapped = lane < col
    zero = jnp.zeros((WIN, LANES), jnp.float32)
    grads[...] = jnp.zeros_like(grads)
    for part in range(2):
        start = pltpu.roll(terms[part][:, :LANES], ahead, 1)
        end = pltpu.roll(terms[part][:, LANES:], ahead, 1)
        grads[part, 0, pl.ds(row, WIN), :] = jnp.where(wrapped, zero, start)
        grads[part, 1, pl.ds(row, WIN), :] = jnp.where(wrapped, start, end)
        grads[part, 2, pl.ds(row, WIN), :] = jnp.where(wrapped, end, zero)
    window_light = live * (sample_real * sample_real + sample_imag * sample_imag)
    sums[0] = sample_real * miss_real + sample_imag * miss_imag
    sums[1] = sample_real * miss_imag - sample_imag * miss_real
    sums[2] = window_light
    total = jnp.zeros((8, LANES), jnp.float32)
    for line in range(0, WIN, 8):
        total = total + window_light[line : line + 8, :LANES] + window_light[line : line + 8, LANES:]
    spare_line = lax.broadcasted_iota(jnp.int32, (8, LANES), 0)
    spare_lane = lax.broadcasted_iota(jnp.int32, (8, LANES), 1)
    first_lane = 8 * odd
    spare = jnp.where(
        spare_line == 1,
        jnp.broadcast_to(jnp.sum(total, axis=0, keepdims=True), (8, LANES)),
        0.0,
    )
    for lane_off, number in enumerate((row.astype(jnp.float32), col.astype(jnp.float32), live)):
        here = jnp.logical_and(spare_line == 0, spare_lane == first_lane + lane_off)
        spare = jnp.where(here, number, spare)
    spare_out[...] = spare
    for member in range(16):
        first_line = member * PIECE
        top = pl.multiple_of((1 - half) * 128 + member * 8, 8)
        for part in range(3):
            for side in range(2):
                put = first_line + part * 16 + side * 8
                send[put : put + 8, :] = sums[part, pl.ds(top, 8), side * LANES : (side + 1) * LANES]
        send[first_line + SPARE : first_line + PIECE, :] = spare
    for member in range(8):
        lines = slice(member * 40, member * 40 + 40)
        for part in range(2):
            put = 16 * PIECE + member * 80 + part * 40
            send[put : put + 40, :] = grads[part, 2 - 2 * odd, lines, :]


def merge_kernel(sums, grads, spare, got, out):
    tile, _ = my_place()
    odd, half, inside = tile & 1, half_of(tile), far_exists(tile)
    for member in range(16):
        top = pl.multiple_of(half * 128 + member * 8, 8)
        for part in range(3):
            for side in range(2):
                put = part * 16 + side * 8
                other = got[member * PIECE + put : member * PIECE + put + 8, :]
                own = sums[part, pl.ds(top, 8), side * LANES : (side + 1) * LANES]
                out[member, put : put + 8, :] = own + other
        out[member, SPARE:PIECE, :] = spare[...] + got[member * PIECE + SPARE : (member + 1) * PIECE, :]
    for member in range(8):
        lines = slice(member * 40, member * 40 + 40)
        for part in range(2):
            put = PIECE + part * 40
            other = 16 * PIECE + member * 80 + part * 40
            out[8 - 8 * odd + member, put : put + 40, :] = grads[part, 1, lines, :] + got[other : other + 40, :]
            out[8 * odd + member, put : put + 40, :] = jnp.where(
                inside, grads[part, 2 * odd, lines, :], 0.0
            )


def reduce_kernel(pieces, out):
    total = pieces[0, :PIECE, :]
    for member in range(1, 16):
        total = total + pieces[member, :PIECE, :]
    out[...] = total


def probe_kernel(one, two, probe, out):
    tile, group = my_place()
    own_half = half_of(tile)
    for piece, half in enumerate((own_half, 1 - own_half)):
        top = pl.multiple_of(half * 128 + (piece * 8 + group) * 8, 8)
        lines = slice(piece * PIECE, (piece + 1) * PIECE)
        summed = one[lines, :] + two[lines, :]
        mean = jnp.sum(summed[SPARE + 1 : SPARE + 2]) * (1.0 / (WIN * WIN))
        for side in range(2):
            bottom = summed[32 + side * 8 : 40 + side * 8] + 0.25 * mean + 1e-05
            for part in range(2):
                line = part * 16 + side * 8
                old = probe[part, pl.ds(top, 8), side * LANES : (side + 1) * LANES]
                new = old - summed[line : line + 8] / bottom
                for member in range(16):
                    out[member, piece * 32 + line : piece * 32 + line + 8, :] = new


def gather_kernel(mine, other, out):
    ahead = (my_place()[0] & 1) == 1
    for member in range(16):
        x_hi, group = (member >> 1) & 1, (member >> 2) * 2 + (member & 1)
        for piece, half in enumerate((1 - x_hi, x_hi)):
            top = half * 128 + (piece * 8 + group) * 8
            for part in range(2):
                for side in range(2):
                    line = piece * 32 + part * 16 + side * 8
                    out[part, top : top + 8, side * LANES : (side + 1) * LANES] = jnp.where(
                        ahead, mine[member, line : line + 8, :], other[member, line : line + 8, :]
                    )


def shine(light, group, total, at, block):
    row, col = at[0].astype(jnp.int32), at[1].astype(jnp.int32)
    top = 64 + group * 40 - row
    turn = lax.rem(col, LANES)
    lane = lax.broadcasted_iota(jnp.int32, (40, LANES), 1)
    before = pltpu.roll(light[block, pl.ds(top, 40), :], turn, 1)
    after = pltpu.roll(light[block + 1, pl.ds(top, 40), :], turn, 1)
    return total + at[2] * jnp.where(lane < col, before, after)


def prep_kernel(probe, light, peak):
    blank = jnp.zeros((64, LANES), jnp.float32)
    most = jnp.zeros((WIN, LANES), jnp.float32)
    for side in range(2):
        cols = slice(side * LANES, (side + 1) * LANES)
        bright = probe[0, :, cols] * probe[0, :, cols] + probe[1, :, cols] * probe[1, :, cols]
        most = jnp.maximum(most, bright)
        light[1 + side, 64:320, :] = bright
        light[1 + side, 0:64, :] = blank
        light[1 + side, 320:384, :] = blank
        light[3 * side, :, :] = jnp.zeros((384, LANES), jnp.float32)
    peak[...] = jnp.full((8, LANES), jnp.max(most), jnp.float32)


def object_kernel(pieces, old, light, peak, out, at, sem):
    copy = pltpu.make_async_copy(pieces.at[:, SPARE : SPARE + 1, :], at, sem)
    copy.start()
    gradient = pieces[0, PIECE:, :]
    for member in range(1, 16):
        gradient = gradient + pieces[member, PIECE:, :]
    copy.wait()
    tile, group = my_place()
    odd = tile & 1
    mine = 8 - 8 * odd
    total = jnp.zeros((40, LANES), jnp.float32)
    outside = jnp.zeros((40, LANES), jnp.float32)
    for member in range(8):
        for core in range(2):
            block = 1 - core * (1 - odd) + (1 - core) * odd
            seen = [at[mine + member, 0, core * 8 + k] for k in range(3)]
            total = shine(light, group, total, seen, block)
        seen = [at[8 - mine + member, 0, (1 - odd) * 8 + k] for k in range(3)]
        outside = shine(light, group, outside, seen, 2 - 2 * odd)
    total = total + jnp.where(far_exists(tile), outside, 0.0)
    bottom = total + 0.25 * (peak[0:1, :] + 1e-06)
    for part in range(2):
        out[part] = old[part] - gradient[part * 40 : part * 40 + 40, :] / bottom


def my_place():
    return lax.axis_index("tile"), lax.axis_index("group")


def half_of(tile):
    return (tile ^ (tile >> 1)) & 1


def far_exists(tile):
    return jnp.logical_and(tile > 0, tile < TILES - 1)


def swap_cores(value):
    return lax.ppermute(value, "tile", [(i, i ^ 1) for i in range(TILES)])


def swap_z(value, mask):
    pairs = [(tile, tile ^ (4 * mask)) for tile in range(1, TILES, 2)]
    return lax.ppermute(value, "tile", pairs)


def exchange(value):
    groups = []
    for first in range(1, TILES, 2):
        second = (first + 1) % TILES
        groups.append([first * 8 + i for i in range(8)] + [second * 8 + i for i in range(8)])
    return lax.all_to_all(value, ("tile", "group"), 0, 0, axis_index_groups=groups)


def exchange_plane(value):
    groups = []
    for layer in range(TILES // 4):
        for core in range(2):
            groups.append(
                [
                    (layer * 4 + x_hi * 2 + core) * 8 + y * 2 + x_lo
                    for y in range(4)
                    for x_hi in range(2)
                    for x_lo in range(2)
                ]
            )
    return lax.all_to_all(value, ("tile", "group"), 0, 0, axis_index_groups=groups)


def on_chip(value):
    return pltpu.with_memory_space_constraint(value, pltpu.VMEM)


def kernel_call(body, out_shape, in_specs, out_specs, megabytes, **kwargs):
    return pl.pallas_call(
        body,
        out_shape=out_shape,
        in_specs=in_specs,
        out_specs=out_specs,
        compiler_params=pltpu.CompilerParams(vmem_limit_bytes=megabytes << 20),
        name=body.__name__.removesuffix("_kernel"),
        **kwargs,
    )


def local(object_field, probe_field, amplitudes, row_start, column_start, live_slots):
    smem, vmem = pl.BlockSpec(memory_space=SMEM), pl.BlockSpec(memory_space=VMEM)
    row_table, col_table = (on_chip(jnp.asarray(table)) for table in split_tables())
    probe = on_chip(probe_field)

    def buffer(*dims):
        return pltpu.VMEM(dims, jnp.float32)

    own = object_field.reshape(80, LANES)
    stack = exchange(jnp.broadcast_to(own, (16, 80, LANES)))
    light, peak = kernel_call(
        prep_kernel,
        (buffer(4, 384, LANES), buffer(8, LANES)),
        [vmem],
        (vmem,) * 2,
        4,
        cost_estimate=pl.CostEstimate(flops=300000, bytes_accessed=2000000, transcendentals=0),
    )(probe)
    send, sums, grads, spare = kernel_call(
        window_kernel,
        (
            buffer(16 * PIECE + 640, LANES),
            buffer(3, WIN, WIN),
            buffer(2, 3, 320, LANES),
            buffer(8, LANES),
        ),
        [smem] * 3 + [vmem] * 6,
        (vmem,) * 4,
        24,
        scratch_shapes=[buffer(2, 3, 320, LANES)],
    )(
        row_start, column_start, live_slots, on_chip(stack), on_chip(swap_cores(stack)), probe,
        on_chip(amplitudes), row_table, col_table,
    )

    got, light = lax.optimization_barrier((swap_cores(send), light))
    merged = kernel_call(merge_kernel, buffer(16, LINES, LANES), [vmem] * 4, vmem, 4)(
        sums, grads, spare, on_chip(got)
    )
    pieces = exchange(merged)
    total = kernel_call(reduce_kernel, buffer(PIECE, LANES), [vmem], vmem, 4)(on_chip(pieces))
    total = jnp.concatenate([total, swap_cores(total)], axis=0)
    new_object = kernel_call(
        object_kernel,
        jax.ShapeDtypeStruct((2, 40, LANES), jnp.float32),
        [vmem] * 4,
        vmem,
        4,
        scratch_shapes=[pltpu.SMEM((16, 1, LANES), jnp.float32), pltpu.SemaphoreType.DMA],
        cost_estimate=pl.CostEstimate(flops=700000, bytes_accessed=2000000, transcendentals=0),
    )(on_chip(pieces), on_chip(object_field), on_chip(light), peak)
    for mask in (1, 2):
        total = total + swap_z(total, mask)
    got, new_object = lax.optimization_barrier((swap_z(total, 6), new_object))
    piece = kernel_call(probe_kernel, buffer(16, 64, LANES), [vmem] * 3, vmem, 4)(
        on_chip(total), on_chip(got), probe
    )

    mine = exchange_plane(piece)
    new_probe = kernel_call(
        gather_kernel, jax.ShapeDtypeStruct((2, WIN, WIN), jnp.float32), [vmem] * 2, vmem, 4
    )(on_chip(mine), on_chip(swap_cores(mine)))
    return new_object, new_probe


def solution(mesh):
    return jax.shard_map(
        local,
        mesh=mesh,
        in_specs=(
            P(None, "group", "tile"),
            P(),
            P(("tile", "group"), None, None),
            P(("tile", "group")),
            P(("tile", "group")),
            P(("tile", "group")),
        ),
        out_specs=(P(None, "group", "tile"), P()),
        check_vma=False,
    )
```

```python
import jax
import jax.numpy as jnp
import ml_dtypes
import numpy as np
from jax import lax
from jax.experimental import pallas as pl
from jax.experimental.pallas import tpu as pltpu
from jax.sharding import PartitionSpec as P

WIN = 256
LANES = 128
TILES = 32
SPARE = 48
PIECE = 56
LINES = 136
SMEM = pltpu.MemorySpace.SMEM
VMEM = pltpu.MemorySpace.VMEM


def split_tables():
    counter = np.arange(WIN)
    angles = 2.0 * np.pi / WIN * (counter[:, None] * counter[None, :] % WIN)
    cos, sin = np.cos(angles) / np.sqrt(WIN), np.sin(angles) / np.sqrt(WIN)
    both = np.concatenate([cos[:LANES], cos[LANES : LANES + 1], sin[1:LANES]], axis=0)
    order = np.concatenate([counter[: LANES + 1], counter[:LANES:-1]])
    high = both.astype(ml_dtypes.bfloat16)
    low = (both - high.astype(np.float64)).astype(ml_dtypes.bfloat16)
    select = (order[:, None] == counter[None, :]).astype(ml_dtypes.bfloat16)
    rows = np.concatenate([high, low, select], axis=0)
    return rows, np.concatenate([high.T, low.T, select.T], axis=0)


def halves(value):
    high = value.astype(jnp.bfloat16)
    low = (value - high.astype(jnp.float32)).astype(jnp.bfloat16)
    return high, low


def dot(left, right):
    return jnp.dot(left, right, preferred_element_type=jnp.float32)


def product(left, right):
    height = left[0].shape[0]
    tall = dot(jnp.concatenate(left, axis=0), right[0])
    return tall[:height] + tall[height:] + dot(left[0], right[1])


def unfold(cos_real, cos_imag, sin_real, sin_imag, axis):
    zeroth = lax.broadcasted_iota(jnp.int32, cos_real.shape, axis) == 0
    odd_real, odd_imag = jnp.where(zeroth, 0.0, sin_imag), jnp.where(zeroth, 0.0, sin_real)
    low = cos_real + odd_real, cos_imag - odd_imag
    high = (
        jnp.where(zeroth, sin_real, cos_real - odd_real),
        jnp.where(zeroth, sin_imag, cos_imag + odd_imag),
    )
    return tuple(jnp.concatenate(pair, axis=axis) for pair in zip(low, high))


def fold(real, imag, axis):
    if axis == 0:
        (low_r, high_r), (low_i, high_i) = ((v[:LANES], v[LANES:]) for v in (real, imag))
    else:
        (low_r, high_r), (low_i, high_i) = ((v[:, :LANES], v[:, LANES:]) for v in (real, imag))
    zeroth = lax.broadcasted_iota(jnp.int32, low_r.shape, axis) == 0
    even = (low_r + jnp.where(zeroth, 0.0, high_r), low_i + jnp.where(zeroth, 0.0, high_i))
    odd = (jnp.where(zeroth, high_r, high_i - low_i), jnp.where(zeroth, high_i, low_r - high_r))
    return tuple(jnp.concatenate(pair, axis=axis) for pair in zip(even, odd))


def parts(table):
    return table[0:WIN], table[WIN : 2 * WIN]


def forward(real, imag, rows, cols):
    along = product(parts(rows), halves(jnp.concatenate([real, imag], axis=1)))
    real, imag = unfold(
        along[:LANES, :WIN], along[:LANES, WIN:], along[LANES:, :WIN], along[LANES:, WIN:], 0
    )
    across = product(halves(jnp.concatenate([real, imag], axis=0)), parts(cols))
    return unfold(
        across[:WIN, :LANES], across[WIN:, :LANES], across[:WIN, LANES:], across[WIN:, LANES:], 1
    )


def inverse(real, imag, rows, cols):
    real, imag = fold(real, imag, 0)
    along = product(parts(cols), halves(jnp.concatenate([real, imag], axis=1)))
    real, imag = fold(along[:, :WIN], along[:, WIN:], 1)
    across = product(halves(jnp.concatenate([real, imag], axis=0)), parts(rows))
    return across[:WIN], across[WIN:]


def reordered(value, rows, cols):
    taken = dot(rows[2 * WIN :], jnp.concatenate(halves(value), axis=1)).astype(jnp.bfloat16)
    taken = dot(jnp.concatenate([taken[:, :WIN], taken[:, WIN:]], axis=0), cols[2 * WIN :])
    return taken[:WIN] + taken[WIN:]


def own_kernel(stack, out):
    out[...] = stack[pl.ds(8 - 8 * (my_place()[0] & 1), 8)]


def window_kernel(
    row_ref, col_ref, live_ref, stack, near, probe, amps, row_table, col_table,
    send, sums, grads, spare_out, field,
):
    row, col = row_ref[0], col_ref[0]
    live = live_ref[0].astype(jnp.float32)
    tile, _ = my_place()
    odd, half = tile & 1, half_of(tile)
    inside = far_exists(tile)
    for member in range(8):
        lines = slice(member * 40, member * 40 + 40)
        for part in range(2):
            held = slice(part * 40, part * 40 + 40)
            field[part, 1, lines, :] = stack[8 - 8 * odd + member, held, :]
            field[part, 2 * odd, lines, :] = jnp.where(inside, stack[8 * odd + member, held, :], 0.0)
            field[part, 2 - 2 * odd, lines, :] = near[member, held, :]
    lane = lax.broadcasted_iota(jnp.int32, (WIN, LANES), 1)
    back = lax.rem(LANES - col, LANES)
    ahead = lax.rem(col, LANES)
    first = lane < LANES - col

    def cut(part):
        turned = [
            pltpu.roll(field[part, block, pl.ds(row, WIN), :], back, 1) for block in range(3)
        ]
        return jnp.concatenate(
            [jnp.where(first, turned[0], turned[1]), jnp.where(first, turned[1], turned[2])], axis=1
        )

    sample_real, sample_imag = cut(0), cut(1)
    probe_real, probe_imag = probe[0], probe[1]
    exit_real = probe_real * sample_real - probe_imag * sample_imag
    exit_imag = probe_real * sample_imag + probe_imag * sample_real
    rows, cols = row_table[...], col_table[...]
    far_real, far_imag = forward(exit_real, exit_imag, rows, cols)
    power = far_real * far_real + far_imag * far_imag
    factor = 1.0 - reordered(amps[0], rows, cols) * lax.rsqrt(jnp.maximum(power, 0.0625))
    miss_real, miss_imag = inverse(far_real * factor, far_imag * factor, rows, cols)
    miss_real = miss_real * live
    miss_imag = miss_imag * live
    terms = (
        probe_real * miss_real + probe_imag * miss_imag,
        probe_real * miss_imag - probe_imag * miss_real,
    )
    wrapped = lane < col
    zero = jnp.zeros((WIN, LANES), jnp.float32)
    grads[...] = jnp.zeros_like(grads)
    for part in range(2):
        start = pltpu.roll(terms[part][:, :LANES], ahead, 1)
        end = pltpu.roll(terms[part][:, LANES:], ahead, 1)
        grads[part, 0, pl.ds(row, WIN), :] = jnp.where(wrapped, zero, start)
        grads[part, 1, pl.ds(row, WIN), :] = jnp.where(wrapped, start, end)
        grads[part, 2, pl.ds(row, WIN), :] = jnp.where(wrapped, end, zero)
    window_light = live * (sample_real * sample_real + sample_imag * sample_imag)
    sums[0] = sample_real * miss_real + sample_imag * miss_imag
    sums[1] = sample_real * miss_imag - sample_imag * miss_real
    sums[2] = window_light
    total = jnp.zeros((8, LANES), jnp.float32)
    for line in range(0, WIN, 8):
        total = total + window_light[line : line + 8, :LANES] + window_light[line : line + 8, LANES:]
    spare_line = lax.broadcasted_iota(jnp.int32, (8, LANES), 0)
    spare_lane = lax.broadcasted_iota(jnp.int32, (8, LANES), 1)
    first_lane = 8 * odd
    spare = jnp.where(
        spare_line == 1,
        jnp.broadcast_to(jnp.sum(total, axis=0, keepdims=True), (8, LANES)),
        0.0,
    )
    for lane_off, number in enumerate((row.astype(jnp.float32), col.astype(jnp.float32), live)):
        here = jnp.logical_and(spare_line == 0, spare_lane == first_lane + lane_off)
        spare = jnp.where(here, number, spare)
    spare_out[...] = spare
    for member in range(16):
        first_line = member * PIECE
        top = pl.multiple_of((1 - half) * 128 + member * 8, 8)
        for part in range(3):
            for side in range(2):
                put = first_line + part * 16 + side * 8
                send[put : put + 8, :] = sums[part, pl.ds(top, 8), side * LANES : (side + 1) * LANES]
        send[first_line + SPARE : first_line + PIECE, :] = spare
    for member in range(8):
        lines = slice(member * 40, member * 40 + 40)
        for part in range(2):
            put = 16 * PIECE + member * 80 + part * 40
            send[put : put + 40, :] = grads[part, 2 - 2 * odd, lines, :]


def merge_kernel(sums, grads, spare, got, out):
    tile, _ = my_place()
    odd, half, inside = tile & 1, half_of(tile), far_exists(tile)
    for member in range(16):
        top = pl.multiple_of(half * 128 + member * 8, 8)
        for part in range(3):
            for side in range(2):
                put = part * 16 + side * 8
                other = got[member * PIECE + put : member * PIECE + put + 8, :]
                own = sums[part, pl.ds(top, 8), side * LANES : (side + 1) * LANES]
                out[member, put : put + 8, :] = own + other
        out[member, SPARE:PIECE, :] = spare[...] + got[member * PIECE + SPARE : (member + 1) * PIECE, :]
    for member in range(8):
        lines = slice(member * 40, member * 40 + 40)
        for part in range(2):
            put = PIECE + part * 40
            other = 16 * PIECE + member * 80 + part * 40
            out[8 - 8 * odd + member, put : put + 40, :] = grads[part, 1, lines, :] + got[other : other + 40, :]
            out[8 * odd + member, put : put + 40, :] = jnp.where(
                inside, grads[part, 2 * odd, lines, :], 0.0
            )


def reduce_kernel(pieces, out):
    total = pieces[0, :PIECE, :]
    for member in range(1, 16):
        total = total + pieces[member, :PIECE, :]
    out[...] = total


def probe_kernel(one, two, probe, out):
    tile, group = my_place()
    top = pl.multiple_of(half_of(tile) * 128 + (8 - 8 * (tile & 1) + group) * 8, 8)
    summed = one[...] + two[...]
    mean = jnp.sum(summed[SPARE + 1 : SPARE + 2]) * (1.0 / (WIN * WIN))
    for side in range(2):
        bottom = summed[32 + side * 8 : 40 + side * 8] + 0.25 * mean + 1e-05
        for part in range(2):
            lines = part * 16 + side * 8
            old = probe[part, pl.ds(top, 8), side * LANES : (side + 1) * LANES]
            new = old - summed[lines : lines + 8] / bottom
            for member in range(16):
                out[member, lines : lines + 8, :] = new


def gather_kernel(mine, other, out):
    core = my_place()[0] & 1
    for source, which in ((mine, core), (other, 1 - core)):
        for member in range(16):
            x_hi, group = (member >> 1) & 1, (member >> 2) * 2 + (member & 1)
            top = pl.multiple_of((which ^ x_hi) * 128 + (8 - 8 * which + group) * 8, 8)
            for part in range(2):
                for side in range(2):
                    lines = part * 16 + side * 8
                    out[part, pl.ds(top, 8), side * LANES : (side + 1) * LANES] = source[
                        member, lines : lines + 8, :
                    ]


def shine(light, group, total, at, block):
    row, col = at[0].astype(jnp.int32), at[1].astype(jnp.int32)
    top = 64 + group * 40 - row
    turn = lax.rem(col, LANES)
    lane = lax.broadcasted_iota(jnp.int32, (40, LANES), 1)
    before = pltpu.roll(light[block, pl.ds(top, 40), :], turn, 1)
    after = pltpu.roll(light[block + 1, pl.ds(top, 40), :], turn, 1)
    return total + at[2] * jnp.where(lane < col, before, after)


def prep_kernel(probe, light, peak):
    blank = jnp.zeros((64, LANES), jnp.float32)
    most = jnp.zeros((WIN, LANES), jnp.float32)
    for side in range(2):
        cols = slice(side * LANES, (side + 1) * LANES)
        bright = probe[0, :, cols] * probe[0, :, cols] + probe[1, :, cols] * probe[1, :, cols]
        most = jnp.maximum(most, bright)
        light[1 + side, 64:320, :] = bright
        light[1 + side, 0:64, :] = blank
        light[1 + side, 320:384, :] = blank
        light[3 * side, :, :] = jnp.zeros((384, LANES), jnp.float32)
    peak[...] = jnp.full((8, LANES), jnp.max(most), jnp.float32)


def object_kernel(pieces, old, light, peak, out, at, sem):
    copy = pltpu.make_async_copy(pieces.at[:, SPARE : SPARE + 1, :], at, sem)
    copy.start()
    gradient = pieces[0, PIECE:, :]
    for member in range(1, 16):
        gradient = gradient + pieces[member, PIECE:, :]
    copy.wait()
    tile, group = my_place()
    odd = tile & 1
    mine = 8 - 8 * odd
    total = jnp.zeros((40, LANES), jnp.float32)
    outside = jnp.zeros((40, LANES), jnp.float32)
    for member in range(8):
        for core in range(2):
            block = 1 - core * (1 - odd) + (1 - core) * odd
            seen = [at[mine + member, 0, core * 8 + k] for k in range(3)]
            total = shine(light, group, total, seen, block)
        seen = [at[8 - mine + member, 0, (1 - odd) * 8 + k] for k in range(3)]
        outside = shine(light, group, outside, seen, 2 - 2 * odd)
    total = total + jnp.where(far_exists(tile), outside, 0.0)
    bottom = total + 0.25 * (peak[0:1, :] + 1e-06)
    for part in range(2):
        out[part] = old[part] - gradient[part * 40 : part * 40 + 40, :] / bottom


def my_place():
    return lax.axis_index("tile"), lax.axis_index("group")


def half_of(tile):
    return (tile ^ (tile >> 1)) & 1


def far_exists(tile):
    return jnp.logical_and(tile > 0, tile < TILES - 1)


def swap_cores(value):
    return lax.ppermute(value, "tile", [(i, i ^ 1) for i in range(TILES)])


def swap_z(value, mask):
    pairs = []
    for tile in range(TILES):
        layer, rest = divmod(tile, 4)
        ahead = 1 if rest == 0 else 0
        other = (((layer - ahead) % (TILES // 4)) ^ mask) + ahead
        pairs.append((tile, other % (TILES // 4) * 4 + rest))
    return lax.ppermute(value, "tile", pairs)


def exchange(value):
    groups = []
    for first in range(1, TILES, 2):
        second = (first + 1) % TILES
        groups.append([first * 8 + i for i in range(8)] + [second * 8 + i for i in range(8)])
    return lax.all_to_all(value, ("tile", "group"), 0, 0, axis_index_groups=groups)


def exchange_plane(value):
    groups = []
    for layer in range(TILES // 4):
        for core in range(2):
            groups.append(
                [
                    (layer * 4 + x_hi * 2 + core) * 8 + y * 2 + x_lo
                    for y in range(4)
                    for x_hi in range(2)
                    for x_lo in range(2)
                ]
            )
    return lax.all_to_all(value, ("tile", "group"), 0, 0, axis_index_groups=groups)


def on_chip(value):
    return pltpu.with_memory_space_constraint(value, pltpu.VMEM)


def kernel_call(body, out_shape, in_specs, out_specs, megabytes, **kwargs):
    return pl.pallas_call(
        body,
        out_shape=out_shape,
        in_specs=in_specs,
        out_specs=out_specs,
        compiler_params=pltpu.CompilerParams(vmem_limit_bytes=megabytes << 20),
        name=body.__name__.removesuffix("_kernel"),
        **kwargs,
    )


def local(object_field, probe_field, amplitudes, row_start, column_start, live_slots):
    smem, vmem = pl.BlockSpec(memory_space=SMEM), pl.BlockSpec(memory_space=VMEM)
    row_table, col_table = (on_chip(jnp.asarray(table)) for table in split_tables())
    probe = on_chip(probe_field)

    def buffer(*dims):
        return pltpu.VMEM(dims, jnp.float32)

    own = object_field.reshape(80, LANES)
    stack = exchange(jnp.broadcast_to(own, (16, 80, LANES)))
    near = swap_cores(kernel_call(own_kernel, buffer(8, 80, LANES), [vmem], vmem, 4)(on_chip(stack)))
    light, peak = kernel_call(
        prep_kernel,
        (buffer(4, 384, LANES), buffer(8, LANES)),
        [vmem],
        (vmem,) * 2,
        4,
        cost_estimate=pl.CostEstimate(flops=300000, bytes_accessed=2000000, transcendentals=0),
    )(probe)
    send, sums, grads, spare = kernel_call(
        window_kernel,
        (
            buffer(16 * PIECE + 640, LANES),
            buffer(3, WIN, WIN),
            buffer(2, 3, 320, LANES),
            buffer(8, LANES),
        ),
        [smem] * 3 + [vmem] * 6,
        (vmem,) * 4,
        24,
        scratch_shapes=[buffer(2, 3, 320, LANES)],
    )(
        row_start, column_start, live_slots, on_chip(stack), on_chip(near), probe,
        on_chip(amplitudes), row_table, col_table,
    )

    got, light = lax.optimization_barrier((swap_cores(send), light))
    merged = kernel_call(merge_kernel, buffer(16, LINES, LANES), [vmem] * 4, vmem, 4)(
        sums, grads, spare, on_chip(got)
    )
    pieces = exchange(merged)
    total = kernel_call(reduce_kernel, buffer(PIECE, LANES), [vmem], vmem, 4)(on_chip(pieces))
    new_object = kernel_call(
        object_kernel,
        jax.ShapeDtypeStruct((2, 40, LANES), jnp.float32),
        [vmem] * 4,
        vmem,
        4,
        scratch_shapes=[pltpu.SMEM((16, 1, LANES), jnp.float32), pltpu.SemaphoreType.DMA],
        cost_estimate=pl.CostEstimate(flops=700000, bytes_accessed=2000000, transcendentals=0),
    )(on_chip(pieces), on_chip(object_field), on_chip(light), peak)
    for mask in (1, 2):
        total = total + swap_z(total, mask)
    got, new_object = lax.optimization_barrier((swap_z(total, 6), new_object))
    piece = kernel_call(probe_kernel, buffer(16, 32, LANES), [vmem] * 3, vmem, 4)(
        on_chip(total), on_chip(got), probe
    )

    mine = exchange_plane(piece)
    new_probe = kernel_call(
        gather_kernel, jax.ShapeDtypeStruct((2, WIN, WIN), jnp.float32), [vmem] * 2, vmem, 4
    )(on_chip(mine), on_chip(swap_cores(mine)))
    return new_object, new_probe


def solution(mesh):
    return jax.shard_map(
        local,
        mesh=mesh,
        in_specs=(
            P(None, "group", "tile"),
            P(),
            P(("tile", "group"), None, None),
            P(("tile", "group")),
            P(("tile", "group")),
            P(("tile", "group")),
        ),
        out_specs=(P(None, "group", "tile"), P()),
        check_vma=False,
    )
```

```python
import jax
import jax.numpy as jnp
import ml_dtypes
import numpy as np
from jax import lax
from jax.experimental import pallas as pl
from jax.experimental.pallas import tpu as pltpu
from jax.sharding import PartitionSpec as P

WIN = 256
LANES = 128
TILES = 32
SPARE = 48
PIECE = 56
LINES = 136
SMEM = pltpu.MemorySpace.SMEM
VMEM = pltpu.MemorySpace.VMEM


def split_tables():
    counter = np.arange(WIN)
    angles = 2.0 * np.pi / WIN * (counter[:, None] * counter[None, :] % WIN)
    cos, sin = np.cos(angles) / np.sqrt(WIN), np.sin(angles) / np.sqrt(WIN)
    both = np.concatenate([cos[:LANES], cos[LANES : LANES + 1], sin[1:LANES]], axis=0)
    order = np.concatenate([counter[: LANES + 1], counter[:LANES:-1]])
    high = both.astype(ml_dtypes.bfloat16)
    low = (both - high.astype(np.float64)).astype(ml_dtypes.bfloat16)
    select = (order[:, None] == counter[None, :]).astype(ml_dtypes.bfloat16)
    rows = np.concatenate([high, low, select], axis=0)
    return rows, np.concatenate([high.T, low.T, select.T], axis=0)


def halves(value):
    high = value.astype(jnp.bfloat16)
    low = (value - high.astype(jnp.float32)).astype(jnp.bfloat16)
    return high, low


def dot(left, right):
    return jnp.dot(left, right, preferred_element_type=jnp.float32)


def product(left, right):
    height = left[0].shape[0]
    tall = dot(jnp.concatenate(left, axis=0), right[0])
    return tall[:height] + tall[height:] + dot(left[0], right[1])


def unfold(cos_real, cos_imag, sin_real, sin_imag, axis):
    zeroth = lax.broadcasted_iota(jnp.int32, cos_real.shape, axis) == 0
    odd_real, odd_imag = jnp.where(zeroth, 0.0, sin_imag), jnp.where(zeroth, 0.0, sin_real)
    low = cos_real + odd_real, cos_imag - odd_imag
    high = (
        jnp.where(zeroth, sin_real, cos_real - odd_real),
        jnp.where(zeroth, sin_imag, cos_imag + odd_imag),
    )
    return tuple(jnp.concatenate(pair, axis=axis) for pair in zip(low, high))


def fold(real, imag, axis):
    if axis == 0:
        (low_r, high_r), (low_i, high_i) = ((v[:LANES], v[LANES:]) for v in (real, imag))
    else:
        (low_r, high_r), (low_i, high_i) = ((v[:, :LANES], v[:, LANES:]) for v in (real, imag))
    zeroth = lax.broadcasted_iota(jnp.int32, low_r.shape, axis) == 0
    even = (low_r + jnp.where(zeroth, 0.0, high_r), low_i + jnp.where(zeroth, 0.0, high_i))
    odd = (jnp.where(zeroth, high_r, high_i - low_i), jnp.where(zeroth, high_i, low_r - high_r))
    return tuple(jnp.concatenate(pair, axis=axis) for pair in zip(even, odd))


def parts(table):
    return table[0:WIN], table[WIN : 2 * WIN]


def forward(real, imag, rows, cols):
    along = product(parts(rows), halves(jnp.concatenate([real, imag], axis=1)))
    real, imag = unfold(
        along[:LANES, :WIN], along[:LANES, WIN:], along[LANES:, :WIN], along[LANES:, WIN:], 0
    )
    across = product(halves(jnp.concatenate([real, imag], axis=0)), parts(cols))
    return unfold(
        across[:WIN, :LANES], across[WIN:, :LANES], across[:WIN, LANES:], across[WIN:, LANES:], 1
    )


def inverse(real, imag, rows, cols):
    real, imag = fold(real, imag, 0)
    along = product(parts(cols), halves(jnp.concatenate([real, imag], axis=1)))
    real, imag = fold(along[:, :WIN], along[:, WIN:], 1)
    across = product(halves(jnp.concatenate([real, imag], axis=0)), parts(rows))
    return across[:WIN], across[WIN:]


def reordered(value, rows, cols):
    taken = dot(rows[2 * WIN :], jnp.concatenate(halves(value), axis=1)).astype(jnp.bfloat16)
    taken = dot(jnp.concatenate([taken[:, :WIN], taken[:, WIN:]], axis=0), cols[2 * WIN :])
    return taken[:WIN] + taken[WIN:]


def window_kernel(
    row_ref, col_ref, live_ref, stack, near, probe, amps, row_table, col_table,
    send, sums, grads, spare_out, field,
):
    row, col = row_ref[0], col_ref[0]
    live = live_ref[0].astype(jnp.float32)
    tile, _ = my_place()
    odd, half = tile & 1, half_of(tile)
    inside = far_exists(tile)
    for member in range(8):
        lines = slice(member * 40, member * 40 + 40)
        for part in range(2):
            held = slice(part * 40, part * 40 + 40)
            field[part, 1, lines, :] = stack[8 - 8 * odd + member, held, :]
            field[part, 2 * odd, lines, :] = jnp.where(inside, stack[8 * odd + member, held, :], 0.0)
            field[part, 2 - 2 * odd, lines, :] = near[8 * odd + member, held, :]
    lane = lax.broadcasted_iota(jnp.int32, (WIN, LANES), 1)
    back = lax.rem(LANES - col, LANES)
    ahead = lax.rem(col, LANES)
    first = lane < LANES - col

    def cut(part):
        turned = [
            pltpu.roll(field[part, block, pl.ds(row, WIN), :], back, 1) for block in range(3)
        ]
        return jnp.concatenate(
            [jnp.where(first, turned[0], turned[1]), jnp.where(first, turned[1], turned[2])], axis=1
        )

    sample_real, sample_imag = cut(0), cut(1)
    probe_real, probe_imag = probe[0], probe[1]
    exit_real = probe_real * sample_real - probe_imag * sample_imag
    exit_imag = probe_real * sample_imag + probe_imag * sample_real
    rows, cols = row_table[...], col_table[...]
    far_real, far_imag = forward(exit_real, exit_imag, rows, cols)
    power = far_real * far_real + far_imag * far_imag
    factor = 1.0 - reordered(amps[0], rows, cols) * lax.rsqrt(jnp.maximum(power, 0.0625))
    miss_real, miss_imag = inverse(far_real * factor, far_imag * factor, rows, cols)
    miss_real = miss_real * live
    miss_imag = miss_imag * live
    terms = (
        probe_real * miss_real + probe_imag * miss_imag,
        probe_real * miss_imag - probe_imag * miss_real,
    )
    wrapped = lane < col
    zero = jnp.zeros((WIN, LANES), jnp.float32)
    grads[...] = jnp.zeros_like(grads)
    for part in range(2):
        start = pltpu.roll(terms[part][:, :LANES], ahead, 1)
        end = pltpu.roll(terms[part][:, LANES:], ahead, 1)
        grads[part, 0, pl.ds(row, WIN), :] = jnp.where(wrapped, zero, start)
        grads[part, 1, pl.ds(row, WIN), :] = jnp.where(wrapped, start, end)
        grads[part, 2, pl.ds(row, WIN), :] = jnp.where(wrapped, end, zero)
    window_light = live * (sample_real * sample_real + sample_imag * sample_imag)
    sums[0] = sample_real * miss_real + sample_imag * miss_imag
    sums[1] = sample_real * miss_imag - sample_imag * miss_real
    sums[2] = window_light
    total = jnp.zeros((8, LANES), jnp.float32)
    for line in range(0, WIN, 8):
        total = total + window_light[line : line + 8, :LANES] + window_light[line : line + 8, LANES:]
    spare_line = lax.broadcasted_iota(jnp.int32, (8, LANES), 0)
    spare_lane = lax.broadcasted_iota(jnp.int32, (8, LANES), 1)
    first_lane = 8 * odd
    spare = jnp.where(
        spare_line == 1,
        jnp.broadcast_to(jnp.sum(total, axis=0, keepdims=True), (8, LANES)),
        0.0,
    )
    for lane_off, number in enumerate((row.astype(jnp.float32), col.astype(jnp.float32), live)):
        here = jnp.logical_and(spare_line == 0, spare_lane == first_lane + lane_off)
        spare = jnp.where(here, number, spare)
    spare_out[...] = spare
    for member in range(16):
        first_line = member * PIECE
        top = pl.multiple_of((1 - half) * 128 + member * 8, 8)
        for part in range(3):
            for side in range(2):
                put = first_line + part * 16 + side * 8
                send[put : put + 8, :] = sums[part, pl.ds(top, 8), side * LANES : (side + 1) * LANES]
        send[first_line + SPARE : first_line + PIECE, :] = spare
    for member in range(8):
        lines = slice(member * 40, member * 40 + 40)
        for part in range(2):
            put = 16 * PIECE + member * 80 + part * 40
            send[put : put + 40, :] = grads[part, 2 - 2 * odd, lines, :]


def merge_kernel(sums, grads, spare, got, out):
    tile, _ = my_place()
    odd, half, inside = tile & 1, half_of(tile), far_exists(tile)
    for member in range(16):
        top = pl.multiple_of(half * 128 + member * 8, 8)
        for part in range(3):
            for side in range(2):
                put = part * 16 + side * 8
                other = got[member * PIECE + put : member * PIECE + put + 8, :]
                own = sums[part, pl.ds(top, 8), side * LANES : (side + 1) * LANES]
                out[member, put : put + 8, :] = own + other
        out[member, SPARE:PIECE, :] = spare[...] + got[member * PIECE + SPARE : (member + 1) * PIECE, :]
    for member in range(8):
        lines = slice(member * 40, member * 40 + 40)
        for part in range(2):
            put = PIECE + part * 40
            other = 16 * PIECE + member * 80 + part * 40
            out[8 - 8 * odd + member, put : put + 40, :] = grads[part, 1, lines, :] + got[other : other + 40, :]
            out[8 * odd + member, put : put + 40, :] = jnp.where(
                inside, grads[part, 2 * odd, lines, :], 0.0
            )


def reduce_kernel(pieces, out):
    total = pieces[0, :PIECE, :]
    for member in range(1, 16):
        total = total + pieces[member, :PIECE, :]
    out[...] = total


def probe_kernel(one, two, probe, out):
    tile, group = my_place()
    top = pl.multiple_of(half_of(tile) * 128 + (8 - 8 * (tile & 1) + group) * 8, 8)
    summed = one[...] + two[...]
    mean = jnp.sum(summed[SPARE + 1 : SPARE + 2]) * (1.0 / (WIN * WIN))
    for side in range(2):
        bottom = summed[32 + side * 8 : 40 + side * 8] + 0.25 * mean + 1e-05
        for part in range(2):
            lines = part * 16 + side * 8
            old = probe[part, pl.ds(top, 8), side * LANES : (side + 1) * LANES]
            new = old - summed[lines : lines + 8] / bottom
            for member in range(16):
                out[member, lines : lines + 8, :] = new


def gather_kernel(mine, other, out):
    core = my_place()[0] & 1
    for source, which in ((mine, core), (other, 1 - core)):
        for member in range(16):
            x_hi, group = (member >> 1) & 1, (member >> 2) * 2 + (member & 1)
            top = pl.multiple_of((which ^ x_hi) * 128 + (8 - 8 * which + group) * 8, 8)
            for part in range(2):
                for side in range(2):
                    lines = part * 16 + side * 8
                    out[part, pl.ds(top, 8), side * LANES : (side + 1) * LANES] = source[
                        member, lines : lines + 8, :
                    ]


def shine(light, group, total, at, block):
    row, col = at[0].astype(jnp.int32), at[1].astype(jnp.int32)
    top = 64 + group * 40 - row
    turn = lax.rem(col, LANES)
    lane = lax.broadcasted_iota(jnp.int32, (40, LANES), 1)
    before = pltpu.roll(light[block, pl.ds(top, 40), :], turn, 1)
    after = pltpu.roll(light[block + 1, pl.ds(top, 40), :], turn, 1)
    return total + at[2] * jnp.where(lane < col, before, after)


def prep_kernel(probe, light, peak):
    blank = jnp.zeros((64, LANES), jnp.float32)
    most = jnp.zeros((WIN, LANES), jnp.float32)
    for side in range(2):
        cols = slice(side * LANES, (side + 1) * LANES)
        bright = probe[0, :, cols] * probe[0, :, cols] + probe[1, :, cols] * probe[1, :, cols]
        most = jnp.maximum(most, bright)
        light[1 + side, 64:320, :] = bright
        light[1 + side, 0:64, :] = blank
        light[1 + side, 320:384, :] = blank
        light[3 * side, :, :] = jnp.zeros((384, LANES), jnp.float32)
    peak[...] = jnp.full((8, LANES), jnp.max(most), jnp.float32)


def object_kernel(pieces, old, light, peak, out, at, sem):
    copy = pltpu.make_async_copy(pieces.at[:, SPARE : SPARE + 1, :], at, sem)
    copy.start()
    gradient = pieces[0, PIECE:, :]
    for member in range(1, 16):
        gradient = gradient + pieces[member, PIECE:, :]
    copy.wait()
    tile, group = my_place()
    odd = tile & 1
    mine = 8 - 8 * odd
    total = jnp.zeros((40, LANES), jnp.float32)
    outside = jnp.zeros((40, LANES), jnp.float32)
    for member in range(8):
        for core in range(2):
            block = 1 - core * (1 - odd) + (1 - core) * odd
            seen = [at[mine + member, 0, core * 8 + k] for k in range(3)]
            total = shine(light, group, total, seen, block)
        seen = [at[8 - mine + member, 0, (1 - odd) * 8 + k] for k in range(3)]
        outside = shine(light, group, outside, seen, 2 - 2 * odd)
    total = total + jnp.where(far_exists(tile), outside, 0.0)
    bottom = total + 0.25 * (peak[0:1, :] + 1e-06)
    for part in range(2):
        out[part] = old[part] - gradient[part * 40 : part * 40 + 40, :] / bottom


def my_place():
    return lax.axis_index("tile"), lax.axis_index("group")


def half_of(tile):
    return (tile ^ (tile >> 1)) & 1


def far_exists(tile):
    return jnp.logical_and(tile > 0, tile < TILES - 1)


def swap_cores(value):
    return lax.ppermute(value, "tile", [(i, i ^ 1) for i in range(TILES)])


def swap_z(value, mask):
    pairs = []
    for tile in range(TILES):
        layer, rest = divmod(tile, 4)
        ahead = 1 if rest == 0 else 0
        other = (((layer - ahead) % (TILES // 4)) ^ mask) + ahead
        pairs.append((tile, other % (TILES // 4) * 4 + rest))
    return lax.ppermute(value, "tile", pairs)


def exchange(value):
    groups = []
    for first in range(1, TILES, 2):
        second = (first + 1) % TILES
        groups.append([first * 8 + i for i in range(8)] + [second * 8 + i for i in range(8)])
    return lax.all_to_all(value, ("tile", "group"), 0, 0, axis_index_groups=groups)


def exchange_plane(value):
    groups = []
    for layer in range(TILES // 4):
        for core in range(2):
            groups.append(
                [
                    (layer * 4 + x_hi * 2 + core) * 8 + y * 2 + x_lo
                    for y in range(4)
                    for x_hi in range(2)
                    for x_lo in range(2)
                ]
            )
    return lax.all_to_all(value, ("tile", "group"), 0, 0, axis_index_groups=groups)


def on_chip(value):
    return pltpu.with_memory_space_constraint(value, pltpu.VMEM)


def kernel_call(body, out_shape, in_specs, out_specs, megabytes, **kwargs):
    return pl.pallas_call(
        body,
        out_shape=out_shape,
        in_specs=in_specs,
        out_specs=out_specs,
        compiler_params=pltpu.CompilerParams(vmem_limit_bytes=megabytes << 20),
        name=body.__name__.removesuffix("_kernel"),
        **kwargs,
    )


def local(object_field, probe_field, amplitudes, row_start, column_start, live_slots):
    smem, vmem = pl.BlockSpec(memory_space=SMEM), pl.BlockSpec(memory_space=VMEM)
    row_table, col_table = (on_chip(jnp.asarray(table)) for table in split_tables())
    probe = on_chip(probe_field)

    def buffer(*dims):
        return pltpu.VMEM(dims, jnp.float32)

    own = object_field.reshape(80, LANES)
    stack = exchange(jnp.broadcast_to(own, (16, 80, LANES)))
    light, peak = kernel_call(
        prep_kernel,
        (buffer(4, 384, LANES), buffer(8, LANES)),
        [vmem],
        (vmem,) * 2,
        4,
        cost_estimate=pl.CostEstimate(flops=300000, bytes_accessed=2000000, transcendentals=0),
    )(probe)
    send, sums, grads, spare = kernel_call(
        window_kernel,
        (
            buffer(16 * PIECE + 640, LANES),
            buffer(3, WIN, WIN),
            buffer(2, 3, 320, LANES),
            buffer(8, LANES),
        ),
        [smem] * 3 + [vmem] * 6,
        (vmem,) * 4,
        24,
        scratch_shapes=[buffer(2, 3, 320, LANES)],
    )(
        row_start, column_start, live_slots, on_chip(stack), on_chip(swap_cores(stack)), probe,
        on_chip(amplitudes), row_table, col_table,
    )

    got, light = lax.optimization_barrier((swap_cores(send), light))
    merged = kernel_call(merge_kernel, buffer(16, LINES, LANES), [vmem] * 4, vmem, 4)(
        sums, grads, spare, on_chip(got)
    )
    pieces = exchange(merged)
    total = kernel_call(reduce_kernel, buffer(PIECE, LANES), [vmem], vmem, 4)(on_chip(pieces))
    new_object = kernel_call(
        object_kernel,
        jax.ShapeDtypeStruct((2, 40, LANES), jnp.float32),
        [vmem] * 4,
        vmem,
        4,
        scratch_shapes=[pltpu.SMEM((16, 1, LANES), jnp.float32), pltpu.SemaphoreType.DMA],
        cost_estimate=pl.CostEstimate(flops=700000, bytes_accessed=2000000, transcendentals=0),
    )(on_chip(pieces), on_chip(object_field), on_chip(light), peak)
    for mask in (1, 2):
        total = total + swap_z(total, mask)
    got, new_object = lax.optimization_barrier((swap_z(total, 6), new_object))
    piece = kernel_call(probe_kernel, buffer(16, 32, LANES), [vmem] * 3, vmem, 4)(
        on_chip(total), on_chip(got), probe
    )

    mine = exchange_plane(piece)
    new_probe = kernel_call(
        gather_kernel, jax.ShapeDtypeStruct((2, WIN, WIN), jnp.float32), [vmem] * 2, vmem, 4
    )(on_chip(mine), on_chip(swap_cores(mine)))
    return new_object, new_probe


def solution(mesh):
    return jax.shard_map(
        local,
        mesh=mesh,
        in_specs=(
            P(None, "group", "tile"),
            P(),
            P(("tile", "group"), None, None),
            P(("tile", "group")),
            P(("tile", "group")),
            P(("tile", "group")),
        ),
        out_specs=(P(None, "group", "tile"), P()),
        check_vma=False,
    )
```

```python
import jax
import jax.numpy as jnp
import ml_dtypes
import numpy as np
from jax import lax
from jax.experimental import pallas as pl
from jax.experimental.pallas import tpu as pltpu
from jax.sharding import PartitionSpec as P

WIN = 256
LANES = 128
TILES = 32
SPARE = 48
PIECE = 56
LINES = 136
SMEM = pltpu.MemorySpace.SMEM
VMEM = pltpu.MemorySpace.VMEM


def split_tables():
    counter = np.arange(WIN)
    angles = 2.0 * np.pi / WIN * (counter[:, None] * counter[None, :] % WIN)
    cos, sin = np.cos(angles) / np.sqrt(WIN), np.sin(angles) / np.sqrt(WIN)
    both = np.concatenate([cos[:LANES], cos[LANES : LANES + 1], sin[1:LANES]], axis=0)
    order = np.concatenate([counter[: LANES + 1], counter[:LANES:-1]])
    high = both.astype(ml_dtypes.bfloat16)
    low = (both - high.astype(np.float64)).astype(ml_dtypes.bfloat16)
    select = (order[:, None] == counter[None, :]).astype(ml_dtypes.bfloat16)
    rows = np.concatenate([high, low, select], axis=0)
    return rows, np.concatenate([high.T, low.T, select.T], axis=0)


def halves(value):
    high = value.astype(jnp.bfloat16)
    low = (value - high.astype(jnp.float32)).astype(jnp.bfloat16)
    return high, low


def dot(left, right):
    return jnp.dot(left, right, preferred_element_type=jnp.float32)


def product(left, right):
    height = left[0].shape[0]
    tall = dot(jnp.concatenate(left, axis=0), right[0])
    return tall[:height] + tall[height:] + dot(left[0], right[1])


def unfold(cos_real, cos_imag, sin_real, sin_imag, axis):
    zeroth = lax.broadcasted_iota(jnp.int32, cos_real.shape, axis) == 0
    odd_real, odd_imag = jnp.where(zeroth, 0.0, sin_imag), jnp.where(zeroth, 0.0, sin_real)
    low = cos_real + odd_real, cos_imag - odd_imag
    high = (
        jnp.where(zeroth, sin_real, cos_real - odd_real),
        jnp.where(zeroth, sin_imag, cos_imag + odd_imag),
    )
    return tuple(jnp.concatenate(pair, axis=axis) for pair in zip(low, high))


def fold(real, imag, axis):
    if axis == 0:
        (low_r, high_r), (low_i, high_i) = ((v[:LANES], v[LANES:]) for v in (real, imag))
    else:
        (low_r, high_r), (low_i, high_i) = ((v[:, :LANES], v[:, LANES:]) for v in (real, imag))
    zeroth = lax.broadcasted_iota(jnp.int32, low_r.shape, axis) == 0
    even = (low_r + jnp.where(zeroth, 0.0, high_r), low_i + jnp.where(zeroth, 0.0, high_i))
    odd = (jnp.where(zeroth, high_r, high_i - low_i), jnp.where(zeroth, high_i, low_r - high_r))
    return tuple(jnp.concatenate(pair, axis=axis) for pair in zip(even, odd))


def parts(table):
    return table[0:WIN], table[WIN : 2 * WIN]


def forward(real, imag, rows, cols):
    along = product(parts(rows), halves(jnp.concatenate([real, imag], axis=1)))
    real, imag = unfold(
        along[:LANES, :WIN], along[:LANES, WIN:], along[LANES:, :WIN], along[LANES:, WIN:], 0
    )
    across = product(halves(jnp.concatenate([real, imag], axis=0)), parts(cols))
    return unfold(
        across[:WIN, :LANES], across[WIN:, :LANES], across[:WIN, LANES:], across[WIN:, LANES:], 1
    )


def inverse(real, imag, rows, cols):
    real, imag = fold(real, imag, 0)
    along = product(parts(cols), halves(jnp.concatenate([real, imag], axis=1)))
    real, imag = fold(along[:, :WIN], along[:, WIN:], 1)
    across = product(halves(jnp.concatenate([real, imag], axis=0)), parts(rows))
    return across[:WIN], across[WIN:]


def reordered(value, rows, cols):
    taken = dot(rows[2 * WIN :], jnp.concatenate(halves(value), axis=1)).astype(jnp.bfloat16)
    taken = dot(jnp.concatenate([taken[:, :WIN], taken[:, WIN:]], axis=0), cols[2 * WIN :])
    return taken[:WIN] + taken[WIN:]


def window_kernel(
    row_ref, col_ref, live_ref, stack, near, probe, amps, row_table, col_table,
    send, sums, grads, spare_out, field,
):
    row, col = row_ref[0], col_ref[0]
    live = live_ref[0].astype(jnp.float32)
    tile, _ = my_place()
    odd, half = tile & 1, half_of(tile)
    inside = far_exists(tile)
    for member in range(8):
        lines = slice(member * 40, member * 40 + 40)
        for part in range(2):
            held = slice(part * 40, part * 40 + 40)
            field[part, 1, lines, :] = stack[8 - 8 * odd + member, held, :]
            field[part, 2 * odd, lines, :] = jnp.where(inside, stack[8 * odd + member, held, :], 0.0)
            field[part, 2 - 2 * odd, lines, :] = near[8 * odd + member, held, :]
    lane = lax.broadcasted_iota(jnp.int32, (WIN, LANES), 1)
    back = lax.rem(LANES - col, LANES)
    ahead = lax.rem(col, LANES)
    first = lane < LANES - col

    def cut(part):
        turned = [
            pltpu.roll(field[part, block, pl.ds(row, WIN), :], back, 1) for block in range(3)
        ]
        return jnp.concatenate(
            [jnp.where(first, turned[0], turned[1]), jnp.where(first, turned[1], turned[2])], axis=1
        )

    sample_real, sample_imag = cut(0), cut(1)
    probe_real, probe_imag = probe[0], probe[1]
    exit_real = probe_real * sample_real - probe_imag * sample_imag
    exit_imag = probe_real * sample_imag + probe_imag * sample_real
    rows, cols = row_table[...], col_table[...]
    far_real, far_imag = forward(exit_real, exit_imag, rows, cols)
    power = far_real * far_real + far_imag * far_imag
    factor = 1.0 - reordered(amps[0], rows, cols) * lax.rsqrt(jnp.maximum(power, 0.0625))
    miss_real, miss_imag = inverse(far_real * factor, far_imag * factor, rows, cols)
    miss_real = miss_real * live
    miss_imag = miss_imag * live
    terms = (
        probe_real * miss_real + probe_imag * miss_imag,
        probe_real * miss_imag - probe_imag * miss_real,
    )
    wrapped = lane < col
    zero = jnp.zeros((WIN, LANES), jnp.float32)
    grads[...] = jnp.zeros_like(grads)
    for part in range(2):
        start = pltpu.roll(terms[part][:, :LANES], ahead, 1)
        end = pltpu.roll(terms[part][:, LANES:], ahead, 1)
        grads[part, 0, pl.ds(row, WIN), :] = jnp.where(wrapped, zero, start)
        grads[part, 1, pl.ds(row, WIN), :] = jnp.where(wrapped, start, end)
        grads[part, 2, pl.ds(row, WIN), :] = jnp.where(wrapped, end, zero)
    window_light = live * (sample_real * sample_real + sample_imag * sample_imag)
    sums[0] = sample_real * miss_real + sample_imag * miss_imag
    sums[1] = sample_real * miss_imag - sample_imag * miss_real
    sums[2] = window_light
    total = jnp.zeros((8, LANES), jnp.float32)
    for line in range(0, WIN, 8):
        total = total + window_light[line : line + 8, :LANES] + window_light[line : line + 8, LANES:]
    spare_line = lax.broadcasted_iota(jnp.int32, (8, LANES), 0)
    spare_lane = lax.broadcasted_iota(jnp.int32, (8, LANES), 1)
    first_lane = 8 * odd
    spare = jnp.where(
        spare_line == 1,
        jnp.broadcast_to(jnp.sum(total, axis=0, keepdims=True), (8, LANES)),
        0.0,
    )
    for lane_off, number in enumerate((row.astype(jnp.float32), col.astype(jnp.float32), live)):
        here = jnp.logical_and(spare_line == 0, spare_lane == first_lane + lane_off)
        spare = jnp.where(here, number, spare)
    spare_out[...] = spare
    for member in range(16):
        first_line = member * PIECE
        top = pl.multiple_of((1 - half) * 128 + member * 8, 8)
        for part in range(3):
            for side in range(2):
                put = first_line + part * 16 + side * 8
                send[put : put + 8, :] = sums[part, pl.ds(top, 8), side * LANES : (side + 1) * LANES]
        send[first_line + SPARE : first_line + PIECE, :] = spare
    for member in range(8):
        lines = slice(member * 40, member * 40 + 40)
        for part in range(2):
            put = 16 * PIECE + member * 80 + part * 40
            send[put : put + 40, :] = grads[part, 2 - 2 * odd, lines, :]


def merge_kernel(sums, grads, spare, got, out):
    tile, _ = my_place()
    odd, half, inside = tile & 1, half_of(tile), far_exists(tile)
    for member in range(16):
        top = pl.multiple_of(half * 128 + member * 8, 8)
        for part in range(3):
            for side in range(2):
                put = part * 16 + side * 8
                other = got[member * PIECE + put : member * PIECE + put + 8, :]
                own = sums[part, pl.ds(top, 8), side * LANES : (side + 1) * LANES]
                out[member, put : put + 8, :] = own + other
        out[member, SPARE:PIECE, :] = spare[...] + got[member * PIECE + SPARE : (member + 1) * PIECE, :]
    for member in range(8):
        lines = slice(member * 40, member * 40 + 40)
        for part in range(2):
            put = PIECE + part * 40
            other = 16 * PIECE + member * 80 + part * 40
            out[8 - 8 * odd + member, put : put + 40, :] = grads[part, 1, lines, :] + got[other : other + 40, :]
            out[8 * odd + member, put : put + 40, :] = jnp.where(
                inside, grads[part, 2 * odd, lines, :], 0.0
            )


def reduce_kernel(pieces, out):
    total = pieces[0, :PIECE, :]
    for member in range(1, 16):
        total = total + pieces[member, :PIECE, :]
    out[...] = total


def probe_kernel(one, two, probe, out):
    tile, group = my_place()
    top = pl.multiple_of(half_of(tile) * 128 + (8 - 8 * (tile & 1) + group) * 8, 8)
    summed = one[...] + two[...]
    mean = jnp.sum(summed[SPARE + 1 : SPARE + 2]) * (1.0 / (WIN * WIN))
    for side in range(2):
        bottom = summed[32 + side * 8 : 40 + side * 8] + 0.25 * mean + 1e-05
        for part in range(2):
            lines = part * 16 + side * 8
            old = probe[part, pl.ds(top, 8), side * LANES : (side + 1) * LANES]
            new = old - summed[lines : lines + 8] / bottom
            for member in range(16):
                out[member, lines : lines + 8, :] = new


def gather_kernel(mine, other, out):
    core = my_place()[0] & 1
    for source, which in ((mine, core), (other, 1 - core)):
        for member in range(16):
            x_hi, group = (member >> 1) & 1, (member >> 2) * 2 + (member & 1)
            top = pl.multiple_of((which ^ x_hi) * 128 + (8 - 8 * which + group) * 8, 8)
            for part in range(2):
                for side in range(2):
                    lines = part * 16 + side * 8
                    out[part, pl.ds(top, 8), side * LANES : (side + 1) * LANES] = source[
                        member, lines : lines + 8, :
                    ]


def shine(light, group, total, at, block):
    row, col = at[0].astype(jnp.int32), at[1].astype(jnp.int32)
    top = 64 + group * 40 - row
    turn = lax.rem(col, LANES)
    lane = lax.broadcasted_iota(jnp.int32, (40, LANES), 1)
    before = pltpu.roll(light[block, pl.ds(top, 40), :], turn, 1)
    after = pltpu.roll(light[block + 1, pl.ds(top, 40), :], turn, 1)
    return total + at[2] * jnp.where(lane < col, before, after)


def prep_kernel(probe, light, peak):
    blank = jnp.zeros((64, LANES), jnp.float32)
    most = jnp.zeros((WIN, LANES), jnp.float32)
    for side in range(2):
        cols = slice(side * LANES, (side + 1) * LANES)
        bright = probe[0, :, cols] * probe[0, :, cols] + probe[1, :, cols] * probe[1, :, cols]
        most = jnp.maximum(most, bright)
        light[1 + side, 64:320, :] = bright
        light[1 + side, 0:64, :] = blank
        light[1 + side, 320:384, :] = blank
        light[3 * side, :, :] = jnp.zeros((384, LANES), jnp.float32)
    peak[...] = jnp.full((8, LANES), jnp.max(most), jnp.float32)


def object_kernel(pieces, old, light, peak, out, at, sem):
    copy = pltpu.make_async_copy(pieces.at[:, SPARE : SPARE + 1, :], at, sem)
    copy.start()
    gradient = pieces[0, PIECE:, :]
    for member in range(1, 16):
        gradient = gradient + pieces[member, PIECE:, :]
    copy.wait()
    tile, group = my_place()
    odd = tile & 1
    mine = 8 - 8 * odd
    total = jnp.zeros((40, LANES), jnp.float32)
    outside = jnp.zeros((40, LANES), jnp.float32)
    for member in range(8):
        for core in range(2):
            block = 1 - core * (1 - odd) + (1 - core) * odd
            seen = [at[mine + member, 0, core * 8 + k] for k in range(3)]
            total = shine(light, group, total, seen, block)
        seen = [at[8 - mine + member, 0, (1 - odd) * 8 + k] for k in range(3)]
        outside = shine(light, group, outside, seen, 2 - 2 * odd)
    total = total + jnp.where(far_exists(tile), outside, 0.0)
    bottom = total + 0.25 * (peak[0:1, :] + 1e-06)
    for part in range(2):
        out[part] = old[part] - gradient[part * 40 : part * 40 + 40, :] / bottom


def my_place():
    return lax.axis_index("tile"), lax.axis_index("group")


def half_of(tile):
    return (tile ^ (tile >> 1)) & 1


def far_exists(tile):
    return jnp.logical_and(tile > 0, tile < TILES - 1)


def swap_cores(value):
    return lax.ppermute(value, "tile", [(i, i ^ 1) for i in range(TILES)])


def swap_z(value, mask):
    return lax.ppermute(value, "tile", [(tile, tile ^ (4 * mask)) for tile in range(TILES)])


def exchange(value):
    groups = []
    for first in range(1, TILES, 2):
        second = (first + 1) % TILES
        groups.append([first * 8 + i for i in range(8)] + [second * 8 + i for i in range(8)])
    return lax.all_to_all(value, ("tile", "group"), 0, 0, axis_index_groups=groups)


def exchange_plane(value):
    groups = []
    for layer in range(TILES // 4):
        for core in range(2):
            groups.append(
                [
                    (layer * 4 + x_hi * 2 + core) * 8 + y * 2 + x_lo
                    for y in range(4)
                    for x_hi in range(2)
                    for x_lo in range(2)
                ]
            )
    return lax.all_to_all(value, ("tile", "group"), 0, 0, axis_index_groups=groups)


def on_chip(value):
    return pltpu.with_memory_space_constraint(value, pltpu.VMEM)


def kernel_call(body, out_shape, in_specs, out_specs, megabytes, **kwargs):
    return pl.pallas_call(
        body,
        out_shape=out_shape,
        in_specs=in_specs,
        out_specs=out_specs,
        compiler_params=pltpu.CompilerParams(vmem_limit_bytes=megabytes << 20),
        name=body.__name__.removesuffix("_kernel"),
        **kwargs,
    )


def local(object_field, probe_field, amplitudes, row_start, column_start, live_slots):
    smem, vmem = pl.BlockSpec(memory_space=SMEM), pl.BlockSpec(memory_space=VMEM)
    row_table, col_table = (on_chip(jnp.asarray(table)) for table in split_tables())
    probe = on_chip(probe_field)

    def buffer(*dims):
        return pltpu.VMEM(dims, jnp.float32)

    own = object_field.reshape(80, LANES)
    stack = exchange(jnp.broadcast_to(own, (16, 80, LANES)))
    light, peak = kernel_call(
        prep_kernel,
        (buffer(4, 384, LANES), buffer(8, LANES)),
        [vmem],
        (vmem,) * 2,
        4,
        cost_estimate=pl.CostEstimate(flops=300000, bytes_accessed=2000000, transcendentals=0),
    )(probe)
    send, sums, grads, spare = kernel_call(
        window_kernel,
        (
            buffer(16 * PIECE + 640, LANES),
            buffer(3, WIN, WIN),
            buffer(2, 3, 320, LANES),
            buffer(8, LANES),
        ),
        [smem] * 3 + [vmem] * 6,
        (vmem,) * 4,
        24,
        scratch_shapes=[buffer(2, 3, 320, LANES)],
    )(
        row_start, column_start, live_slots, on_chip(stack), on_chip(swap_cores(stack)), probe,
        on_chip(amplitudes), row_table, col_table,
    )

    got, light = lax.optimization_barrier((swap_cores(send), light))
    merged = kernel_call(merge_kernel, buffer(16, LINES, LANES), [vmem] * 4, vmem, 4)(
        sums, grads, spare, on_chip(got)
    )
    pieces = exchange(merged)
    total = kernel_call(reduce_kernel, buffer(PIECE, LANES), [vmem], vmem, 4)(on_chip(pieces))
    new_object = kernel_call(
        object_kernel,
        jax.ShapeDtypeStruct((2, 40, LANES), jnp.float32),
        [vmem] * 4,
        vmem,
        4,
        scratch_shapes=[pltpu.SMEM((16, 1, LANES), jnp.float32), pltpu.SemaphoreType.DMA],
        cost_estimate=pl.CostEstimate(flops=700000, bytes_accessed=2000000, transcendentals=0),
    )(on_chip(pieces), on_chip(object_field), on_chip(light), peak)
    for mask in (1, 2):
        total = total + swap_z(total, mask)
    got, new_object = lax.optimization_barrier((swap_z(total, 6), new_object))
    piece = kernel_call(probe_kernel, buffer(16, 32, LANES), [vmem] * 3, vmem, 4)(
        on_chip(total), on_chip(got), probe
    )

    mine = exchange_plane(piece)
    new_probe = kernel_call(
        gather_kernel, jax.ShapeDtypeStruct((2, WIN, WIN), jnp.float32), [vmem] * 2, vmem, 4
    )(on_chip(mine), on_chip(swap_cores(mine)))
    return new_object, new_probe


def solution(mesh):
    return jax.shard_map(
        local,
        mesh=mesh,
        in_specs=(
            P(None, "group", "tile"),
            P(),
            P(("tile", "group"), None, None),
            P(("tile", "group")),
            P(("tile", "group")),
            P(("tile", "group")),
        ),
        out_specs=(P(None, "group", "tile"), P()),
        check_vma=False,
    )
```

```python
import jax
import jax.numpy as jnp
import ml_dtypes
import numpy as np
from jax import lax
from jax.experimental import pallas as pl
from jax.experimental.pallas import tpu as pltpu
from jax.sharding import PartitionSpec as P

WIN = 256
LANES = 128
TILES = 32
SPARE = 48
PIECE = 56
LINES = 136
SMEM = pltpu.MemorySpace.SMEM
VMEM = pltpu.MemorySpace.VMEM


def split_tables():
    counter = np.arange(WIN)
    angles = 2.0 * np.pi / WIN * (counter[:, None] * counter[None, :] % WIN)
    cos, sin = np.cos(angles) / np.sqrt(WIN), np.sin(angles) / np.sqrt(WIN)
    both = np.concatenate([cos[:LANES], cos[LANES : LANES + 1], sin[1:LANES]], axis=0)
    order = np.concatenate([counter[: LANES + 1], counter[:LANES:-1]])
    high = both.astype(ml_dtypes.bfloat16)
    low = (both - high.astype(np.float64)).astype(ml_dtypes.bfloat16)
    select = (order[:, None] == counter[None, :]).astype(ml_dtypes.bfloat16)
    rows = np.concatenate([high, low, select], axis=0)
    return rows, np.concatenate([high.T, low.T, select.T], axis=0)


def halves(value):
    high = value.astype(jnp.bfloat16)
    low = (value - high.astype(jnp.float32)).astype(jnp.bfloat16)
    return high, low


def dot(left, right):
    return jnp.dot(left, right, preferred_element_type=jnp.float32)


def product(left, right):
    height = left[0].shape[0]
    tall = dot(jnp.concatenate(left, axis=0), right[0])
    return tall[:height] + tall[height:] + dot(left[0], right[1])


def unfold(cos_real, cos_imag, sin_real, sin_imag, axis):
    zeroth = lax.broadcasted_iota(jnp.int32, cos_real.shape, axis) == 0
    odd_real, odd_imag = jnp.where(zeroth, 0.0, sin_imag), jnp.where(zeroth, 0.0, sin_real)
    low = cos_real + odd_real, cos_imag - odd_imag
    high = (
        jnp.where(zeroth, sin_real, cos_real - odd_real),
        jnp.where(zeroth, sin_imag, cos_imag + odd_imag),
    )
    return tuple(jnp.concatenate(pair, axis=axis) for pair in zip(low, high))


def fold(real, imag, axis):
    if axis == 0:
        (low_r, high_r), (low_i, high_i) = ((v[:LANES], v[LANES:]) for v in (real, imag))
    else:
        (low_r, high_r), (low_i, high_i) = ((v[:, :LANES], v[:, LANES:]) for v in (real, imag))
    zeroth = lax.broadcasted_iota(jnp.int32, low_r.shape, axis) == 0
    even = (low_r + jnp.where(zeroth, 0.0, high_r), low_i + jnp.where(zeroth, 0.0, high_i))
    odd = (jnp.where(zeroth, high_r, high_i - low_i), jnp.where(zeroth, high_i, low_r - high_r))
    return tuple(jnp.concatenate(pair, axis=axis) for pair in zip(even, odd))


def parts(table):
    return table[0:WIN], table[WIN : 2 * WIN]


def forward(real, imag, rows, cols):
    along = product(parts(rows), halves(jnp.concatenate([real, imag], axis=1)))
    real, imag = unfold(
        along[:LANES, :WIN], along[:LANES, WIN:], along[LANES:, :WIN], along[LANES:, WIN:], 0
    )
    across = product(halves(jnp.concatenate([real, imag], axis=0)), parts(cols))
    return unfold(
        across[:WIN, :LANES], across[WIN:, :LANES], across[:WIN, LANES:], across[WIN:, LANES:], 1
    )


def inverse(real, imag, rows, cols):
    real, imag = fold(real, imag, 0)
    along = product(parts(cols), halves(jnp.concatenate([real, imag], axis=1)))
    real, imag = fold(along[:, :WIN], along[:, WIN:], 1)
    across = product(halves(jnp.concatenate([real, imag], axis=0)), parts(rows))
    return across[:WIN], across[WIN:]


def reordered(value, rows, cols):
    taken = dot(rows[2 * WIN :], jnp.concatenate(halves(value), axis=1)).astype(jnp.bfloat16)
    taken = dot(jnp.concatenate([taken[:, :WIN], taken[:, WIN:]], axis=0), cols[2 * WIN :])
    return taken[:WIN] + taken[WIN:]


def window_kernel(
    row_ref, col_ref, live_ref, stack, near, probe, amps, row_table, col_table,
    send, sums, grads, spare_out, field,
):
    row, col = row_ref[0], col_ref[0]
    live = live_ref[0].astype(jnp.float32)
    tile, _ = my_place()
    odd, half = tile & 1, half_of(tile)
    inside = far_exists(tile)
    for member in range(8):
        lines = slice(member * 40, member * 40 + 40)
        for part in range(2):
            held = slice(part * 40, part * 40 + 40)
            field[part, 1, lines, :] = stack[8 - 8 * odd + member, held, :]
            field[part, 2 * odd, lines, :] = jnp.where(inside, stack[8 * odd + member, held, :], 0.0)
            field[part, 2 - 2 * odd, lines, :] = near[8 * odd + member, held, :]
    lane = lax.broadcasted_iota(jnp.int32, (WIN, LANES), 1)
    back = lax.rem(LANES - col, LANES)
    ahead = lax.rem(col, LANES)
    first = lane < LANES - col

    def cut(part):
        turned = [
            pltpu.roll(field[part, block, pl.ds(row, WIN), :], back, 1) for block in range(3)
        ]
        return jnp.concatenate(
            [jnp.where(first, turned[0], turned[1]), jnp.where(first, turned[1], turned[2])], axis=1
        )

    sample_real, sample_imag = cut(0), cut(1)
    probe_real, probe_imag = probe[0], probe[1]
    exit_real = probe_real * sample_real - probe_imag * sample_imag
    exit_imag = probe_real * sample_imag + probe_imag * sample_real
    rows, cols = row_table[...], col_table[...]
    far_real, far_imag = forward(exit_real, exit_imag, rows, cols)
    power = far_real * far_real + far_imag * far_imag
    factor = 1.0 - reordered(amps[0], rows, cols) * lax.rsqrt(jnp.maximum(power, 0.0625))
    miss_real, miss_imag = inverse(far_real * factor, far_imag * factor, rows, cols)
    miss_real = miss_real * live
    miss_imag = miss_imag * live
    terms = (
        probe_real * miss_real + probe_imag * miss_imag,
        probe_real * miss_imag - probe_imag * miss_real,
    )
    wrapped = lane < col
    zero = jnp.zeros((WIN, LANES), jnp.float32)
    grads[...] = jnp.zeros_like(grads)
    for part in range(2):
        start = pltpu.roll(terms[part][:, :LANES], ahead, 1)
        end = pltpu.roll(terms[part][:, LANES:], ahead, 1)
        grads[part, 0, pl.ds(row, WIN), :] = jnp.where(wrapped, zero, start)
        grads[part, 1, pl.ds(row, WIN), :] = jnp.where(wrapped, start, end)
        grads[part, 2, pl.ds(row, WIN), :] = jnp.where(wrapped, end, zero)
    window_light = live * (sample_real * sample_real + sample_imag * sample_imag)
    sums[0] = sample_real * miss_real + sample_imag * miss_imag
    sums[1] = sample_real * miss_imag - sample_imag * miss_real
    sums[2] = window_light
    total = jnp.zeros((8, LANES), jnp.float32)
    for line in range(0, WIN, 8):
        total = total + window_light[line : line + 8, :LANES] + window_light[line : line + 8, LANES:]
    spare_line = lax.broadcasted_iota(jnp.int32, (8, LANES), 0)
    spare_lane = lax.broadcasted_iota(jnp.int32, (8, LANES), 1)
    first_lane = 8 * odd
    spare = jnp.where(
        spare_line == 1,
        jnp.broadcast_to(jnp.sum(total, axis=0, keepdims=True), (8, LANES)),
        0.0,
    )
    for lane_off, number in enumerate((row.astype(jnp.float32), col.astype(jnp.float32), live)):
        here = jnp.logical_and(spare_line == 0, spare_lane == first_lane + lane_off)
        spare = jnp.where(here, number, spare)
    spare_out[...] = spare
    send[16 * SPARE : 16 * SPARE + 8, :] = spare
    for member in range(16):
        first_line = member * SPARE
        top = pl.multiple_of((1 - half) * 128 + member * 8, 8)
        for part in range(3):
            for side in range(2):
                put = first_line + part * 16 + side * 8
                send[put : put + 8, :] = sums[part, pl.ds(top, 8), side * LANES : (side + 1) * LANES]
    for member in range(8):
        lines = slice(member * 40, member * 40 + 40)
        for part in range(2):
            put = 16 * SPARE + 8 + member * 80 + part * 40
            send[put : put + 40, :] = grads[part, 2 - 2 * odd, lines, :]


def merge_kernel(sums, grads, spare, got, out):
    tile, _ = my_place()
    odd, half, inside = tile & 1, half_of(tile), far_exists(tile)
    for member in range(16):
        top = pl.multiple_of(half * 128 + member * 8, 8)
        for part in range(3):
            for side in range(2):
                put = part * 16 + side * 8
                other = got[member * SPARE + put : member * SPARE + put + 8, :]
                own = sums[part, pl.ds(top, 8), side * LANES : (side + 1) * LANES]
                out[member, put : put + 8, :] = own + other
        out[member, SPARE:PIECE, :] = spare[...] + got[16 * SPARE : 16 * SPARE + 8, :]
    for member in range(8):
        lines = slice(member * 40, member * 40 + 40)
        for part in range(2):
            put = PIECE + part * 40
            other = 16 * SPARE + 8 + member * 80 + part * 40
            out[8 - 8 * odd + member, put : put + 40, :] = grads[part, 1, lines, :] + got[other : other + 40, :]
            out[8 * odd + member, put : put + 40, :] = jnp.where(
                inside, grads[part, 2 * odd, lines, :], 0.0
            )


def reduce_kernel(pieces, out):
    total = pieces[0, :PIECE, :]
    for member in range(1, 16):
        total = total + pieces[member, :PIECE, :]
    out[...] = total


def probe_kernel(one, two, probe, out):
    tile, group = my_place()
    top = pl.multiple_of(half_of(tile) * 128 + (8 - 8 * (tile & 1) + group) * 8, 8)
    summed = one[...] + two[...]
    mean = jnp.sum(summed[SPARE + 1 : SPARE + 2]) * (1.0 / (WIN * WIN))
    for side in range(2):
        bottom = summed[32 + side * 8 : 40 + side * 8] + 0.25 * mean + 1e-05
        for part in range(2):
            lines = part * 16 + side * 8
            old = probe[part, pl.ds(top, 8), side * LANES : (side + 1) * LANES]
            new = old - summed[lines : lines + 8] / bottom
            for member in range(16):
                out[member, lines : lines + 8, :] = new


def gather_kernel(mine, other, out):
    core = my_place()[0] & 1
    for source, which in ((mine, core), (other, 1 - core)):
        for member in range(16):
            x_hi, group = (member >> 1) & 1, (member >> 2) * 2 + (member & 1)
            top = pl.multiple_of((which ^ x_hi) * 128 + (8 - 8 * which + group) * 8, 8)
            for part in range(2):
                for side in range(2):
                    lines = part * 16 + side * 8
                    out[part, pl.ds(top, 8), side * LANES : (side + 1) * LANES] = source[
                        member, lines : lines + 8, :
                    ]


def shine(light, group, total, at, block):
    row, col = at[0].astype(jnp.int32), at[1].astype(jnp.int32)
    top = 64 + group * 40 - row
    turn = lax.rem(col, LANES)
    lane = lax.broadcasted_iota(jnp.int32, (40, LANES), 1)
    before = pltpu.roll(light[block, pl.ds(top, 40), :], turn, 1)
    after = pltpu.roll(light[block + 1, pl.ds(top, 40), :], turn, 1)
    return total + at[2] * jnp.where(lane < col, before, after)


def prep_kernel(probe, light, peak):
    blank = jnp.zeros((64, LANES), jnp.float32)
    most = jnp.zeros((WIN, LANES), jnp.float32)
    for side in range(2):
        cols = slice(side * LANES, (side + 1) * LANES)
        bright = probe[0, :, cols] * probe[0, :, cols] + probe[1, :, cols] * probe[1, :, cols]
        most = jnp.maximum(most, bright)
        light[1 + side, 64:320, :] = bright
        light[1 + side, 0:64, :] = blank
        light[1 + side, 320:384, :] = blank
        light[3 * side, :, :] = jnp.zeros((384, LANES), jnp.float32)
    peak[...] = jnp.full((8, LANES), jnp.max(most), jnp.float32)


def object_kernel(pieces, old, light, peak, out, at, sem):
    copy = pltpu.make_async_copy(pieces.at[:, SPARE : SPARE + 1, :], at, sem)
    copy.start()
    gradient = pieces[0, PIECE:, :]
    for member in range(1, 16):
        gradient = gradient + pieces[member, PIECE:, :]
    copy.wait()
    tile, group = my_place()
    odd = tile & 1
    mine = 8 - 8 * odd
    total = jnp.zeros((40, LANES), jnp.float32)
    outside = jnp.zeros((40, LANES), jnp.float32)
    for member in range(8):
        for core in range(2):
            block = 1 - core * (1 - odd) + (1 - core) * odd
            seen = [at[mine + member, 0, core * 8 + k] for k in range(3)]
            total = shine(light, group, total, seen, block)
        seen = [at[8 - mine + member, 0, (1 - odd) * 8 + k] for k in range(3)]
        outside = shine(light, group, outside, seen, 2 - 2 * odd)
    total = total + jnp.where(far_exists(tile), outside, 0.0)
    bottom = total + 0.25 * (peak[0:1, :] + 1e-06)
    for part in range(2):
        out[part] = old[part] - gradient[part * 40 : part * 40 + 40, :] / bottom


def my_place():
    return lax.axis_index("tile"), lax.axis_index("group")


def half_of(tile):
    return (tile ^ (tile >> 1)) & 1


def far_exists(tile):
    return jnp.logical_and(tile > 0, tile < TILES - 1)


def swap_cores(value):
    return lax.ppermute(value, "tile", [(i, i ^ 1) for i in range(TILES)])


def swap_z(value, mask):
    return lax.ppermute(value, "tile", [(tile, tile ^ (4 * mask)) for tile in range(TILES)])


def exchange(value):
    groups = []
    for first in range(1, TILES, 2):
        second = (first + 1) % TILES
        groups.append([first * 8 + i for i in range(8)] + [second * 8 + i for i in range(8)])
    return lax.all_to_all(value, ("tile", "group"), 0, 0, axis_index_groups=groups)


def exchange_plane(value):
    groups = []
    for layer in range(TILES // 4):
        for core in range(2):
            groups.append(
                [
                    (layer * 4 + x_hi * 2 + core) * 8 + y * 2 + x_lo
                    for y in range(4)
                    for x_hi in range(2)
                    for x_lo in range(2)
                ]
            )
    return lax.all_to_all(value, ("tile", "group"), 0, 0, axis_index_groups=groups)


def on_chip(value):
    return pltpu.with_memory_space_constraint(value, pltpu.VMEM)


def kernel_call(body, out_shape, in_specs, out_specs, megabytes, **kwargs):
    return pl.pallas_call(
        body,
        out_shape=out_shape,
        in_specs=in_specs,
        out_specs=out_specs,
        compiler_params=pltpu.CompilerParams(vmem_limit_bytes=megabytes << 20),
        name=body.__name__.removesuffix("_kernel"),
        **kwargs,
    )


def local(object_field, probe_field, amplitudes, row_start, column_start, live_slots):
    smem, vmem = pl.BlockSpec(memory_space=SMEM), pl.BlockSpec(memory_space=VMEM)
    row_table, col_table = (on_chip(jnp.asarray(table)) for table in split_tables())
    probe = on_chip(probe_field)

    def buffer(*dims):
        return pltpu.VMEM(dims, jnp.float32)

    own = object_field.reshape(80, LANES)
    stack = exchange(jnp.broadcast_to(own, (16, 80, LANES)))
    light, peak = kernel_call(
        prep_kernel,
        (buffer(4, 384, LANES), buffer(8, LANES)),
        [vmem],
        (vmem,) * 2,
        4,
        cost_estimate=pl.CostEstimate(flops=300000, bytes_accessed=2000000, transcendentals=0),
    )(probe)
    send, sums, grads, spare = kernel_call(
        window_kernel,
        (
            buffer(16 * SPARE + 648, LANES),
            buffer(3, WIN, WIN),
            buffer(2, 3, 320, LANES),
            buffer(8, LANES),
        ),
        [smem] * 3 + [vmem] * 6,
        (vmem,) * 4,
        24,
        scratch_shapes=[buffer(2, 3, 320, LANES)],
    )(
        row_start, column_start, live_slots, on_chip(stack), on_chip(swap_cores(stack)), probe,
        on_chip(amplitudes), row_table, col_table,
    )

    got, light = lax.optimization_barrier((swap_cores(send), light))
    merged = kernel_call(merge_kernel, buffer(16, LINES, LANES), [vmem] * 4, vmem, 4)(
        sums, grads, spare, on_chip(got)
    )
    pieces = exchange(merged)
    total = kernel_call(reduce_kernel, buffer(PIECE, LANES), [vmem], vmem, 4)(on_chip(pieces))
    new_object = kernel_call(
        object_kernel,
        jax.ShapeDtypeStruct((2, 40, LANES), jnp.float32),
        [vmem] * 4,
        vmem,
        4,
        scratch_shapes=[pltpu.SMEM((16, 1, LANES), jnp.float32), pltpu.SemaphoreType.DMA],
        cost_estimate=pl.CostEstimate(flops=700000, bytes_accessed=2000000, transcendentals=0),
    )(on_chip(pieces), on_chip(object_field), on_chip(light), peak)
    for mask in (1, 2):
        total = total + swap_z(total, mask)
    got, new_object = lax.optimization_barrier((swap_z(total, 6), new_object))
    piece = kernel_call(probe_kernel, buffer(16, 32, LANES), [vmem] * 3, vmem, 4)(
        on_chip(total), on_chip(got), probe
    )

    mine = exchange_plane(piece)
    new_probe = kernel_call(
        gather_kernel, jax.ShapeDtypeStruct((2, WIN, WIN), jnp.float32), [vmem] * 2, vmem, 4
    )(on_chip(mine), on_chip(swap_cores(mine)))
    return new_object, new_probe


def solution(mesh):
    return jax.shard_map(
        local,
        mesh=mesh,
        in_specs=(
            P(None, "group", "tile"),
            P(),
            P(("tile", "group"), None, None),
            P(("tile", "group")),
            P(("tile", "group")),
            P(("tile", "group")),
        ),
        out_specs=(P(None, "group", "tile"), P()),
        check_vma=False,
    )
```
